32 devices in a mesh: dp: 8 (over z, x), tensor: 4 (over y, core).
Axes of the slice: x: 2, y: 2, z: 4, core: 2. Of those that a mesh axis runs over, the one named last changes fastest.
Arguments:
- tokens: bfloat16 [8192, 2048], P(('dp', 'tensor')), may hold values from -6 to 6
- parents: int32 [8, 8], P('dp'), may hold values from 0 to 6, as said below
- attn_gain: bfloat16 [2048], P('dp'), may hold values from 0.099609375 to 1.8984375
- w_query: bfloat16 [2048, 2048], P('dp', 'tensor'), may hold values from -0.125 to 0.125
- key_matrix: bfloat16 [2048, 1024], P('dp', 'tensor'), may hold values from -0.125 to 0.125
- value_matrix: bfloat16 [2048, 1024], P('dp', 'tensor'), may hold values from -0.125 to 0.125
- w_out: bfloat16 [2048, 2048], P('tensor', 'dp'), may hold values from -0.5 to 0.5
- mlp_gain: bfloat16 [2048], P('dp'), may hold values from 0.099609375 to 1.8984375
- w_gate: bfloat16 [2048, 8192], P('dp', 'tensor'), may hold values from -0.125 to 0.125
- w_up: bfloat16 [2048, 8192], P('dp', 'tensor'), may hold values from -0.125 to 0.125
- w_down: bfloat16 [8192, 2048], P('tensor', 'dp'), may hold values from -0.0625 to 0.0625
- cotangent: bfloat16 [8192, 2048], P(('dp', 'tensor')), may hold values from -6 to 6
Outputs:
- output: bfloat16 [8192, 2048], P(('dp', 'tensor'))
- grad_tokens: bfloat16 [8192, 2048], P(('dp', 'tensor'))
- grad_attn_gain: float32 [2048], P('dp')
- grad_query: float32 [2048, 2048], P('dp', 'tensor')
- grad_key: float32 [2048, 1024], P('dp', 'tensor')
- grad_value: float32 [2048, 1024], P('dp', 'tensor')
- grad_out: float32 [2048, 2048], P('tensor', 'dp')
- grad_mlp_gain: float32 [2048], P('dp')
- grad_gate: float32 [2048, 8192], P('dp', 'tensor')
- grad_up: float32 [2048, 8192], P('dp', 'tensor')
- grad_down: float32 [8192, 2048], P('tensor', 'dp')
The draws below stay inside these ranges and needn't reach their ends.
Inputs may be any that keep to these rules, and one draw needn't show every extreme that they name: parents[t, 0] is 0, parents[t, b] is below b for b >= 1, and the last segment's parent is segment 8 - 2, so segment 0 is each tree's root and every segment's ancestors come earlier.
All inputs are finite; a program needn't handle non-finite values.
Results may differ from the reference program's by a relative error of at most 0.014.
Values may be sent and summed in bfloat16 or wider, within the bound.
A program may use at most 256 MiB of HBM per device.

```python
import jax
import jax.numpy as jnp
from jax import lax

MODEL_WIDTH = 2048
QUERY_HEADS = 8
KEY_VALUE_HEADS = 4
HEAD_SIZE = 256
FF = 8192
BLK = 128
BLOCKS = 8
TREE_TOKENS = 1024
TREES = 8
TOKENS = 8192


def draw_parents(key, part):
    limits = jnp.maximum(jnp.arange(BLOCKS, dtype=jnp.int32), 1)
    drawn = jax.random.randint(key, (TREES, BLOCKS), 0, limits[None, :]).astype(jnp.int32)
    column = jnp.arange(BLOCKS, dtype=jnp.int32)[None, :]
    return jnp.where(column == BLOCKS - 1, BLOCKS - 2, drawn).astype(jnp.int32)


def steps_of(rng, extent, split, least, high):
    def one(dim, blocks):
        draws = jax.random.uniform(jax.random.fold_in(jax.random.fold_in(rng, 6), dim), (blocks,), jnp.float32, least / len(split), high / len(split))
        return jnp.repeat(jnp.exp(draws), extent[dim] // blocks).reshape((-1,) + (1,) * (len(extent) - dim - 1))

    factor_of = one(*split[0])
    for cut in split[1:]:
        factor_of = factor_of * one(*cut)
    return factor_of


def bell_draw(own_key, shape, scale, limit, cuts=(), kind=jnp.bfloat16):
    values = scale * jax.random.normal(own_key, shape, jnp.float32)
    if cuts:
        values = values * steps_of(own_key, shape, cuts, -0.22, 0.18)
    return jnp.clip(values, -limit, limit).astype(kind)


def setup_inputs(seed: int = 0) -> dict:
    key_list = jax.random.split(jax.random.key(seed), 13)
    return {
        "tokens": bell_draw(key_list[0], (TOKENS, MODEL_WIDTH), 1.0, 6.0, ((0, 32),)),
        "parents": draw_parents(jax.random.fold_in(key_list[12], 71), 0),
        "attn_gain": jnp.clip(1.0 + 0.18 * jax.random.normal(key_list[2], (MODEL_WIDTH,), jnp.float32), 0.099609375, 1.8984375).astype(jnp.bfloat16),
        "w_query": bell_draw(key_list[3], (MODEL_WIDTH, QUERY_HEADS * HEAD_SIZE), MODEL_WIDTH ** -0.5, 0.125, ((0, 8), (1, 4))),
        "key_matrix": bell_draw(key_list[4], (MODEL_WIDTH, KEY_VALUE_HEADS * HEAD_SIZE), MODEL_WIDTH ** -0.5, 0.125, ((0, 8), (1, 4))),
        "value_matrix": bell_draw(key_list[5], (MODEL_WIDTH, KEY_VALUE_HEADS * HEAD_SIZE), MODEL_WIDTH ** -0.5, 0.125, ((0, 8), (1, 4))),
        "w_out": bell_draw(key_list[6], (QUERY_HEADS * HEAD_SIZE, MODEL_WIDTH), (QUERY_HEADS * HEAD_SIZE // 16) ** -0.5, 0.5, ((0, 4), (1, 8))),
        "mlp_gain": jnp.clip(1.0 + 0.18 * jax.random.normal(key_list[7], (MODEL_WIDTH,), jnp.float32), 0.099609375, 1.8984375).astype(jnp.bfloat16),
        "w_gate": bell_draw(key_list[8], (MODEL_WIDTH, FF), MODEL_WIDTH ** -0.5, 0.125, ((0, 8), (1, 4))),
        "w_up": bell_draw(key_list[9], (MODEL_WIDTH, FF), MODEL_WIDTH ** -0.5, 0.125, ((0, 8), (1, 4))),
        "w_down": bell_draw(key_list[10], (FF, MODEL_WIDTH), FF ** -0.5, 0.0625, ((0, 4), (1, 8))),
        "cotangent": bell_draw(key_list[11], (TOKENS, MODEL_WIDTH), 1.0, 6.0, ((0, 32),)),
    }


EPS = 1e-06
THETA = 1000042.0
NEG = -1e+30
HIGH = lax.Precision.HIGHEST

@jax.custom_vjp
def reduced_precision(v):
    return lax.optimization_barrier(v.astype(jnp.bfloat16)).astype(jnp.float32)

@jax.custom_vjp
def low_back(v):
    return v

def low_keep(v):
    return (reduced_precision(v), None)

def low_pass(kept, grad):
    return (grad,)

def back_keep(v):
    return (v, None)

def back_low(kept, grad):
    return (reduced_precision(grad),)
reduced_precision.defvjp(low_keep, low_pass)
low_back.defvjp(back_keep, back_low)

def tree_tables(parent_row, tree_len, block_len):
    blocks = parent_row.shape[0]
    nodes = jnp.arange(blocks, dtype=jnp.int32)
    hops = (parent_row[:, None] == nodes[None, :]).astype(jnp.float32)
    reach = jnp.eye(blocks, dtype=jnp.float32)
    walk = reach
    for hop_count in range(blocks):
        walk = jnp.dot(walk, hops, precision=HIGH)
        reach = jnp.maximum(reach, walk)
    depth = lax.optimization_barrier(jnp.sum(reach, axis=1)) - 1.0
    rows = jnp.arange(tree_len, dtype=jnp.int32)
    member = (rows[:, None] // block_len == nodes[None, :]).astype(jnp.float32)
    visible = jnp.dot(jnp.dot(member, reach, precision=HIGH), member.T, precision=HIGH) > 0.5
    allowed_mask = visible & (rows[None, :] <= rows[:, None])
    place = jnp.dot(member, depth, precision=HIGH) * block_len + (rows % block_len).astype(jnp.float32)
    return (allowed_mask, place)

def rope_tables(place, head_dim):
    half = head_dim // 2
    freq = THETA ** (-2.0 * jnp.arange(half, dtype=jnp.float32) / head_dim)
    angle = place[:, None] * freq[None, :]
    cosine_table = jnp.cos(angle)
    sine_table = jnp.sin(angle)
    return (jnp.concatenate([cosine_table, cosine_table], -1), jnp.concatenate([sine_table, sine_table], -1))

def apply_rotation(values, cosine_table, sine_table):
    half = values.shape[-1] // 2
    turned = jnp.concatenate([-values[..., half:], values[..., :half]], -1)
    return values * cosine_table[:, None, :] + turned * sine_table[:, None, :]

def rms_norm(values, gain):
    inverse = lax.rsqrt(lax.optimization_barrier(jnp.mean(values * values, axis=-1, keepdims=True)) + EPS)
    return values * inverse * gain

def root_path_attention(pack):
    query_rows, key, value_rows, allowed_mask = pack
    query_group = QUERY_HEADS // KEY_VALUE_HEADS
    keys = jnp.repeat(key, query_group, axis=1)
    values = jnp.repeat(value_rows, query_group, axis=1)
    raw = low_back(jnp.einsum('qhd,khd->hqk', query_rows, keys, precision=HIGH))
    scores = jnp.where(allowed_mask[None], raw * HEAD_SIZE ** (-0.5), NEG)
    top = lax.optimization_barrier(jnp.max(scores, axis=-1, keepdims=True))
    weights = jnp.exp(scores - top)
    probs = reduced_precision(weights / lax.optimization_barrier(jnp.sum(weights, axis=-1, keepdims=True)))
    attended_rows = jnp.einsum('hqk,khd->qhd', probs, values, precision=HIGH)
    return low_back(reduced_precision(attended_rows))

def forward(inputs, attn_gain, w_query, key_matrix, value_matrix, w_out, mlp_gain, w_gate, w_up, w_down, allowed_mask, cosine_table, sine_table):
    packed_trees = inputs.shape[0] // TREE_TOKENS
    normed = reduced_precision(rms_norm(inputs, attn_gain))
    query_raw = low_back(jnp.dot(normed, w_query, precision=HIGH))
    unrotated_key = low_back(jnp.dot(normed, key_matrix, precision=HIGH))
    unprojected_value = low_back(jnp.dot(normed, value_matrix, precision=HIGH))
    query_rows = reduced_precision(apply_rotation(query_raw.reshape(-1, QUERY_HEADS, HEAD_SIZE), cosine_table, sine_table))
    key = reduced_precision(apply_rotation(unrotated_key.reshape(-1, KEY_VALUE_HEADS, HEAD_SIZE), cosine_table, sine_table))
    value_rows = reduced_precision(unprojected_value.reshape(-1, KEY_VALUE_HEADS, HEAD_SIZE))
    attended_rows = lax.map(jax.checkpoint(root_path_attention), (query_rows.reshape(packed_trees, TREE_TOKENS, QUERY_HEADS, HEAD_SIZE), key.reshape(packed_trees, TREE_TOKENS, KEY_VALUE_HEADS, HEAD_SIZE), value_rows.reshape(packed_trees, TREE_TOKENS, KEY_VALUE_HEADS, HEAD_SIZE), allowed_mask))
    attended_rows = attended_rows.reshape(-1, QUERY_HEADS * HEAD_SIZE)
    mixed = inputs + low_back(jnp.dot(attended_rows, w_out, precision=HIGH))
    normed_two = reduced_precision(rms_norm(mixed, mlp_gain))
    gate = low_back(jnp.dot(normed_two, w_gate, precision=HIGH))
    upper = low_back(jnp.dot(normed_two, w_up, precision=HIGH))
    hidden = reduced_precision(jax.nn.silu(gate) * upper)
    return mixed + low_back(jnp.dot(hidden, w_down, precision=HIGH))

def reference(tokens, parents, attn_gain, w_query, key_matrix, value_matrix, w_out, mlp_gain, w_gate, w_up, w_down, cotangent):

    def tables(parent_row):
        return tree_tables(parent_row, TREE_TOKENS, BLK)
    allowed_mask, place = jax.vmap(tables)(parents)
    cosine_table, sine_table = rope_tables(place.reshape(-1), HEAD_SIZE)

    def run(inputs, gain_a, query_w, key_w, value_w, out_w, gain_m, gate_w, up_w, down_w):
        return forward(inputs, gain_a, query_w, key_w, value_w, out_w, gain_m, gate_w, up_w, down_w, allowed_mask, cosine_table, sine_table)
    weights = [tokens, attn_gain, w_query, key_matrix, value_matrix, w_out, mlp_gain, w_gate, w_up, w_down]
    floats = [item.astype(jnp.float32) for item in weights]
    result, pull = jax.vjp(run, *floats)
    grads = pull(cotangent.astype(jnp.float32))
    return (result.astype(jnp.bfloat16), grads[0].astype(jnp.bfloat16), grads[1], grads[2], grads[3], grads[4], grads[5], grads[6], grads[7], grads[8], grads[9])
```

```python
import jax
import jax.numpy as jnp
from jax import lax
from jax.sharding import PartitionSpec as P

HEAD_SIZE = 256
BLK = 128


EPS = 1e-06
THETA = 1000042.0
NEG = -1e30
HIGH = lax.Precision.HIGHEST
F32 = jnp.float32
BF16 = jnp.bfloat16


def tree_tables(parent_row, rows, block_len):
    blocks = parent_row.shape[0]
    nodes = jnp.arange(blocks, dtype=jnp.int32)
    hops = (parent_row[:, None] == nodes[None, :]).astype(F32)
    reach = jnp.eye(blocks, dtype=F32)
    walk = reach
    for hop_count in range(blocks):
        walk = jnp.dot(walk, hops, precision=HIGH)
        reach = jnp.maximum(reach, walk)
    depth = jnp.sum(reach, axis=1) - 1.0
    member = (rows[:, None] // block_len == nodes[None, :]).astype(F32)
    visible = jnp.dot(jnp.dot(member, reach, precision=HIGH), member.T, precision=HIGH) > 0.5
    allowed_mask = visible & (rows[None, :] <= rows[:, None])
    place = jnp.dot(member, depth, precision=HIGH) * block_len + (rows % block_len).astype(F32)
    return (allowed_mask, place)


def rope_tables(place, head_dim):
    half = head_dim // 2
    freq = THETA ** (-2.0 * jnp.arange(half, dtype=F32) / head_dim)
    angle = place[:, None] * freq[None, :]
    cosine_table = jnp.cos(angle)
    sine_table = jnp.sin(angle)
    return (
        jnp.concatenate([cosine_table, cosine_table], -1),
        jnp.concatenate([sine_table, sine_table], -1),
    )


def apply_rotation(values, cosine_table, sine_table, sign):
    half = values.shape[-1] // 2
    turned = jnp.concatenate([-values[..., half:], values[..., :half]], -1)
    return values * cosine_table[:, None, :] + sign * turned * sine_table[:, None, :]


def normalize(values):
    inverse = lax.rsqrt(jnp.mean(values * values, axis=-1, keepdims=True) + EPS)
    return (values * inverse, inverse)


def norm_back(grad_normed, gain, scaled, inverse):
    grad_scaled = grad_normed * gain
    inner = jnp.mean(grad_scaled * scaled, axis=-1, keepdims=True)
    return inverse * (grad_scaled - scaled * inner)


def dot_nn(left, right):
    return jnp.dot(left, right, preferred_element_type=F32)


def dot_nt(left, right):
    return lax.dot_general(left, right, (((1,), (1,)), ((), ())), preferred_element_type=F32)


def dot_tn(left, right):
    return lax.dot_general(left, right, (((0,), (0,)), ((), ())), preferred_element_type=F32)


def after(value, *earlier):
    return lax.optimization_barrier((value,) + earlier)[0]


def make_body(dp, tp):
    devices = dp * tp
    outer = dp // 2
    assert tp == 4 and dp == 2 * outer and outer & (outer - 1) == 0
    X = tp

    def swap(value, mask):
        return lax.ppermute(value, ("dp", "tensor"), [(i, i ^ mask) for i in range(devices)])

    def zmask(k):
        return k * 2 * tp

    def relative(value, zi):
        width = value.shape[-1] // outer
        step = 1
        while step < outer:
            blocks = [value[..., i * width : (i + 1) * width] for i in range(outer)]
            swapped = jnp.concatenate([blocks[i ^ step] for i in range(outer)], -1)
            value = jnp.where((zi // step) % 2 == 1, swapped, value)
            step *= 2
        return value

    def gather_tensor(a0):
        a1 = swap(a0, 1)
        a2 = swap(a0, 2)
        a3 = swap(a2, 1)
        return [a0, a1, a2, a3]

    def gather_units(a0):
        rows = a0.shape[0] // 2
        ay = swap(a0, 2)
        ax = swap(a0, X)
        d0 = swap(ax[:rows], 2)
        d1 = swap(ay[rows:], X)
        axy = jnp.concatenate([d0, d1], 0)
        even = [a0, ay, ax, axy]
        odd = [swap(e, 1) for e in even]
        return [even[0], odd[0], even[1], odd[1], even[2], odd[2], even[3], odd[3]]

    def scatter_tensor(part):
        b = part.astype(BF16)
        got = swap(jnp.stack([b[1], b[3]]), 1).astype(F32)
        own = part[0] + got[0]
        far = (part[2] + got[1]).astype(BF16)
        return own + swap(far, 2).astype(F32)

    def scatter_units(part):
        rows = part.shape[1] // 2
        got = swap(jnp.stack([part[1], part[3], part[5], part[7]]), 1).astype(F32)
        s0 = part[0].astype(F32) + got[0]
        sy = part[2].astype(F32) + got[1]
        sx = part[4].astype(F32) + got[2]
        sxy = (part[6].astype(F32) + got[3]).astype(BF16)
        top = swap(sxy[:rows], X).astype(F32)
        bottom = swap(sxy[rows:], 2).astype(F32)
        sy = jnp.concatenate([sy[:rows] + top, sy[rows:]], 0).astype(BF16)
        sx = jnp.concatenate([sx[:rows], sx[rows:] + bottom], 0).astype(BF16)
        return s0 + swap(sy, 2).astype(F32) + swap(sx, X).astype(F32)

    def body(
        tokens,
        parents,
        attn_gain,
        w_query,
        key_matrix,
        value_matrix,
        w_out,
        mlp_gain,
        w_gate,
        w_up,
        w_down,
        cotangent,
    ):
        di = lax.axis_index("dp")
        ti = lax.axis_index("tensor")
        zi = di // 2
        upper_x = di % 2 == 1
        rows, model = tokens.shape
        tree_len = rows * tp
        q_width = w_query.shape[1]
        kv_width = key_matrix.shape[1]
        local_q = q_width // HEAD_SIZE
        local_kv = kv_width // HEAD_SIZE
        group = local_q // local_kv
        qkv_width = q_width + 2 * kv_width
        shard = w_query.shape[0]
        units = w_gate.shape[1] // 2
        scale = HEAD_SIZE ** (-0.5)

        def order_x(mine, theirs, axis):
            low = jnp.where(upper_x, theirs, mine)
            high = jnp.where(upper_x, mine, theirs)
            return jnp.concatenate([low, high], axis)

        gains = jnp.stack([attn_gain, mlp_gain])
        gains = order_x(gains, swap(gains, X), 1)
        gains = jnp.concatenate([gains] + [swap(gains, zmask(k)) for k in range(1, outer)], 1)
        gain_a = gains[0].astype(F32)
        gain_m = gains[1].astype(F32)

        wa = jnp.concatenate([w_query, key_matrix, value_matrix, w_out.T], 1)
        wa_z = [wa] + [swap(wa, zmask(k)) for k in range(1, outer)]
        wa_x = [swap(w, X) for w in wa_z]
        wa_all = [order_x(a, b, 0) for a, b in zip(wa_z, wa_x)]
        w_qkv = jnp.concatenate([w[:, :qkv_width] for w in wa_all], 0)
        w_o = jnp.concatenate([w[:, qkv_width:] for w in wa_all], 0)

        def halves(w):
            low, high = w[:, :units], w[:, units:]
            return jnp.where(upper_x, high, low), jnp.where(upper_x, low, high)

        def paired(w):
            keep, send = halves(w)
            return order_x(keep, swap(send, X), 0)

        pieces = [paired(w) for w in (w_gate, w_up, w_down.T)]
        started = after((pieces[0], pieces[1]), wa_z[-1])
        pieces = [started[0], started[1], pieces[2]]
        gate_z = [swap(pieces[0], zmask(k)) for k in range(1, outer)]
        up_z = [swap(pieces[1], zmask(k)) for k in range(1, outer)]
        pieces[2] = after(pieces[2], gate_z[-1])
        down_z = [swap(pieces[2], zmask(k)) for k in range(1, outer)]
        gate_w = jnp.concatenate([pieces[0]] + gate_z, 0)
        up_w = jnp.concatenate([pieces[1]] + up_z, 0)
        down_w = jnp.concatenate([pieces[2]] + down_z, 0)

        row_ids = jnp.concatenate(
            [(ti ^ j) * rows + jnp.arange(rows, dtype=jnp.int32) for j in range(tp)]
        )
        allowed_mask, place = tree_tables(parents[0], row_ids, BLK)
        cosine_table, sine_table = rope_tables(place, HEAD_SIZE)
        inputs = relative(tokens, zi).astype(F32)
        scaled_a, inverse_a = normalize(inputs)
        normed_a = (scaled_a * gain_a).astype(BF16)
        normed_all = jnp.concatenate(gather_tensor(normed_a), 0)
        qkv = dot_nn(normed_all, w_qkv)
        query_rows = apply_rotation(
            qkv[:, :q_width].reshape(tree_len, local_q, HEAD_SIZE), cosine_table, sine_table, 1.0
        ).astype(BF16)
        key = apply_rotation(
            qkv[:, q_width : q_width + kv_width].reshape(tree_len, local_kv, HEAD_SIZE),
            cosine_table,
            sine_table,
            1.0,
        ).astype(BF16)
        value_rows = qkv[:, q_width + kv_width :].reshape(tree_len, local_kv, HEAD_SIZE)
        value_rows = value_rows.astype(BF16)
        grouped = query_rows.reshape(tree_len, local_kv, group, HEAD_SIZE)
        raw = jnp.einsum("qkgd,skd->kgqs", grouped, key, preferred_element_type=F32)
        scores = jnp.where(allowed_mask[None, None], raw * scale, NEG)
        top = jnp.max(scores, axis=-1, keepdims=True)
        weights = jnp.exp(scores - top)
        total = jnp.sum(weights, axis=-1, keepdims=True)
        probs = (weights / total).astype(BF16)
        attended = jnp.einsum("kgqs,skd->qkgd", probs, value_rows, preferred_element_type=F32)
        attended = attended.reshape(tree_len, q_width).astype(BF16)
        mixed = inputs + scatter_tensor(dot_nt(attended, w_o).reshape(tp, rows, model))

        scaled_m, inverse_m = normalize(mixed)
        normed_m = (scaled_m * gain_m).astype(BF16)
        normed_m_all = jnp.concatenate(gather_units(normed_m), 0)
        cot = relative(cotangent, zi)
        cot_all = jnp.concatenate(gather_units(cot), 0)
        gate = dot_nn(normed_m_all, gate_w)
        upper = dot_nn(normed_m_all, up_w)
        sigma = jax.nn.sigmoid(gate)
        swish = gate * sigma
        hidden = (swish * upper).astype(BF16)
        grad_down = dot_tn(cot_all, hidden).astype(BF16)

        grad_hidden = dot_nn(cot_all, down_w)
        grad_gate_act = (grad_hidden * upper * sigma * (1.0 + gate * (1.0 - sigma))).astype(BF16)
        grad_up_act = (grad_hidden * swish).astype(BF16)
        grad_normed_m = scatter_units(
            (dot_nt(grad_gate_act, gate_w) + dot_nt(grad_up_act, up_w))
            .astype(BF16)
            .reshape(2 * tp, rows, model)
        )
        grad_mixed = cot.astype(F32) + norm_back(grad_normed_m, gain_m, scaled_m, inverse_m)
        grad_gate = dot_tn(normed_m_all, grad_gate_act).astype(BF16)
        grad_up = dot_tn(normed_m_all, grad_up_act).astype(BF16)
        mlp_part = dot_nt(hidden, down_w).astype(BF16).reshape(2 * tp, rows, model)
        output = relative((mixed + scatter_units(mlp_part)).astype(BF16), zi)

        def reduce_z(grad):
            block = grad.reshape(outer, 2 * shard, grad.shape[1])
            total = block[0].astype(F32)
            for k in range(1, outer):
                total = total + swap(block[k], zmask(k)).astype(F32)
            return total

        def unpaired(grad):
            s = reduce_z(grad)
            keep = jnp.where(upper_x, s[shard:], s[:shard])
            send = jnp.where(upper_x, s[:shard], s[shard:]).astype(BF16)
            return order_x(keep, swap(send, X).astype(F32), 1)

        grad_down = unpaired(grad_down)
        grad_gate = unpaired(grad_gate)
        grad_up = unpaired(grad_up)

        grad_mixed_all = jnp.concatenate(gather_tensor(grad_mixed.astype(BF16)), 0)
        grad_attended = dot_nn(grad_mixed_all, w_o).astype(BF16)
        grad_grouped = grad_attended.reshape(tree_len, local_kv, group, HEAD_SIZE)
        grad_value_act = jnp.einsum(
            "kgqs,qkgd->skd", probs, grad_grouped, preferred_element_type=F32
        )
        grad_probs = jnp.einsum(
            "qkgd,skd->kgqs", grad_grouped, value_rows, preferred_element_type=F32
        )
        probs_full = probs.astype(F32)
        inner = jnp.sum(probs_full * grad_probs, axis=-1, keepdims=True)
        grad_scores = (probs_full * (grad_probs - inner) * scale).astype(BF16)
        grad_query_rot = jnp.einsum(
            "kgqs,skd->qkgd", grad_scores, key, preferred_element_type=F32
        )
        grad_key_rot = jnp.einsum(
            "kgqs,qkgd->skd", grad_scores, grouped, preferred_element_type=F32
        )
        grad_query_act = apply_rotation(
            grad_query_rot.reshape(tree_len, local_q, HEAD_SIZE), cosine_table, sine_table, -1.0
        )
        grad_key_act = apply_rotation(grad_key_rot, cosine_table, sine_table, -1.0)
        grad_qkv = jnp.concatenate(
            [
                grad_query_act.astype(BF16).reshape(tree_len, q_width),
                grad_key_act.astype(BF16).reshape(tree_len, kv_width),
                grad_value_act.astype(BF16).reshape(tree_len, kv_width),
            ],
            1,
        )
        grad_normed_a = scatter_tensor(dot_nt(grad_qkv, w_qkv).reshape(tp, rows, model))
        grad_input = norm_back(grad_normed_a, gain_a, scaled_a, inverse_a)
        grad_tokens = relative((grad_mixed + grad_input).astype(BF16), zi)
        grad_wa = jnp.concatenate(
            [
                dot_tn(normed_all, grad_qkv).astype(BF16),
                dot_tn(grad_mixed_all, attended).astype(BF16),
            ],
            1,
        ).reshape(outer, 2, shard, qkv_width + q_width)
        keep = jnp.where(upper_x, grad_wa[:, 1], grad_wa[:, 0])
        send = jnp.where(upper_x, grad_wa[:, 0], grad_wa[:, 1])
        pair_sum = keep.astype(F32) + swap(send, X).astype(F32)
        far = pair_sum.astype(BF16)
        total_a = pair_sum[0]
        for k in range(1, outer):
            total_a = total_a + swap(far[k], zmask(k)).astype(F32)
        grad_query = total_a[:, :q_width]
        grad_key = total_a[:, q_width : q_width + kv_width]
        grad_value = total_a[:, q_width + kv_width : qkv_width]
        grad_out = total_a[:, qkv_width:].T

        gain_sum_a = (
            jnp.sum(w_query.astype(F32) * grad_query, 1)
            + jnp.sum(key_matrix.astype(F32) * grad_key, 1)
            + jnp.sum(value_matrix.astype(F32) * grad_value, 1)
        )
        gain_sum_m = jnp.sum(w_gate.astype(F32) * grad_gate, 1) + jnp.sum(
            w_up.astype(F32) * grad_up, 1
        )

        def sum_tensor(v):
            v = v + swap(v, 1)
            return v + swap(v, 2)

        grad_attn_gain = sum_tensor(gain_sum_a) / attn_gain.astype(F32)
        grad_mlp_gain = sum_tensor(gain_sum_m) / mlp_gain.astype(F32)
        return (
            output,
            grad_tokens,
            grad_attn_gain,
            grad_query,
            grad_key,
            grad_value,
            grad_out,
            grad_mlp_gain,
            grad_gate,
            grad_up,
            grad_down.T,
        )

    return body


def solution(mesh):
    in_specs = (
        P(("dp", "tensor"), None),
        P("dp", None),
        P("dp"),
        P("dp", "tensor"),
        P("dp", "tensor"),
        P("dp", "tensor"),
        P("tensor", "dp"),
        P("dp"),
        P("dp", "tensor"),
        P("dp", "tensor"),
        P("tensor", "dp"),
        P(("dp", "tensor"), None),
    )
    out_specs = (
        P(("dp", "tensor"), None),
        P(("dp", "tensor"), None),
        P("dp"),
        P("dp", "tensor"),
        P("dp", "tensor"),
        P("dp", "tensor"),
        P("tensor", "dp"),
        P("dp"),
        P("dp", "tensor"),
        P("dp", "tensor"),
        P("tensor", "dp"),
    )
    body = make_body(mesh.shape["dp"], mesh.shape["tensor"])
    return jax.shard_map(body, mesh=mesh, in_specs=in_specs, out_specs=out_specs, check_vma=False)
```

```python
import functools

import jax
import jax.numpy as jnp
from jax import lax
from jax.experimental import pallas as pl
from jax.experimental.pallas import tpu as pltpu
from jax.sharding import PartitionSpec as P

HEAD_SIZE = 256
BLK = 128


EPS = 1e-06
THETA = 1000042.0
NEG = -1e30
HIGH = lax.Precision.HIGHEST
F32 = jnp.float32
BF16 = jnp.bfloat16
MESH = pl.DeviceIdType.MESH
VMEM_LIMIT = 56 * 2**20


def tree_tables(parent_row, tree_len, block_len):
    blocks = parent_row.shape[0]
    nodes = jnp.arange(blocks, dtype=jnp.int32)
    hops = (parent_row[:, None] == nodes[None, :]).astype(F32)
    reach = jnp.eye(blocks, dtype=F32)
    walk = reach
    for hop_count in range(blocks):
        walk = jnp.dot(walk, hops, precision=HIGH)
        reach = jnp.maximum(reach, walk)
    depth = jnp.sum(reach, axis=1) - 1.0
    rows = jnp.arange(tree_len, dtype=jnp.int32)
    member = (rows[:, None] // block_len == nodes[None, :]).astype(F32)
    visible = jnp.dot(jnp.dot(member, reach, precision=HIGH), member.T, precision=HIGH) > 0.5
    allowed_mask = visible & (rows[None, :] <= rows[:, None])
    place = jnp.dot(member, depth, precision=HIGH) * block_len + (rows % block_len).astype(F32)
    return (allowed_mask, place)


def rope_tables(place, head_dim):
    half = head_dim // 2
    freq = THETA ** (-2.0 * jnp.arange(half, dtype=F32) / head_dim)
    angle = place[:, None] * freq[None, :]
    return (jnp.cos(angle), jnp.sin(angle))


def rotate(values, cosine, sine, sign):
    half = values.shape[-1] // 2
    first, second = values[..., :half], values[..., half:]
    return jnp.concatenate(
        [first * cosine - sign * second * sine, second * cosine + sign * first * sine], -1
    )


def normalize(values):
    inverse = lax.rsqrt(jnp.mean(values * values, axis=-1, keepdims=True) + EPS)
    return (values * inverse, inverse)


def norm_back(grad_scaled, scaled, inverse):
    inner = jnp.mean(grad_scaled * scaled, axis=-1, keepdims=True)
    return inverse * (grad_scaled - scaled * inner)


def dot_nn(left, right):
    return jnp.dot(left, right, preferred_element_type=F32)


def dot_nt(left, right):
    return lax.dot_general(left, right, (((1,), (1,)), ((), ())), preferred_element_type=F32)


def dot_tn(left, right):
    return lax.dot_general(left, right, (((0,), (0,)), ((), ())), preferred_element_type=F32)


def flip(index, mask):
    out = index
    bit = 1
    while bit <= mask:
        if mask & bit:
            out = out + bit * (1 - 2 * (index // bit % 2))
        bit *= 2
    return out


class Links:
    def __init__(self, tp, send_sems, recv_sems, local_sems):
        self.tp = tp
        self.di = lax.axis_index("dp")
        self.ti = lax.axis_index("tensor")
        self.send_sems, self.recv_sems, self.local_sems = send_sems, recv_sems, local_sems
        self.used = 0
        self.used_local = 0

    def partner(self, mask):
        return (flip(self.di, mask // self.tp), flip(self.ti, mask % self.tp))

    def greet(self, masks):
        barrier = pltpu.get_barrier_semaphore()
        for mask in masks:
            pl.semaphore_signal(barrier, inc=1, device_id=self.partner(mask), device_id_type=MESH)
        pl.semaphore_wait(barrier, len(masks))

    def remote(self, src, dst, mask):
        index = self.used
        self.used += 1
        return pltpu.make_async_remote_copy(
            src_ref=src,
            dst_ref=dst,
            send_sem=self.send_sems.at[index],
            recv_sem=self.recv_sems.at[index],
            device_id=self.partner(mask),
            device_id_type=MESH,
        )

    def send(self, src, dst, mask):
        copy = self.remote(src, dst, mask)
        copy.start()
        return copy

    def local(self, src, dst):
        copy = pltpu.make_async_copy(src, dst, self.local_sems.at[self.used_local])
        self.used_local += 1
        copy.start()
        return copy


class Spread:
    def __init__(self, links, outer, block_of):
        self.links, self.outer = links, outer
        self.block_of = block_of
        self.zi = links.di // 2
        self.middle = (self.zi == 1) | (self.zi == 2)

    def start(self):
        links, at = self.links, self.block_of
        step = 2 * links.tp
        self.copies = {}
        if self.outer != 4:
            for k in range(1, self.outer):
                self.copies[k] = links.send(at(0), at(k), k * step)
            return
        self.copies[2] = links.send(at(0), at(2), 2 * step)
        self.copies[1] = links.send(at(0), at(1), step)
        self.copies[3] = links.remote(at(0), at(3), 3 * step)
        self.onward = links.remote(at(2), at(3), step)

        @pl.when(self.middle)
        def _():
            self.copies[3].start()

    def forward(self):
        if self.outer != 4:
            return
        self.copies[2].wait_recv()

        @pl.when(self.middle)
        def _():
            self.onward.start()

    def arrive(self, k):
        if self.outer != 4 or k == 1:
            self.copies[k].wait_recv()
        elif k == 3:

            @pl.when(self.middle)
            def _():
                self.copies[3].wait_recv()

            @pl.when(jnp.logical_not(self.middle))
            def _():
                self.onward.wait_recv()

    def sent(self):
        if self.outer != 4:
            for copy in self.copies.values():
                copy.wait_send()
            return
        self.copies[1].wait_send()
        self.copies[2].wait_send()

        @pl.when(self.middle)
        def _():
            self.copies[3].wait_send()
            self.onward.wait_send()


def gather_units(links, full, rows):
    tp = links.tp

    def block(m, lo=0, n=None):
        return full.at[pl.ds(m * rows + lo, rows if n is None else n)]

    half = rows // 2
    sent = []

    def send(m, mask, lo=0, n=None):
        copy = links.send(block(m, lo, n), block(m ^ mask, lo, n), mask)
        sent.append(copy)
        return copy

    x = send(0, tp)
    y = send(0, 2)
    c0 = send(0, 1)
    yield
    y.wait_recv()
    low = send(2, tp, half, half)
    c2 = send(2, 1)
    x.wait_recv()
    high = send(tp, 2, 0, half)
    c4 = send(tp, 1)
    yield
    low.wait_recv()
    high.wait_recv()
    c6 = send(tp + 2, 1)
    yield
    for copy in (c0, c2, c4, c6):
        copy.wait_recv()
    for copy in sent:
        copy.wait_send()
    yield


def run(stages):
    for _ in stages:
        pass


def pipe(body, grid, in_specs, out_specs, *refs):
    pltpu.emit_pipeline(body, grid=grid, in_specs=in_specs, out_specs=out_specs)(*refs)


def rows_spec(rows, width):
    return pl.BlockSpec((rows, width), lambda i: (i, 0))


def whole_spec(rows, width):
    return pl.BlockSpec((rows, width), lambda i: (0, 0))


def forward_kernel(
    outer,
    tp,
    wa,
    wg,
    wu,
    wd,
    x,
    xh,
    cot,
    cosine,
    sine,
    bias,
    wa_all,
    gate_w,
    up_w,
    down_w,
    xh_all,
    qkv,
    probs,
    att,
    x1,
    h2,
    cot_all,
    gate,
    upper,
    hid,
    grad_down,
    part,
    got_c,
    got_y,
    far,
    send_sems,
    recv_sems,
    local_sems,
):
    links = Links(tp, send_sems, recv_sems, local_sems)
    step = 2 * tp
    shard, attn_width = wa.shape
    units = gate_w.shape[1]
    rows, model = xh.shape
    tree_len = rows * tp
    q_width = att.shape[1]
    qkv_width = qkv.shape[1]
    kv_width = (qkv_width - q_width) // 2
    xi = links.di % 2
    ti = links.ti
    links.greet([1, 2, tp] + [k * step for k in range(1, outer)])

    def tree_rows(mask):
        return pl.ds(pl.multiple_of(flip(ti, mask) * rows, rows), rows)

    own_wa = wa_all.at[pl.ds(pl.multiple_of(xi * shard, shard), shard)]
    own_copy = links.local(wa, own_wa)
    here = [links.local(xh, xh_all.at[tree_rows(0)])]

    def wa_block(k):
        return wa_all.at[pl.ds(pl.multiple_of((2 * k + xi) * shard, shard), shard)]

    tok_y = links.send(xh, xh_all.at[tree_rows(0)], 2)
    tok_c = links.send(xh, xh_all.at[tree_rows(0)], 1)
    own_copy.wait()
    attn = Spread(links, outer, wa_block)
    attn.start()
    across = [links.send(wa_block(0), wa_block(0), tp)]
    mine = pl.ds(pl.multiple_of(xi * units, units), units)
    peers = pl.ds(pl.multiple_of((1 - xi) * units, units), units)
    place = pl.ds(pl.multiple_of(xi * shard, shard), shard)
    pair = []
    for w, full in ((wg, gate_w), (wu, up_w), (wd, down_w)):
        here.append(links.local(w.at[:, mine], full.at[place]))
        pair.append(links.send(w.at[:, peers], full.at[place], tp))
    tok_y.wait_recv()
    tok_yc = links.send(xh_all.at[tree_rows(2)], xh_all.at[tree_rows(2)], 1)

    def mlp_spread(full):
        return Spread(links, outer, lambda k: full.at[pl.ds(k * 2 * shard, 2 * shard)])

    attn.forward()
    for k in range(1, outer):
        if k != 2 or outer != 4:
            attn.arrive(k)
        across.append(links.send(wa_block(k), wa_block(k), tp))
    for copy in here:
        copy.wait()
    spreads = [mlp_spread(full) for full in (gate_w, up_w, down_w)]
    pair[0].wait_recv()
    spreads[0].start()
    pair[1].wait_recv()
    spreads[1].start()
    pair[2].wait_recv()
    tok_c.wait_recv()
    tok_yc.wait_recv()
    for copy in across:
        copy.wait_recv()

    head = HEAD_SIZE

    def project(x_ref, w_ref, cos_ref, sin_ref, out_ref):
        raw = dot_nn(x_ref[...], w_ref[...])
        for slot in range((q_width + kv_width) // head):
            cols = slice(slot * head, (slot + 1) * head)
            out_ref[:, cols] = rotate(raw[:, cols], cos_ref[...], sin_ref[...], 1.0).astype(BF16)
        out_ref[:, q_width + kv_width :] = raw[:, q_width + kv_width :].astype(BF16)

    pipe(
        project,
        (tp,),
        [
            rows_spec(rows, model),
            whole_spec(model, qkv_width),
            rows_spec(rows, head // 2),
            rows_spec(rows, head // 2),
        ],
        [rows_spec(rows, qkv_width)],
        xh_all,
        wa_all.at[:, pl.ds(0, qkv_width)],
        cosine,
        sine,
        qkv,
    )
    spreads[0].forward()

    group = q_width // kv_width

    def attend(q_ref, k_ref, v_ref, b_ref, p_ref, o_ref):
        scores = dot_nt(q_ref[...], k_ref[...]) * (head**-0.5) + b_ref[...].astype(F32)
        weights = jnp.exp(scores - jnp.max(scores, axis=-1, keepdims=True))
        weights = (weights / jnp.sum(weights, axis=-1, keepdims=True)).astype(BF16)
        p_ref[0] = weights
        o_ref[...] = dot_nn(weights, v_ref[...]).astype(BF16)

    pipe(
        attend,
        (tp, q_width // head),
        [
            pl.BlockSpec((rows, head), lambda i, h: (i, h)),
            pl.BlockSpec((tree_len, head), lambda i, h: (0, q_width // head + h // group)),
            pl.BlockSpec((tree_len, head), lambda i, h: (0, (q_width + kv_width) // head + h // group)),
            pl.BlockSpec((rows, tree_len), lambda i, h: (i, 0)),
        ],
        [
            pl.BlockSpec((1, rows, tree_len), lambda i, h: (h, i, 0)),
            pl.BlockSpec((rows, head), lambda i, h: (i, h)),
        ],
        qkv,
        qkv,
        qkv,
        bias,
        probs,
        att,
    )

    def out_project(a_ref, w_ref, o_ref):
        o_ref[...] = dot_nt(a_ref[...], w_ref[...]).astype(BF16)

    pipe(
        out_project,
        (tp,),
        [rows_spec(rows, q_width), whole_spec(model, q_width)],
        [rows_spec(rows, model)],
        att,
        wa_all.at[:, pl.ds(qkv_width, q_width)],
        part,
    )
    rc = [
        links.send(part.at[tree_rows(3)], got_c.at[1], 1),
        links.send(part.at[tree_rows(1)], got_c.at[0], 1),
    ]
    spreads[1].forward()
    spreads[2].start()
    strip = rows // 4

    def add(a_ref, b_ref, o_ref):
        o_ref[...] = (a_ref[...].astype(F32) + b_ref[...].astype(F32)).astype(BF16)

    rc[0].wait_recv()
    spec = rows_spec(strip, model)
    pipe(add, (4,), [spec, spec], [spec], part.at[tree_rows(2)], got_c.at[1], far)
    ry = links.send(far, got_y, 2)
    rc[1].wait_recv()
    ry.wait_recv()

    def residual(x_ref, a_ref, b_ref, c_ref, x1_ref, h_ref):
        total = x_ref[...] + (
            a_ref[...].astype(F32) + b_ref[...].astype(F32) + c_ref[...].astype(F32)
        )
        x1_ref[...] = total
        h_ref[...] = normalize(total)[0].astype(BF16)

    pipe(
        residual,
        (4,),
        [spec] * 4,
        [spec] * 2,
        x,
        part.at[tree_rows(0)],
        got_c.at[0],
        got_y,
        x1,
        h2.at[pl.ds(0, rows)],
    )
    run(gather_units(links, h2, rows))
    here_c = links.local(cot, cot_all.at[pl.ds(0, rows)])
    here_c.wait()
    stages = gather_units(links, cot_all, rows)
    next(stages)

    for spread in spreads[:2]:
        for k in range(1, outer):
            spread.arrive(k)
    next(stages)

    def expand(x_ref, g_ref, u_ref, go_ref, uo_ref, h_ref):
        g = dot_nn(x_ref[...], g_ref[...])
        u = dot_nn(x_ref[...], u_ref[...])
        go_ref[...] = g.astype(BF16)
        uo_ref[...] = u.astype(BF16)
        h_ref[...] = (g * jax.nn.sigmoid(g) * u).astype(BF16)

    pipe(
        expand,
        (2 * tp,),
        [rows_spec(rows, model), whole_spec(model, units), whole_spec(model, units)],
        [rows_spec(rows, units)] * 3,
        h2,
        gate_w,
        up_w,
        gate,
        upper,
        hid,
    )
    spreads[2].forward()
    run(stages)

    def weight_grad(a_ref, b_ref, o_ref):
        o_ref[...] = dot_tn(a_ref[...], b_ref[...]).astype(BF16)

    tokens = 2 * tree_len
    pipe(
        weight_grad,
        (4,),
        [pl.BlockSpec((tokens, model // 4), lambda i: (0, i)), whole_spec(tokens, units)],
        [rows_spec(model // 4, units)],
        cot_all,
        hid,
        grad_down,
    )
    for k in range(1, outer):
        spreads[2].arrive(k)
    for spread in spreads + [attn]:
        spread.sent()
    for copy in across + pair + rc + [tok_y, tok_c, tok_yc, ry]:
        copy.wait_send()


def forward_call(outer, tp, wa, wg, wu, wd, x, xh, cot, cosine, sine, bias, q_width, qkv_width):
    shard, attn_width = wa.shape
    rows, model = xh.shape
    tree_len = rows * tp
    units = wg.shape[1] // 2
    heads = q_width // HEAD_SIZE

    def out(shape, dtype=BF16):
        return jax.ShapeDtypeStruct(shape, dtype)

    shapes = [
        out((model, attn_width)),
        out((model, units)),
        out((model, units)),
        out((model, units)),
        out((tree_len, model)),
        out((tree_len, qkv_width)),
        out((heads, tree_len, tree_len)),
        out((tree_len, q_width)),
        out((rows, model), F32),
        out((2 * tree_len, model)),
        out((2 * tree_len, model)),
        out((2 * tree_len, units)),
        out((2 * tree_len, units)),
        out((2 * tree_len, units)),
        out((model, units)),
        out((tree_len, model)),
        out((2, rows, model)),
        out((rows, model)),
        out((rows, model)),
    ]
    count = 40 + 5 * outer
    return pl.pallas_call(
        functools.partial(forward_kernel, outer, tp),
        out_shape=shapes,
        in_specs=[pl.BlockSpec(memory_space=pl.ANY)] * 10,
        out_specs=[pl.BlockSpec(memory_space=pl.ANY)] * len(shapes),
        scratch_shapes=[
            pltpu.SemaphoreType.DMA((count,)),
            pltpu.SemaphoreType.DMA((count,)),
            pltpu.SemaphoreType.DMA((12,)),
        ],
        compiler_params=pltpu.CompilerParams(
            collective_id=0, has_side_effects=True, vmem_limit_bytes=VMEM_LIMIT
        ),
        name="layer_forward",
    )(wa, wg, wu, wd, x, xh, cot, cosine, sine, bias)


def make_body(dp, tp):
    devices = dp * tp
    outer = dp // 2
    assert tp == 4 and dp == 2 * outer and outer & (outer - 1) == 0
    X = tp

    def swap(value, mask):
        return lax.ppermute(value, ("dp", "tensor"), [(i, i ^ mask) for i in range(devices)])

    def zmask(k):
        return k * 2 * tp

    def relative(value, zi):
        width = value.shape[-1] // outer
        step = 1
        while step < outer:
            blocks = [value[..., i * width : (i + 1) * width] for i in range(outer)]
            swapped = jnp.concatenate([blocks[i ^ step] for i in range(outer)], -1)
            value = jnp.where((zi // step) % 2 == 1, swapped, value)
            step *= 2
        return value

    def scatter_units(part):
        rows = part.shape[1] // 2
        got = swap(jnp.stack([part[1], part[3], part[5], part[7]]), 1).astype(F32)
        s0 = part[0].astype(F32) + got[0]
        sy = part[2].astype(F32) + got[1]
        sx = part[4].astype(F32) + got[2]
        sxy = (part[6].astype(F32) + got[3]).astype(BF16)
        top = swap(sxy[:rows], X).astype(F32)
        bottom = swap(sxy[rows:], 2).astype(F32)
        sy = jnp.concatenate([sy[:rows] + top, sy[rows:]], 0).astype(BF16)
        sx = jnp.concatenate([sx[:rows], sx[rows:] + bottom], 0).astype(BF16)
        return s0 + swap(sy, 2).astype(F32) + swap(sx, X).astype(F32)

    def body(
        tokens,
        parents,
        attn_gain,
        w_query,
        key_matrix,
        value_matrix,
        w_out,
        mlp_gain,
        w_gate,
        w_up,
        w_down,
        cotangent,
    ):
        di = lax.axis_index("dp")
        ti = lax.axis_index("tensor")
        zi = di // 2
        upper_x = di % 2 == 1
        rows, model = tokens.shape
        tree_len = rows * tp
        q_width = w_query.shape[1]
        kv_width = key_matrix.shape[1]
        local_q = q_width // HEAD_SIZE
        local_kv = kv_width // HEAD_SIZE
        group = local_q // local_kv
        qkv_width = q_width + 2 * kv_width
        shard = w_query.shape[0]
        units = w_gate.shape[1] // 2
        scale = HEAD_SIZE ** (-0.5)
        gain_a = attn_gain.astype(F32)[:, None]
        gain_m = mlp_gain.astype(F32)[:, None]

        def order_x(mine, theirs, axis):
            low = jnp.where(upper_x, theirs, mine)
            high = jnp.where(upper_x, mine, theirs)
            return jnp.concatenate([low, high], axis)

        w_qkv_own = jnp.concatenate([w_query, key_matrix, value_matrix], 1).astype(F32)
        wa = jnp.concatenate([(w_qkv_own * gain_a).astype(BF16), w_out.T], 1)
        wg = (w_gate.astype(F32) * gain_m).astype(BF16)
        wu = (w_up.astype(F32) * gain_m).astype(BF16)
        allowed_mask, place = tree_tables(parents[0], tree_len, BLK)
        cosine, sine = rope_tables(place, HEAD_SIZE)
        bias = jnp.where(allowed_mask, 0.0, NEG).astype(BF16)
        inputs = relative(tokens, zi).astype(F32)
        scaled_a, inverse_a = normalize(inputs)
        cot = relative(cotangent, zi)
        (
            wa_all,
            gate_w,
            up_w,
            down_w,
            normed_all,
            qkv,
            probs,
            attended,
            mixed,
            normed_m_all,
            cot_all,
            gate,
            upper,
            hidden,
            grad_down,
        ) = forward_call(
            outer,
            tp,
            wa,
            wg,
            wu,
            w_down.T,
            inputs,
            scaled_a.astype(BF16),
            cot,
            cosine,
            sine,
            bias,
            q_width,
            qkv_width,
        )[:15]
        w_qkv = wa_all[:, :qkv_width]
        w_o = wa_all[:, qkv_width:]
        query_rows = qkv[:, :q_width]
        key = qkv[:, q_width : q_width + kv_width].reshape(tree_len, local_kv, HEAD_SIZE)
        value_rows = qkv[:, q_width + kv_width :].reshape(tree_len, local_kv, HEAD_SIZE)
        grouped = query_rows.reshape(tree_len, local_kv, group, HEAD_SIZE)
        probs = probs.reshape(local_kv, group, tree_len, tree_len)

        scaled_m, inverse_m = normalize(mixed)
        gate = gate.astype(F32)
        sigma = jax.nn.sigmoid(gate)
        grad_hidden = dot_nn(cot_all, down_w)
        grad_gate_act = (
            grad_hidden * upper.astype(F32) * sigma * (1.0 + gate * (1.0 - sigma))
        ).astype(BF16)
        grad_up_act = (grad_hidden * gate * sigma).astype(BF16)
        grad_normed_m = scatter_units(
            (dot_nt(grad_gate_act, gate_w) + dot_nt(grad_up_act, up_w))
            .astype(BF16)
            .reshape(2 * tp, rows, model)
        )
        grad_mixed = cot.astype(F32) + norm_back(grad_normed_m, scaled_m, inverse_m)
        grad_gate = dot_tn(normed_m_all, grad_gate_act).astype(BF16)
        grad_up = dot_tn(normed_m_all, grad_up_act).astype(BF16)
        mlp_part = dot_nt(hidden, down_w).astype(BF16).reshape(2 * tp, rows, model)
        output = relative((mixed + scatter_units(mlp_part)).astype(BF16), zi)

        def reduce_z(grad):
            block = grad.reshape(outer, 2 * shard, grad.shape[1])
            total = block[0].astype(F32)
            for k in range(1, outer):
                total = total + swap(block[k], zmask(k)).astype(F32)
            return total

        def unpaired(grad):
            s = reduce_z(grad)
            keep = jnp.where(upper_x, s[shard:], s[:shard])
            send = jnp.where(upper_x, s[:shard], s[shard:]).astype(BF16)
            return order_x(keep, swap(send, X).astype(F32), 1)

        grad_down = unpaired(grad_down)
        grad_gate = unpaired(grad_gate)
        grad_up = unpaired(grad_up)

        order = [(ti ^ j) * rows for j in range(tp)]

        def gather_tensor(a0):
            a1 = swap(a0, 1)
            a2 = swap(a0, 2)
            a3 = swap(a2, 1)
            full = jnp.zeros((tree_len, model), a0.dtype)
            for start, a in zip(order, (a0, a1, a2, a3)):
                full = lax.dynamic_update_slice(full, a, (start, 0))
            return full

        def scatter_tensor(part):
            blocks = [lax.dynamic_slice(part, (start, 0), (rows, model)) for start in order]
            b = [block.astype(BF16) for block in blocks]
            got = swap(jnp.stack([b[1], b[3]]), 1).astype(F32)
            far = (blocks[2] + got[1]).astype(BF16)
            return blocks[0] + got[0] + swap(far, 2).astype(F32)

        grad_mixed_all = gather_tensor(grad_mixed.astype(BF16))
        grad_attended = dot_nn(grad_mixed_all, w_o).astype(BF16)
        grad_grouped = grad_attended.reshape(tree_len, local_kv, group, HEAD_SIZE)
        grad_value_act = jnp.einsum(
            "kgqs,qkgd->skd", probs, grad_grouped, preferred_element_type=F32
        )
        grad_probs = jnp.einsum(
            "qkgd,skd->kgqs", grad_grouped, value_rows, preferred_element_type=F32
        )
        probs_full = probs.astype(F32)
        inner = jnp.sum(probs_full * grad_probs, axis=-1, keepdims=True)
        grad_scores = (probs_full * (grad_probs - inner) * scale).astype(BF16)
        grad_query_rot = jnp.einsum(
            "kgqs,skd->qkgd", grad_scores, key, preferred_element_type=F32
        )
        grad_key_rot = jnp.einsum(
            "kgqs,qkgd->skd", grad_scores, grouped, preferred_element_type=F32
        )
        turn_back = (cosine[:, None], sine[:, None], -1.0)
        grad_query_act = rotate(
            grad_query_rot.reshape(tree_len, local_q, HEAD_SIZE), *turn_back
        )
        grad_key_act = rotate(grad_key_rot, *turn_back)
        grad_qkv = jnp.concatenate(
            [
                grad_query_act.astype(BF16).reshape(tree_len, q_width),
                grad_key_act.astype(BF16).reshape(tree_len, kv_width),
                grad_value_act.astype(BF16).reshape(tree_len, kv_width),
            ],
            1,
        )
        grad_normed_a = scatter_tensor(dot_nt(grad_qkv, w_qkv))
        grad_input = norm_back(grad_normed_a, scaled_a, inverse_a)
        grad_tokens = relative((grad_mixed + grad_input).astype(BF16), zi)
        grad_wa = jnp.concatenate(
            [
                dot_tn(normed_all, grad_qkv).astype(BF16),
                dot_tn(grad_mixed_all, attended).astype(BF16),
            ],
            1,
        ).reshape(outer, 2, shard, qkv_width + q_width)
        keep = jnp.where(upper_x, grad_wa[:, 1], grad_wa[:, 0])
        send = jnp.where(upper_x, grad_wa[:, 0], grad_wa[:, 1])
        pair_sum = keep.astype(F32) + swap(send, X).astype(F32)
        far = pair_sum.astype(BF16)
        total_a = pair_sum[0]
        for k in range(1, outer):
            total_a = total_a + swap(far[k], zmask(k)).astype(F32)

        grad_qkv_w = total_a[:, :qkv_width]
        gain_sum_a = jnp.sum(w_qkv_own * grad_qkv_w, 1)
        gain_sum_m = jnp.sum(w_gate.astype(F32) * grad_gate, 1) + jnp.sum(
            w_up.astype(F32) * grad_up, 1
        )
        grad_qkv_w = grad_qkv_w * gain_a

        def sum_tensor(v):
            v = v + swap(v, 1)
            return v + swap(v, 2)

        return (
            output,
            grad_tokens,
            sum_tensor(gain_sum_a),
            grad_qkv_w[:, :q_width],
            grad_qkv_w[:, q_width : q_width + kv_width],
            grad_qkv_w[:, q_width + kv_width :],
            total_a[:, qkv_width:].T,
            sum_tensor(gain_sum_m),
            grad_gate * gain_m,
            grad_up * gain_m,
            grad_down.T,
        )

    return body


def solution(mesh):
    in_specs = (
        P(("dp", "tensor"), None),
        P("dp", None),
        P("dp"),
        P("dp", "tensor"),
        P("dp", "tensor"),
        P("dp", "tensor"),
        P("tensor", "dp"),
        P("dp"),
        P("dp", "tensor"),
        P("dp", "tensor"),
        P("tensor", "dp"),
        P(("dp", "tensor"), None),
    )
    out_specs = (
        P(("dp", "tensor"), None),
        P(("dp", "tensor"), None),
        P("dp"),
        P("dp", "tensor"),
        P("dp", "tensor"),
        P("dp", "tensor"),
        P("tensor", "dp"),
        P("dp"),
        P("dp", "tensor"),
        P("dp", "tensor"),
        P("tensor", "dp"),
    )
    body = make_body(mesh.shape["dp"], mesh.shape["tensor"])
    return jax.shard_map(body, mesh=mesh, in_specs=in_specs, out_specs=out_specs, check_vma=False)
```

```python
import functools

import jax
import jax.numpy as jnp
from jax import lax
from jax.experimental import pallas as pl
from jax.experimental.pallas import tpu as pltpu
from jax.sharding import PartitionSpec as P

HEAD_SIZE = 256
BLK = 128


EPS = 1e-06
THETA = 1000042.0
NEG = -1e30
HIGH = lax.Precision.HIGHEST
F32 = jnp.float32
BF16 = jnp.bfloat16
MESH = pl.DeviceIdType.MESH
VMEM_LIMIT = 56 * 2**20


def tree_tables(parent_row, tree_len, block_len):
    blocks = parent_row.shape[0]
    nodes = jnp.arange(blocks, dtype=jnp.int32)
    hops = (parent_row[:, None] == nodes[None, :]).astype(F32)
    reach = jnp.eye(blocks, dtype=F32)
    walk = reach
    for hop_count in range(blocks):
        walk = jnp.dot(walk, hops, precision=HIGH)
        reach = jnp.maximum(reach, walk)
    depth = jnp.sum(reach, axis=1) - 1.0
    rows = jnp.arange(tree_len, dtype=jnp.int32)
    member = (rows[:, None] // block_len == nodes[None, :]).astype(F32)
    visible = jnp.dot(jnp.dot(member, reach, precision=HIGH), member.T, precision=HIGH) > 0.5
    allowed_mask = visible & (rows[None, :] <= rows[:, None])
    place = jnp.dot(member, depth, precision=HIGH) * block_len + (rows % block_len).astype(F32)
    return (allowed_mask, place)


def rope_tables(place, head_dim):
    half = head_dim // 2
    freq = THETA ** (-2.0 * jnp.arange(half, dtype=F32) / head_dim)
    angle = place[:, None] * freq[None, :]
    return (jnp.cos(angle), jnp.sin(angle))


def rotate(values, cosine, sine, sign):
    half = values.shape[-1] // 2
    first, second = values[..., :half], values[..., half:]
    return jnp.concatenate(
        [first * cosine - sign * second * sine, second * cosine + sign * first * sine], -1
    )


def normalize(values):
    inverse = lax.rsqrt(jnp.mean(values * values, axis=-1, keepdims=True) + EPS)
    return (values * inverse, inverse)


def norm_back(grad_normed, gain, values):
    scaled, inverse = normalize(values)
    grad_scaled = grad_normed * gain
    inner = jnp.mean(grad_scaled * scaled, axis=-1, keepdims=True)
    return inverse * (grad_scaled - scaled * inner)


def dot_nn(left, right):
    return jnp.dot(left, right, preferred_element_type=F32)


def dot_nt(left, right):
    return lax.dot_general(left, right, (((1,), (1,)), ((), ())), preferred_element_type=F32)


def dot_tn(left, right):
    return lax.dot_general(left, right, (((0,), (0,)), ((), ())), preferred_element_type=F32)


def flip(index, mask):
    out = index
    bit = 1
    while bit <= mask:
        if mask & bit:
            out = out + bit * (1 - 2 * (index // bit % 2))
        bit *= 2
    return out


class Links:
    def __init__(self, tp, send_sems, recv_sems, local_sems):
        self.tp = tp
        self.di = lax.axis_index("dp")
        self.ti = lax.axis_index("tensor")
        self.send_sems, self.recv_sems, self.local_sems = send_sems, recv_sems, local_sems
        self.used = 0
        self.used_local = 0

    def partner(self, mask):
        return (flip(self.di, mask // self.tp), flip(self.ti, mask % self.tp))

    def greet(self, masks):
        barrier = pltpu.get_barrier_semaphore()
        for mask in masks:
            pl.semaphore_signal(barrier, inc=1, device_id=self.partner(mask), device_id_type=MESH)
        pl.semaphore_wait(barrier, len(masks))

    def remote(self, src, dst, mask):
        index = self.used
        self.used += 1
        return pltpu.make_async_remote_copy(
            src_ref=src,
            dst_ref=dst,
            send_sem=self.send_sems.at[index],
            recv_sem=self.recv_sems.at[index],
            device_id=self.partner(mask),
            device_id_type=MESH,
        )

    def send(self, src, dst, mask):
        copy = self.remote(src, dst, mask)
        copy.start()
        return copy

    def local(self, src, dst):
        copy = pltpu.make_async_copy(src, dst, self.local_sems.at[self.used_local])
        self.used_local += 1
        copy.start()
        return copy


def line_middle(links):
    zi = links.di // 2
    return (zi == 1) | (zi == 2)


class Spread:
    def __init__(self, links, outer, own, block):
        self.links, self.outer = links, outer
        step = 2 * links.tp
        self.middle = line_middle(links)
        self.copies = {k: links.remote(own, block(k), k * step) for k in range(1, outer)}
        if outer == 4:
            self.onward = links.remote(block(2), block(3), step)

    def start(self):
        if self.outer != 4:
            for copy in self.copies.values():
                copy.start()
            return
        self.copies[2].start()
        self.copies[1].start()

        @pl.when(self.middle)
        def _():
            self.copies[3].start()

    def forward(self):
        self.copies[2].wait_recv()
        if self.outer != 4:
            return

        @pl.when(self.middle)
        def _():
            self.onward.start()

    def arrive(self, k):
        if k == 1 or (self.outer != 4 and k != 2):
            self.copies[k].wait_recv()
        elif k == 3:

            @pl.when(self.middle)
            def _():
                self.copies[3].wait_recv()

            @pl.when(jnp.logical_not(self.middle))
            def _():
                self.onward.wait_recv()

    def sent(self):
        if self.outer != 4:
            for copy in self.copies.values():
                copy.wait_send()
            return
        self.copies[1].wait_send()
        self.copies[2].wait_send()

        @pl.when(self.middle)
        def _():
            self.copies[3].wait_send()
            self.onward.wait_send()


class ReduceZ:
    def __init__(self, links, outer, block, held, staged):
        self.links, self.outer, self.block, self.held, self.staged = (
            links,
            outer,
            block,
            held,
            staged,
        )
        step = 2 * links.tp
        self.middle = line_middle(links)
        self.copies = {k: links.remote(block(k), held.at[k], k * step) for k in range(1, outer)}
        if outer == 4:
            self.inward = links.remote(block(3), held.at[0], step)
            self.summed = links.remote(staged, held.at[2], 2 * step)

    def on_ends(self, *actions):
        @pl.when(jnp.logical_not(self.middle))
        def _():
            for action in actions:
                action()

    def on_middle(self, *actions):
        @pl.when(self.middle)
        def _():
            for action in actions:
                action()

    def start(self, k):
        if self.outer != 4 or k == 1:
            self.copies[k].start()
        elif k == 3:
            self.on_ends(self.inward.start)
            self.on_middle(self.copies[3].start)
        elif k == 2:
            self.on_ends(self.copies[2].start)

    def start_all(self):
        for k in range(self.outer - 1, 0, -1):
            self.start(k)

    def pump(self):
        if self.outer != 4:
            return

        def add():
            rows, width = self.staged.shape
            spec = rows_spec(min(rows, 128), width)
            add_pipe(spec, rows, self.block(2), self.held.at[0], self.staged)

        self.on_middle(self.inward.wait_recv, add, self.summed.start)

    def arrive(self):
        if self.outer != 4:
            for copy in self.copies.values():
                copy.wait_recv()
            return
        self.copies[1].wait_recv()
        self.on_middle(self.copies[2].wait_recv, self.copies[3].wait_recv)
        self.on_ends(self.summed.wait_recv)

    def total(self, lo, rows, out):
        width = self.staged.shape[1]
        spec = rows_spec(min(rows, 128), width)

        def add(*refs):
            value = refs[0][...].astype(F32)
            for ref in refs[1:-1]:
                value = value + ref[...].astype(F32)
            refs[-1][...] = value.astype(refs[-1].dtype)

        def over(kept):
            parts = [self.block(0)] + [self.held.at[k] for k in kept]
            parts = [part.at[pl.ds(lo, rows)] for part in parts]
            grid = (rows // min(rows, 128),)
            pipe(add, grid, [spec] * len(parts), [spec], *parts, out)

        if self.outer != 4:
            over(range(1, self.outer))
            return
        self.on_middle(lambda: over([1, 2, 3]))
        self.on_ends(lambda: over([1, 2]))

    def sent(self):
        if self.outer != 4:
            for copy in self.copies.values():
                copy.wait_send()
            return
        self.copies[1].wait_send()
        self.on_middle(self.copies[3].wait_send, self.summed.wait_send)
        self.on_ends(self.copies[2].wait_send, self.inward.wait_send)


def gather_units(links, full, rows):
    tp = links.tp

    def block(m, lo=0, n=None):
        return full.at[pl.ds(m * rows + lo, rows if n is None else n)]

    half = rows // 2
    sent = []

    def send(m, mask, lo=0, n=None):
        copy = links.send(block(m, lo, n), block(m ^ mask, lo, n), mask)
        sent.append(copy)
        return copy

    x = send(0, tp)
    y = send(0, 2)
    c0 = send(0, 1)
    yield
    y.wait_recv()
    low = send(2, tp, half, half)
    c2 = send(2, 1)
    x.wait_recv()
    high = send(tp, 2, 0, half)
    c4 = send(tp, 1)
    yield
    low.wait_recv()
    high.wait_recv()
    c6 = send(tp + 2, 1)
    yield
    for copy in (c0, c2, c4, c6):
        copy.wait_recv()
    for copy in sent:
        copy.wait_send()
    yield


def run(stages):
    for _ in stages:
        pass


def pipe(body, grid, in_specs, out_specs, *refs):
    pltpu.emit_pipeline(body, grid=grid, in_specs=in_specs, out_specs=out_specs)(*refs)


def rows_spec(rows, width):
    return pl.BlockSpec((rows, width), lambda i: (i, 0))


def whole_spec(rows, width):
    return pl.BlockSpec((rows, width), lambda i: (0, 0))


def add_refs(a_ref, b_ref, o_ref):
    o_ref[...] = (a_ref[...].astype(F32) + b_ref[...].astype(F32)).astype(o_ref.dtype)


def add_pipe(spec, rows, a, b, out):
    pipe(add_refs, (rows // spec.block_shape[0],), [spec, spec], [spec], a, b, out)


def nt_body(a_ref, b_ref, o_ref):
    o_ref[...] = dot_nt(a_ref[...], b_ref[...]).astype(BF16)


def nn_body(a_ref, b_ref, o_ref):
    o_ref[...] = dot_nn(a_ref[...], b_ref[...]).astype(BF16)


def tn_body(a_ref, b_ref, o_ref):
    o_ref[...] = dot_tn(a_ref[...], b_ref[...]).astype(BF16)


def weight_grad(acts, grads, out, blocks, first=0, count=None):
    tokens, model = acts.shape
    width = grads.shape[1]
    size = model // blocks
    count = blocks if count is None else count
    pipe(
        tn_body,
        (count,),
        [pl.BlockSpec((tokens, size), lambda i: (0, first + i)), whole_spec(tokens, width)],
        [pl.BlockSpec((size, width), lambda i: (first + i, 0))],
        acts,
        grads,
        out,
    )


class ScatterTensor:
    def __init__(self, links, part, got_c, got_y, far, rows):
        self.links, self.part, self.got_c, self.got_y, self.far = links, part, got_c, got_y, far
        self.rows = rows
        self.model = part.shape[1]
        self.spec = rows_spec(rows // 2, self.model)

    def block(self, mask):
        rows = self.rows
        return self.part.at[
            pl.ds(pl.multiple_of(flip(self.links.ti, mask) * rows, rows), rows)
        ]

    def start(self):
        self.copies = [
            self.links.send(self.block(3), self.got_c.at[1], 1),
            self.links.send(self.block(1), self.got_c.at[0], 1),
        ]

    def across(self):
        self.copies[0].wait_recv()
        add_pipe(self.spec, self.rows, self.block(2), self.got_c.at[1], self.far)
        self.copies.append(self.links.send(self.far, self.got_y, 2))

    def arrive(self):
        self.copies[1].wait_recv()
        self.copies[2].wait_recv()
        return [self.block(0), self.got_c.at[0], self.got_y]

    def sent(self):
        for copy in self.copies:
            copy.wait_send()


class ScatterUnits:
    def __init__(self, links, part, got_c, near, got, rows):
        self.links, self.part, self.got_c, self.near, self.got = links, part, got_c, near, got
        self.rows, self.model = rows, part.shape[1]
        self.sends = []

    def send(self, src, dst, mask):
        copy = self.links.send(src, dst, mask)
        self.sends.append(copy)
        return copy

    def block(self, m):
        return self.part.at[pl.ds(m * self.rows, self.rows)]

    def start(self):
        self.from_c = [self.send(self.block(2 * i + 1), self.got_c.at[i], 1) for i in range(4)]

    def add(self, m, slot, lo, n):
        rows = pl.ds(lo, n)
        add_pipe(
            rows_spec(n, self.model),
            n,
            self.block(m).at[rows],
            self.got_c.at[m // 2].at[rows],
            self.near.at[slot].at[rows],
        )

    def across(self):
        tp, rows, half = self.links.tp, self.rows, self.rows // 2
        low, high = pl.ds(0, half), pl.ds(half, half)
        near, got = self.near, self.got
        for copy in self.from_c:
            copy.wait_recv()
        self.add(6, 2, 0, half)
        self.top = self.send(near.at[2].at[low], got.at[2].at[low], tp)
        self.add(6, 2, half, half)
        self.bottom = self.send(near.at[2].at[high], got.at[2].at[high], 2)
        self.add(4, 0, 0, half)
        self.x_low = self.send(near.at[0].at[low], got.at[0].at[low], tp)
        self.add(2, 1, half, half)
        self.y_high = self.send(near.at[1].at[high], got.at[1].at[high], 2)

    def finish(self):
        tp, half = self.links.tp, self.rows // 2
        low, high = pl.ds(0, half), pl.ds(half, half)
        near, got = self.near, self.got

        def add3(m, slot, rows):
            def body(a_ref, b_ref, c_ref, o_ref):
                o_ref[...] = (
                    a_ref[...].astype(F32) + b_ref[...].astype(F32) + c_ref[...].astype(F32)
                ).astype(BF16)

            spec = rows_spec(half, self.model)
            pipe(
                body,
                (1,),
                [spec] * 3,
                [spec],
                self.block(m).at[rows],
                self.got_c.at[m // 2].at[rows],
                got.at[2].at[rows],
                near.at[slot].at[rows],
            )

        self.top.wait_recv()
        add3(2, 1, low)
        self.y_low = self.send(near.at[1].at[low], got.at[1].at[low], 2)
        self.bottom.wait_recv()
        add3(4, 0, high)
        self.x_high = self.send(near.at[0].at[high], got.at[0].at[high], tp)

    def arrive(self):
        for copy in (self.x_low, self.x_high, self.y_low, self.y_high):
            copy.wait_recv()
        return [self.block(0), self.got_c.at[0], self.got.at[0], self.got.at[1]]

    def sent(self):
        for copy in self.sends:
            copy.wait_send()


def sum_refs(refs):
    value = refs[0][...].astype(F32)
    for ref in refs[1:]:
        value = value + ref[...].astype(F32)
    return value


class GatherTree:
    def __init__(self, links, full, rows):
        self.links, self.full, self.rows = links, full, rows

    def block(self, mask):
        rows = self.rows
        return self.full.at[
            pl.ds(pl.multiple_of(flip(self.links.ti, mask) * rows, rows), rows)
        ]

    def start(self):
        self.y = self.links.send(self.block(0), self.block(0), 2)
        self.c = self.links.send(self.block(0), self.block(0), 1)

    def across(self):
        self.y.wait_recv()
        self.yc = self.links.send(self.block(2), self.block(2), 1)

    def arrive(self):
        self.c.wait_recv()
        self.yc.wait_recv()

    def sent(self):
        for copy in (self.y, self.c, self.yc):
            copy.wait_send()


def greet_all(links, outer):
    step = 2 * links.tp
    links.greet([1, 2, links.tp] + [k * step for k in range(1, outer)])


def forward_kernel(
    outer,
    tp,
    wa,
    wg,
    wu,
    wd,
    gn,
    x,
    xh,
    cot,
    cosine,
    sine,
    bias,
    wa_all,
    gate_w,
    up_w,
    down_w,
    gain_rows,
    h1,
    qkv,
    probs,
    att,
    x1,
    h2,
    cot_all,
    gate,
    upper,
    hid,
    grad_down,
    gn_all,
    part,
    got_c,
    got_y,
    far,
    send_sems,
    recv_sems,
    local_sems,
):
    links = Links(tp, send_sems, recv_sems, local_sems)
    shard, attn_width = wa.shape
    units = gate_w.shape[1]
    rows, model = xh.shape
    tree_len = rows * tp
    q_width = att.shape[1]
    qkv_width = qkv.shape[1]
    kv_width = (qkv_width - q_width) // 2
    head = HEAD_SIZE
    xi = links.di % 2
    greet_all(links, outer)

    def shard_block(full, k):
        return full.at[pl.ds(pl.multiple_of((2 * k + xi) * shard, shard), shard)]

    mine = pl.ds(pl.multiple_of(xi * units, units), units)
    peers = pl.ds(pl.multiple_of((1 - xi) * units, units), units)
    place = pl.ds(pl.multiple_of(xi * shard, shard), shard)

    def send_pair(w, full):
        return links.send(w.at[:, peers], full.at[place], tp)

    def mlp_spread(full):
        return Spread(
            links,
            outer,
            full.at[pl.ds(0, 2 * shard)],
            lambda k: full.at[pl.ds(k * 2 * shard, 2 * shard)],
        )

    gains = Spread(links, outer, gn, lambda k: shard_block(gn_all, k))
    attn = Spread(links, outer, wa, lambda k: shard_block(wa_all, k))
    gains.start()
    across_gn = [links.send(gn, shard_block(gn_all, 0), tp)]
    attn.start()
    across = [links.send(wa, shard_block(wa_all, 0), tp)]
    pair = [send_pair(wg, gate_w)]
    here = [
        links.local(gn, shard_block(gn_all, 0)),
        links.local(wa, shard_block(wa_all, 0)),
        links.local(cot, cot_all.at[pl.ds(0, rows)]),
    ]
    for w, full in ((wg, gate_w), (wu, up_w), (wd, down_w)):
        here.append(links.local(w.at[:, mine], full.at[place]))

    gains.forward()
    for k in range(1, outer):
        gains.arrive(k)
        across_gn.append(links.send(shard_block(gn_all, k), shard_block(gn_all, k), tp))
    for copy in across_gn:
        copy.wait_recv()
    for copy in here:
        copy.wait()

    def gain_rows_of(g_ref, o_ref):
        lane = lax.broadcasted_iota(jnp.int32, (8, 128), 1)
        row = lax.broadcasted_iota(jnp.int32, (8, 128), 0)
        pick = jnp.where((row < 2) & (lane == row * 64), 1.0, 0.0).astype(BF16)
        o_ref[...] = dot_nt(pick, g_ref[...])

    pipe(gain_rows_of, (1,), [whole_spec(model, 128)], [whole_spec(8, model)], gn_all, gain_rows)
    spec = rows_spec(rows // 2, model)
    gain_spec = whole_spec(8, model)

    def scale_tokens(x_ref, g_ref, o_ref):
        o_ref[...] = (x_ref[...] * g_ref[0:1]).astype(BF16)

    tree = GatherTree(links, h1, rows)
    pipe(scale_tokens, (2,), [spec, gain_spec], [spec], xh, gain_rows, tree.block(0))
    tree.start()

    spreads = [mlp_spread(full) for full in (gate_w, up_w, down_w)]
    attn.forward()
    across.append(links.send(shard_block(wa_all, 2), shard_block(wa_all, 2), tp))
    pair[0].wait_recv()
    spreads[0].start()
    tree.across()
    for k in range(1, outer):
        if k != 2:
            attn.arrive(k)
            across.append(links.send(shard_block(wa_all, k), shard_block(wa_all, k), tp))
        if k == 1:
            pair.append(send_pair(wu, up_w))
    pair.append(send_pair(wd, down_w))
    tree.arrive()
    pair[1].wait_recv()
    spreads[1].start()
    for copy in across:
        copy.wait_recv()

    def project(x_ref, w_ref, cos_ref, sin_ref, out_ref):
        raw = dot_nn(x_ref[...], w_ref[...])
        for slot in range((q_width + kv_width) // head):
            cols = slice(slot * head, (slot + 1) * head)
            out_ref[:, cols] = rotate(raw[:, cols], cos_ref[...], sin_ref[...], 1.0).astype(BF16)
        out_ref[:, q_width + kv_width :] = raw[:, q_width + kv_width :].astype(BF16)

    pipe(
        project,
        (tp,),
        [
            rows_spec(rows, model),
            whole_spec(model, qkv_width),
            rows_spec(rows, head // 2),
            rows_spec(rows, head // 2),
        ],
        [rows_spec(rows, qkv_width)],
        h1,
        wa_all.at[:, pl.ds(0, qkv_width)],
        cosine,
        sine,
        qkv,
    )
    spreads[0].forward()
    pair[2].wait_recv()
    spreads[2].start()

    group = q_width // kv_width

    def attend(q_ref, k_ref, v_ref, b_ref, p_ref, o_ref):
        scores = dot_nt(q_ref[...], k_ref[...]) * (head**-0.5) + b_ref[...].astype(F32)
        weights = jnp.exp(scores - jnp.max(scores, axis=-1, keepdims=True))
        weights = (weights / jnp.sum(weights, axis=-1, keepdims=True)).astype(BF16)
        p_ref[0] = weights
        o_ref[...] = dot_nn(weights, v_ref[...]).astype(BF16)

    k_at, v_at = q_width // head, (q_width + kv_width) // head
    pipe(
        attend,
        (tp, q_width // head),
        [
            pl.BlockSpec((rows, head), lambda i, h: (i, h)),
            pl.BlockSpec((tree_len, head), lambda i, h: (0, k_at + h // group)),
            pl.BlockSpec((tree_len, head), lambda i, h: (0, v_at + h // group)),
            pl.BlockSpec((rows, tree_len), lambda i, h: (i, 0)),
        ],
        [
            pl.BlockSpec((1, rows, tree_len), lambda i, h: (h, i, 0)),
            pl.BlockSpec((rows, head), lambda i, h: (i, h)),
        ],
        qkv,
        qkv,
        qkv,
        bias,
        probs,
        att,
    )
    pipe(
        nt_body,
        (tp,),
        [rows_spec(rows, q_width), whole_spec(model, q_width)],
        [rows_spec(rows, model)],
        att,
        wa_all.at[:, pl.ds(qkv_width, q_width)],
        part,
    )
    mixed = ScatterTensor(links, part, got_c, got_y, far, rows)
    mixed.start()
    mixed.across()
    parts = mixed.arrive()

    def residual(x_ref, a_ref, b_ref, c_ref, g_ref, x1_ref, h_ref):
        total = x_ref[...] + sum_refs((a_ref, b_ref, c_ref))
        x1_ref[...] = total
        h_ref[...] = (normalize(total)[0] * g_ref[1:2]).astype(BF16)

    pipe(
        residual,
        (2,),
        [spec] * 4 + [gain_spec],
        [spec] * 2,
        x,
        *parts,
        gain_rows,
        x1,
        h2.at[pl.ds(0, rows)],
    )
    stages = gather_units(links, h2, rows)
    next(stages)
    later = gather_units(links, cot_all, rows)
    next(later)
    next(stages)
    spreads[1].forward()
    next(stages)
    next(later)
    next(stages)

    for spread in spreads[:2]:
        for k in range(1, outer):
            spread.arrive(k)

    def expand(x_ref, g_ref, u_ref, go_ref, uo_ref, h_ref):
        g = dot_nn(x_ref[...], g_ref[...])
        u = dot_nn(x_ref[...], u_ref[...])
        go_ref[...] = g.astype(BF16)
        uo_ref[...] = u.astype(BF16)
        h_ref[...] = (g * jax.nn.sigmoid(g) * u).astype(BF16)

    pipe(
        expand,
        (2 * tp,),
        [rows_spec(rows, model), whole_spec(model, units), whole_spec(model, units)],
        [rows_spec(rows, units)] * 3,
        h2,
        gate_w,
        up_w,
        gate,
        upper,
        hid,
    )
    run(later)
    spreads[2].forward()
    weight_grad(cot_all, hid, grad_down, 4)
    for k in range(1, outer):
        spreads[2].arrive(k)
    for spread in [gains, attn] + spreads:
        spread.sent()
    for copy in across_gn + across + pair:
        copy.wait_send()
    tree.sent()
    mixed.sent()


def backward_kernel(
    outer,
    tp,
    wa_all,
    gate_w,
    up_w,
    down_w,
    gain_rows,
    h1,
    qkv,
    probs,
    att,
    x1,
    h2,
    cot_all,
    gate,
    upper,
    hid,
    grad_down,
    x,
    cosine,
    sine,
    out,
    grad_tok,
    down_mine,
    down_theirs,
    gate_mine,
    gate_theirs,
    up_mine,
    up_theirs,
    out_total,
    qkv_total,
    dgate,
    dupper,
    e_part,
    y_part,
    e_got_c,
    y_got_c,
    e_near,
    y_near,
    e_got,
    y_got,
    dx1,
    dx1_low,
    dout,
    dscores,
    dqkv,
    f_part,
    f_got_c,
    f_got_y,
    f_far,
    grad_gate,
    grad_up,
    grad_out,
    grad_qkv,
    out_pair,
    qkv_pair,
    out_sum,
    qkv_sum,
    down_held,
    gate_held,
    up_held,
    out_held,
    qkv_held,
    down_staged,
    gate_staged,
    up_staged,
    out_staged,
    qkv_staged,
    down_give,
    gate_give,
    up_give,
    send_sems,
    recv_sems,
    local_sems,
):
    links = Links(tp, send_sems, recv_sems, local_sems)
    rows, model = x.shape
    tree_len = rows * tp
    units = gate_w.shape[1]
    q_width = att.shape[1]
    qkv_width = qkv.shape[1]
    kv_width = (qkv_width - q_width) // 2
    head = HEAD_SIZE
    group = q_width // kv_width
    shard = model // (2 * outer)
    xi = links.di % 2
    half = pl.multiple_of(xi * shard, shard)
    other = pl.multiple_of((1 - xi) * shard, shard)
    spec = rows_spec(rows // 2, model)
    gain_spec = whole_spec(8, model)
    greet_all(links, outer)

    def mlp_reduce(grad, held, staged):
        return ReduceZ(
            links, outer, lambda k: grad.at[pl.ds(k * 2 * shard, 2 * shard)], held, staged
        )

    def trade(reduce, mine, give, theirs):
        reduce.arrive()
        reduce.total(other, shard, give)
        copy = links.send(give, theirs, tp)
        reduce.total(half, shard, mine)
        return copy

    red_down = mlp_reduce(grad_down, down_held, down_staged)
    red_gate = mlp_reduce(grad_gate, gate_held, gate_staged)
    red_up = mlp_reduce(grad_up, up_held, up_staged)
    red_down.start_all()

    def contract(c_ref, w_ref, g_ref, u_ref, dg_ref, du_ref):
        dhid = dot_nn(c_ref[...], w_ref[...])
        g = g_ref[...].astype(F32)
        sigma = jax.nn.sigmoid(g)
        dg_ref[...] = (dhid * u_ref[...].astype(F32) * sigma * (1.0 + g * (1.0 - sigma))).astype(
            BF16
        )
        du_ref[...] = (dhid * g * sigma).astype(BF16)

    unit_spec = rows_spec(rows, units)
    pipe(
        contract,
        (2 * tp,),
        [rows_spec(rows, model), whole_spec(model, units), unit_spec, unit_spec],
        [unit_spec] * 2,
        cot_all,
        down_w,
        gate,
        upper,
        dgate,
        dupper,
    )

    def every_other(first, block_rows, width):
        return pl.BlockSpec((block_rows, width), lambda i: (2 * i + first, 0))

    def back(dg_ref, du_ref, g_ref, u_ref, o_ref):
        o_ref[...] = (dot_nt(dg_ref[...], g_ref[...]) + dot_nt(du_ref[...], u_ref[...])).astype(
            BF16
        )

    def back_blocks(first):
        pipe(
            back,
            (tp,),
            [every_other(first, rows, units)] * 2 + [whole_spec(model, units)] * 2,
            [every_other(first, rows, model)],
            dgate,
            dupper,
            gate_w,
            up_w,
            e_part,
        )

    def down_blocks(first):
        pipe(
            nt_body,
            (tp,),
            [every_other(first, rows, units), whole_spec(model, units)],
            [every_other(first, rows, model)],
            hid,
            down_w,
            y_part,
        )

    e_sum = ScatterUnits(links, e_part, e_got_c, e_near, e_got, rows)
    y_sum = ScatterUnits(links, y_part, y_got_c, y_near, y_got, rows)
    back_blocks(1)
    e_sum.start()
    red_down.pump()
    back_blocks(0)
    e_sum.across()
    weight_grad(h2, dgate, grad_gate, 4)
    red_gate.start_all()
    e_sum.finish()
    weight_grad(h2, dupper, grad_up, 4)
    red_up.start_all()
    down_blocks(1)
    y_sum.start()
    down_blocks(0)
    trades = [trade(red_down, down_mine, down_give, down_theirs)]

    tree = GatherTree(links, dx1_low, rows)

    def through_norm(c_ref, x_ref, g_ref, *refs):
        value = c_ref[...].astype(F32) + norm_back(sum_refs(refs[:-2]), g_ref[1:2], x_ref[...])
        refs[-2][...] = value
        refs[-1][...] = value.astype(BF16)

    parts = e_sum.arrive()
    pipe(
        through_norm,
        (2,),
        [spec, spec, gain_spec] + [spec] * len(parts),
        [spec] * 2,
        cot_all.at[pl.ds(0, rows)],
        x1,
        gain_rows,
        *parts,
        dx1,
        tree.block(0),
    )
    tree.start()
    y_sum.across()
    red_gate.pump()
    tree.across()
    tree.arrive()

    pipe(
        nn_body,
        (tp,),
        [rows_spec(rows, model), whole_spec(model, q_width)],
        [rows_spec(rows, q_width)],
        dx1_low,
        wa_all.at[:, pl.ds(qkv_width, q_width)],
        dout,
    )

    def pair_block(full, k, at):
        return full.at[pl.ds(pl.multiple_of(k * 2 * shard + at, shard), shard)]

    def pair_send(grad, held, k):
        return links.send(pair_block(grad, k, other), held.at[k], tp)

    red_out = ReduceZ(links, outer, lambda k: out_sum.at[k], out_held, out_staged)
    red_qkv = ReduceZ(links, outer, lambda k: qkv_sum.at[k], qkv_held, qkv_staged)
    weight_grad(dx1_low, att, grad_out, 4)
    order = list(range(outer - 1, -1, -1))
    out_across = {k: pair_send(grad_out, out_pair, k) for k in order}
    y_sum.finish()

    def score_grads(do_ref, k_ref, v_ref, p_ref, cos_ref, sin_ref, ds_ref, dq_ref):
        p = p_ref[0].astype(F32)
        dp = dot_nt(do_ref[...], v_ref[...])
        inner = jnp.sum(p * dp, axis=-1, keepdims=True)
        ds = (p * (dp - inner) * (head**-0.5)).astype(BF16)
        ds_ref[0] = ds
        dq_ref[...] = rotate(dot_nn(ds, k_ref[...]), cos_ref[...], sin_ref[...], -1.0).astype(BF16)

    k_at, v_at = q_width // head, (q_width + kv_width) // head
    pipe(
        score_grads,
        (tp, q_width // head),
        [
            pl.BlockSpec((rows, head), lambda i, h: (i, h)),
            pl.BlockSpec((tree_len, head), lambda i, h: (0, k_at + h // group)),
            pl.BlockSpec((tree_len, head), lambda i, h: (0, v_at + h // group)),
            pl.BlockSpec((1, rows, tree_len), lambda i, h: (h, i, 0)),
            pl.BlockSpec((rows, head // 2), lambda i, h: (i, 0)),
            pl.BlockSpec((rows, head // 2), lambda i, h: (i, 0)),
        ],
        [
            pl.BlockSpec((1, rows, tree_len), lambda i, h: (h, i, 0)),
            pl.BlockSpec((rows, head), lambda i, h: (i, h)),
        ],
        dout,
        qkv,
        qkv,
        probs,
        cosine,
        sine,
        dscores,
        dqkv,
    )

    def key_grads(ds_ref, p_ref, q_ref, do_ref, cos_ref, sin_ref, dkv_ref):
        dk = jnp.zeros((rows, head), F32)
        dv = jnp.zeros((rows, head), F32)
        for h in range(group):
            cols = slice(h * head, (h + 1) * head)
            dk = dk + dot_tn(ds_ref[h], q_ref[:, cols])
            dv = dv + dot_tn(p_ref[h], do_ref[:, cols])
        dkv_ref[:, :head] = rotate(dk, cos_ref[...], sin_ref[...], -1.0).astype(BF16)
        dkv_ref[:, head:] = dv.astype(BF16)

    by_key = pl.BlockSpec((group, tree_len, rows), lambda i: (0, 0, i))
    pipe(
        key_grads,
        (tp,),
        [by_key, by_key]
        + [whole_spec(tree_len, q_width)] * 2
        + [rows_spec(rows, head // 2)] * 2,
        [rows_spec(rows, 2 * kv_width)],
        dscores,
        probs,
        qkv.at[:, pl.ds(0, q_width)],
        dout,
        cosine,
        sine,
        dqkv.at[:, pl.ds(q_width, 2 * kv_width)],
    )

    def pair_add(grad, held, total, k):
        add_pipe(
            rows_spec(min(shard, 128), grad.shape[1]),
            shard,
            pair_block(grad, k, half),
            held.at[k],
            total.at[k],
        )

    qkv_across = {}
    for k in order:
        weight_grad(h1, dqkv, grad_qkv, outer, k, 1)
        qkv_across[k] = pair_send(grad_qkv, qkv_pair, k)
    pipe(
        nt_body,
        (tp,),
        [rows_spec(rows, qkv_width), whole_spec(model, qkv_width)],
        [rows_spec(rows, model)],
        dqkv,
        wa_all.at[:, pl.ds(0, qkv_width)],
        f_part,
    )
    f_sum = ScatterTensor(links, f_part, f_got_c, f_got_y, f_far, rows)
    f_sum.start()
    f_sum.across()
    red_up.pump()
    for k in order:
        out_across[k].wait_recv()
        pair_add(grad_out, out_pair, out_sum, k)
        if k:
            red_out.start(k)
    trades.append(trade(red_gate, gate_mine, gate_give, gate_theirs))

    def finish_output(x_ref, *refs):
        refs[-1][...] = (x_ref[...] + sum_refs(refs[:-1])).astype(BF16)

    parts = y_sum.arrive()
    pipe(finish_output, (2,), [spec] * (1 + len(parts)), [spec], x1, *parts, out)

    for k in order:
        qkv_across[k].wait_recv()
        pair_add(grad_qkv, qkv_pair, qkv_sum, k)
        if k:
            red_qkv.start(k)

    def finish_tokens(d_ref, x_ref, g_ref, *refs):
        refs[-1][...] = (
            d_ref[...] + norm_back(sum_refs(refs[:-1]), g_ref[0:1], x_ref[...])
        ).astype(BF16)

    parts = f_sum.arrive()
    pipe(
        finish_tokens,
        (2,),
        [spec, spec, gain_spec] + [spec] * len(parts),
        [spec],
        dx1,
        x,
        gain_rows,
        *parts,
        grad_tok,
    )
    trades.append(trade(red_up, up_mine, up_give, up_theirs))
    red_out.pump()
    red_qkv.pump()
    red_out.arrive()
    red_out.total(0, shard, out_total)
    red_qkv.arrive()
    red_qkv.total(0, shard, qkv_total)
    for copy in trades:
        copy.wait()
    for copy in list(out_across.values()) + list(qkv_across.values()):
        copy.wait_send()
    for item in (red_down, red_gate, red_up, red_out, red_qkv, e_sum, y_sum, f_sum, tree):
        item.sent()


def call(kernel, name, collective, count, shapes, operands):
    anywhere = pl.BlockSpec(memory_space=pl.ANY)
    return pl.pallas_call(
        kernel,
        out_shape=[jax.ShapeDtypeStruct(shape, dtype) for shape, dtype in shapes],
        in_specs=[anywhere] * len(operands),
        out_specs=[anywhere] * len(shapes),
        scratch_shapes=[
            pltpu.SemaphoreType.DMA((count,)),
            pltpu.SemaphoreType.DMA((count,)),
            pltpu.SemaphoreType.DMA((8,)),
        ],
        compiler_params=pltpu.CompilerParams(
            collective_id=collective, has_side_effects=True, vmem_limit_bytes=VMEM_LIMIT
        ),
        name=name,
    )(*operands)


def make_body(dp, tp):
    outer = dp // 2
    assert tp == 4 and dp == 2 * outer and outer >= 4 and outer & (outer - 1) == 0

    def swap(value, mask):
        return lax.ppermute(value, ("dp", "tensor"), [(i, i ^ mask) for i in range(dp * tp)])

    def relative(value, zi):
        width = value.shape[-1] // outer
        step = 1
        while step < outer:
            blocks = [value[..., i * width : (i + 1) * width] for i in range(outer)]
            swapped = jnp.concatenate([blocks[i ^ step] for i in range(outer)], -1)
            value = jnp.where((zi // step) % 2 == 1, swapped, value)
            step *= 2
        return value

    def body(
        tokens,
        parents,
        attn_gain,
        w_query,
        key_matrix,
        value_matrix,
        w_out,
        mlp_gain,
        w_gate,
        w_up,
        w_down,
        cotangent,
    ):
        di = lax.axis_index("dp")
        zi = di // 2
        upper_x = di % 2 == 1
        rows, model = tokens.shape
        tree_len = rows * tp
        q_width = w_query.shape[1]
        kv_width = key_matrix.shape[1]
        qkv_width = q_width + 2 * kv_width
        heads = q_width // HEAD_SIZE
        assert kv_width == HEAD_SIZE
        shard = w_query.shape[0]
        units = w_gate.shape[1] // 2

        wa = jnp.concatenate([w_query, key_matrix, value_matrix, w_out.T], 1)
        gn = jnp.concatenate(
            [
                jnp.broadcast_to(attn_gain[:, None], (shard, 64)),
                jnp.broadcast_to(mlp_gain[:, None], (shard, 64)),
            ],
            1,
        )
        allowed_mask, place = tree_tables(parents[0], tree_len, BLK)
        cosine, sine = rope_tables(place, HEAD_SIZE)
        bias = jnp.where(allowed_mask, 0.0, NEG).astype(BF16)
        x = relative(tokens, zi).astype(F32)
        xh = normalize(x)[0]
        cot = relative(cotangent, zi)
        (
            wa_all,
            gate_w,
            up_w,
            down_w,
            gain_rows,
            h1,
            qkv,
            probs,
            att,
            x1,
            h2,
            cot_all,
            gate,
            upper,
            hid,
            grad_down,
        ) = call(
            functools.partial(forward_kernel, outer, tp),
            "layer_forward",
            0,
            50 + 7 * outer,
            [
                ((model, qkv_width + q_width), BF16),
                ((model, units), BF16),
                ((model, units), BF16),
                ((model, units), BF16),
                ((8, model), F32),
                ((tree_len, model), BF16),
                ((tree_len, qkv_width), BF16),
                ((heads, tree_len, tree_len), BF16),
                ((tree_len, q_width), BF16),
                ((rows, model), F32),
                ((2 * tree_len, model), BF16),
                ((2 * tree_len, model), BF16),
                ((2 * tree_len, units), BF16),
                ((2 * tree_len, units), BF16),
                ((2 * tree_len, units), BF16),
                ((model, units), BF16),
                ((model, 128), BF16),
                ((tree_len, model), BF16),
                ((2, rows, model), BF16),
                ((rows, model), BF16),
                ((rows, model), BF16),
            ],
            (wa, w_gate, w_up, w_down.T, gn, x, xh, cot, cosine, sine, bias),
        )[:16]

        mlp_held = [((outer, 2 * shard, units), BF16)]
        (
            out,
            grad_tok,
            down_mine,
            down_theirs,
            gate_mine,
            gate_theirs,
            up_mine,
            up_theirs,
            out_total,
            qkv_total,
        ) = call(
            functools.partial(backward_kernel, outer, tp),
            "layer_backward",
            1,
            60 + 10 * outer,
            [((rows, model), BF16)] * 2
            + [((shard, units), F32), ((shard, units), BF16)] * 3
            + [((shard, q_width), F32), ((shard, qkv_width), F32)]
            + [((2 * tree_len, units), BF16)] * 2
            + [((2 * tree_len, model), BF16)] * 2
            + [((4, rows, model), BF16)] * 2
            + [((3, rows, model), BF16)] * 4
            + [((rows, model), F32), ((tree_len, model), BF16)]
            + [((tree_len, q_width), BF16), ((heads, tree_len, tree_len), BF16)]
            + [((tree_len, qkv_width), BF16), ((tree_len, model), BF16)]
            + [((2, rows, model), BF16)]
            + [((rows, model), BF16)] * 2
            + [((model, units), BF16)] * 2
            + [((model, q_width), BF16), ((model, qkv_width), BF16)]
            + [((outer, shard, q_width), BF16), ((outer, shard, qkv_width), BF16)] * 2
            + mlp_held * 3
            + [((outer, shard, q_width), BF16), ((outer, shard, qkv_width), BF16)]
            + [((2 * shard, units), BF16)] * 3
            + [((shard, q_width), BF16), ((shard, qkv_width), BF16)]
            + [((shard, units), BF16)] * 3,
            (
                wa_all,
                gate_w,
                up_w,
                down_w,
                gain_rows,
                h1,
                qkv,
                probs,
                att,
                x1,
                h2,
                cot_all,
                gate,
                upper,
                hid,
                grad_down,
                x,
                cosine,
                sine,
            ),
        )[:10]

        def order_x(mine, theirs):
            theirs = theirs.astype(F32)
            low = jnp.where(upper_x, theirs, mine)
            high = jnp.where(upper_x, mine, theirs)
            return jnp.concatenate([low, high], 1)

        grad_gate = order_x(gate_mine, gate_theirs)
        grad_up = order_x(up_mine, up_theirs)
        grad_query = qkv_total[:, :q_width]
        grad_key = qkv_total[:, q_width : q_width + kv_width]
        grad_value = qkv_total[:, q_width + kv_width :]

        gain_sums = jnp.stack(
            [
                jnp.sum(w_query.astype(F32) * grad_query, 1)
                + jnp.sum(key_matrix.astype(F32) * grad_key, 1)
                + jnp.sum(value_matrix.astype(F32) * grad_value, 1),
                jnp.sum(w_gate.astype(F32) * grad_gate, 1)
                + jnp.sum(w_up.astype(F32) * grad_up, 1),
            ]
        )
        gain_sums = gain_sums + swap(gain_sums, 1)
        gain_sums = gain_sums + swap(gain_sums, 2)
        return (
            relative(out, zi),
            relative(grad_tok, zi),
            gain_sums[0] / attn_gain.astype(F32),
            grad_query,
            grad_key,
            grad_value,
            out_total.T,
            gain_sums[1] / mlp_gain.astype(F32),
            grad_gate,
            grad_up,
            order_x(down_mine, down_theirs).T,
        )

    return body


def solution(mesh):
    in_specs = (
        P(("dp", "tensor"), None),
        P("dp", None),
        P("dp"),
        P("dp", "tensor"),
        P("dp", "tensor"),
        P("dp", "tensor"),
        P("tensor", "dp"),
        P("dp"),
        P("dp", "tensor"),
        P("dp", "tensor"),
        P("tensor", "dp"),
        P(("dp", "tensor"), None),
    )
    out_specs = (
        P(("dp", "tensor"), None),
        P(("dp", "tensor"), None),
        P("dp"),
        P("dp", "tensor"),
        P("dp", "tensor"),
        P("dp", "tensor"),
        P("tensor", "dp"),
        P("dp"),
        P("dp", "tensor"),
        P("dp", "tensor"),
        P("tensor", "dp"),
    )
    body = make_body(mesh.shape["dp"], mesh.shape["tensor"])
    return jax.shard_map(body, mesh=mesh, in_specs=in_specs, out_specs=out_specs, check_vma=False)
```

```python
import functools

import jax
import jax.numpy as jnp
from jax import lax
from jax.experimental import pallas as pl
from jax.experimental.pallas import tpu as pltpu
from jax.sharding import PartitionSpec as P

HEAD_SIZE = 256
BLK = 128


EPS = 1e-06
THETA = 1000042.0
NEG = -1e30
HIGH = lax.Precision.HIGHEST
F32 = jnp.float32
BF16 = jnp.bfloat16
MESH = pl.DeviceIdType.MESH
VMEM_LIMIT = 56 * 2**20


def tree_tables(parent_row, tree_len, block_len):
    blocks = parent_row.shape[0]
    nodes = jnp.arange(blocks, dtype=jnp.int32)
    hops = (parent_row[:, None] == nodes[None, :]).astype(F32)
    reach = jnp.eye(blocks, dtype=F32)
    walk = reach
    for hop_count in range(blocks):
        walk = jnp.dot(walk, hops, precision=HIGH)
        reach = jnp.maximum(reach, walk)
    depth = jnp.sum(reach, axis=1) - 1.0
    rows = jnp.arange(tree_len, dtype=jnp.int32)
    member = (rows[:, None] // block_len == nodes[None, :]).astype(F32)
    visible = jnp.dot(jnp.dot(member, reach, precision=HIGH), member.T, precision=HIGH) > 0.5
    allowed_mask = visible & (rows[None, :] <= rows[:, None])
    place = jnp.dot(member, depth, precision=HIGH) * block_len + (rows % block_len).astype(F32)
    return (allowed_mask, place)


def rope_tables(place, head_dim):
    half = head_dim // 2
    freq = THETA ** (-2.0 * jnp.arange(half, dtype=F32) / head_dim)
    angle = place[:, None] * freq[None, :]
    return (jnp.cos(angle), jnp.sin(angle))


def rotate(values, cosine, sine, sign):
    half = values.shape[-1] // 2
    first, second = values[..., :half], values[..., half:]
    return jnp.concatenate(
        [first * cosine - sign * second * sine, second * cosine + sign * first * sine], -1
    )


def normalize(values):
    inverse = lax.rsqrt(jnp.mean(values * values, axis=-1, keepdims=True) + EPS)
    return (values * inverse, inverse)


def norm_back(grad_normed, gain, values):
    scaled, inverse = normalize(values)
    grad_scaled = grad_normed * gain
    inner = jnp.mean(grad_scaled * scaled, axis=-1, keepdims=True)
    return inverse * (grad_scaled - scaled * inner)


def dot_nn(left, right):
    return jnp.dot(left, right, preferred_element_type=F32)


def dot_nt(left, right):
    return lax.dot_general(left, right, (((1,), (1,)), ((), ())), preferred_element_type=F32)


def dot_tn(left, right):
    return lax.dot_general(left, right, (((0,), (0,)), ((), ())), preferred_element_type=F32)


def flip(index, mask):
    out = index
    bit = 1
    while bit <= mask:
        if mask & bit:
            out = out + bit * (1 - 2 * (index // bit % 2))
        bit *= 2
    return out


class Links:
    def __init__(self, tp, send_sems, recv_sems):
        self.tp = tp
        self.di = lax.axis_index("dp")
        self.ti = lax.axis_index("tensor")
        self.send_sems, self.recv_sems = send_sems, recv_sems
        self.used = 0

    def partner(self, mask):
        return (flip(self.di, mask // self.tp), flip(self.ti, mask % self.tp))

    def greet(self, masks):
        barrier = pltpu.get_barrier_semaphore()
        for mask in masks:
            pl.semaphore_signal(barrier, inc=1, device_id=self.partner(mask), device_id_type=MESH)
        pl.semaphore_wait(barrier, len(masks))

    def remote(self, src, dst, mask):
        index = self.used
        self.used += 1
        return pltpu.make_async_remote_copy(
            src_ref=src,
            dst_ref=dst,
            send_sem=self.send_sems.at[index],
            recv_sem=self.recv_sems.at[index],
            device_id=self.partner(mask),
            device_id_type=MESH,
        )

    def send(self, src, dst, mask):
        copy = self.remote(src, dst, mask)
        copy.start()
        return copy


def line_middle(links):
    zi = links.di // 2
    return (zi == 1) | (zi == 2)


class Spread:
    def __init__(self, links, outer, own, block):
        self.links, self.outer = links, outer
        step = 2 * links.tp
        self.middle = line_middle(links)
        self.copies = {k: links.remote(own, block(k), k * step) for k in range(1, outer)}
        if outer == 4:
            self.onward = links.remote(block(2), block(3), step)

    def start(self):
        if self.outer != 4:
            for copy in self.copies.values():
                copy.start()
            return
        self.copies[2].start()
        self.copies[1].start()

        @pl.when(self.middle)
        def _():
            self.copies[3].start()

    def forward(self):
        self.copies[2].wait_recv()
        if self.outer != 4:
            return

        @pl.when(self.middle)
        def _():
            self.onward.start()

    def arrive(self, k):
        if k == 1 or (self.outer != 4 and k != 2):
            self.copies[k].wait_recv()
        elif k == 3:

            @pl.when(self.middle)
            def _():
                self.copies[3].wait_recv()

            @pl.when(jnp.logical_not(self.middle))
            def _():
                self.onward.wait_recv()

    def sent(self):
        if self.outer != 4:
            for copy in self.copies.values():
                copy.wait_send()
            return
        self.copies[1].wait_send()
        self.copies[2].wait_send()

        @pl.when(self.middle)
        def _():
            self.copies[3].wait_send()
            self.onward.wait_send()


class ReduceZ:
    def __init__(self, links, outer, block, held, staged):
        self.links, self.outer, self.block, self.held, self.staged = (
            links,
            outer,
            block,
            held,
            staged,
        )
        step = 2 * links.tp
        self.middle = line_middle(links)
        self.copies = {k: links.remote(block(k), held.at[k], k * step) for k in range(1, outer)}
        if outer == 4:
            self.inward = links.remote(block(3), held.at[0], step)
            self.summed = links.remote(staged, held.at[2], 2 * step)

    def on_ends(self, *actions):
        @pl.when(jnp.logical_not(self.middle))
        def _():
            for action in actions:
                action()

    def on_middle(self, *actions):
        @pl.when(self.middle)
        def _():
            for action in actions:
                action()

    def start(self, k):
        if self.outer != 4 or k == 1:
            self.copies[k].start()
        elif k == 3:
            self.on_ends(self.inward.start)
            self.on_middle(self.copies[3].start)
        elif k == 2:
            self.on_ends(self.copies[2].start)

    def start_all(self):
        for k in range(self.outer - 1, 0, -1):
            self.start(k)

    def pump(self):
        if self.outer != 4:
            return

        def add():
            rows, width = self.staged.shape
            spec = rows_spec(min(rows, 128), width)
            add_pipe(spec, rows, self.block(2), self.held.at[0], self.staged)

        self.on_middle(self.inward.wait_recv, add, self.summed.start)

    def arrive(self):
        if self.outer != 4:
            for copy in self.copies.values():
                copy.wait_recv()
            return
        self.copies[1].wait_recv()
        self.on_middle(self.copies[2].wait_recv, self.copies[3].wait_recv)
        self.on_ends(self.summed.wait_recv)

    def total(self, lo, rows, out):
        width = self.staged.shape[1]
        spec = rows_spec(min(rows, 128), width)

        def add(*refs):
            value = refs[0][...].astype(F32)
            for ref in refs[1:-1]:
                value = value + ref[...].astype(F32)
            refs[-1][...] = value.astype(refs[-1].dtype)

        def over(kept):
            parts = [self.block(0)] + [self.held.at[k] for k in kept]
            parts = [part.at[pl.ds(lo, rows)] for part in parts]
            grid = (rows // min(rows, 128),)
            pipe(add, grid, [spec] * len(parts), [spec], *parts, out)

        if self.outer != 4:
            over(range(1, self.outer))
            return
        self.on_middle(lambda: over([1, 2, 3]))
        self.on_ends(lambda: over([1, 2]))

    def sent(self):
        if self.outer != 4:
            for copy in self.copies.values():
                copy.wait_send()
            return
        self.copies[1].wait_send()
        self.on_middle(self.copies[3].wait_send, self.summed.wait_send)
        self.on_ends(self.copies[2].wait_send, self.inward.wait_send)


def gather_units(links, full, rows):
    tp = links.tp

    def block(m, lo=0, n=None):
        return full.at[pl.ds(m * rows + lo, rows if n is None else n)]

    half = rows // 2
    sent = []

    def send(m, mask, lo=0, n=None):
        copy = links.send(block(m, lo, n), block(m ^ mask, lo, n), mask)
        sent.append(copy)
        return copy

    x = send(0, tp)
    y = send(0, 2)
    c0 = send(0, 1)
    yield
    y.wait_recv()
    low = send(2, tp, half, half)
    c2 = send(2, 1)
    x.wait_recv()
    high = send(tp, 2, 0, half)
    c4 = send(tp, 1)
    yield
    low.wait_recv()
    high.wait_recv()
    c6 = send(tp + 2, 1)
    yield
    for copy in (c0, c2, c4, c6):
        copy.wait_recv()
    for copy in sent:
        copy.wait_send()
    yield


def run(stages):
    for _ in stages:
        pass


def pipe(body, grid, in_specs, out_specs, *refs):
    pltpu.emit_pipeline(body, grid=grid, in_specs=in_specs, out_specs=out_specs)(*refs)


def rows_spec(rows, width):
    return pl.BlockSpec((rows, width), lambda i: (i, 0))


def whole_spec(rows, width):
    return pl.BlockSpec((rows, width), lambda i: (0, 0))


def add_refs(a_ref, b_ref, o_ref):
    o_ref[...] = (a_ref[...].astype(F32) + b_ref[...].astype(F32)).astype(o_ref.dtype)


def add_pipe(spec, rows, a, b, out):
    pipe(add_refs, (rows // spec.block_shape[0],), [spec, spec], [spec], a, b, out)


def copy_body(a_ref, o_ref):
    o_ref[...] = a_ref[...]


def keep(src, dst):
    rows, width = src.shape
    spec = rows_spec(min(rows, 128), width)
    pipe(copy_body, (rows // min(rows, 128),), [spec], [spec], src, dst)


def nt_body(a_ref, b_ref, o_ref):
    o_ref[...] = dot_nt(a_ref[...], b_ref[...]).astype(BF16)


def nn_body(a_ref, b_ref, o_ref):
    o_ref[...] = dot_nn(a_ref[...], b_ref[...]).astype(BF16)


def tn_body(a_ref, b_ref, o_ref):
    o_ref[...] = dot_tn(a_ref[...], b_ref[...]).astype(BF16)


def weight_grad(acts, grads, out, blocks, first=0, count=None):
    tokens, model = acts.shape
    width = grads.shape[1]
    size = model // blocks
    count = blocks if count is None else count
    pipe(
        tn_body,
        (count,),
        [pl.BlockSpec((tokens, size), lambda i: (0, first + i)), whole_spec(tokens, width)],
        [pl.BlockSpec((size, width), lambda i: (first + i, 0))],
        acts,
        grads,
        out,
    )


class ScatterTensor:
    def __init__(self, links, part, got_c, got_y, far, rows):
        self.links, self.part, self.got_c, self.got_y, self.far = links, part, got_c, got_y, far
        self.rows = rows
        self.model = part.shape[1]
        self.spec = rows_spec(rows // 2, self.model)

    def block(self, mask):
        rows = self.rows
        return self.part.at[
            pl.ds(pl.multiple_of(flip(self.links.ti, mask) * rows, rows), rows)
        ]

    def start(self):
        self.copies = [
            self.links.send(self.block(3), self.got_c.at[1], 1),
            self.links.send(self.block(1), self.got_c.at[0], 1),
        ]

    def across(self):
        self.copies[0].wait_recv()
        add_pipe(self.spec, self.rows, self.block(2), self.got_c.at[1], self.far)
        self.copies.append(self.links.send(self.far, self.got_y, 2))

    def arrive(self):
        self.copies[1].wait_recv()
        self.copies[2].wait_recv()
        return [self.block(0), self.got_c.at[0], self.got_y]

    def sent(self):
        for copy in self.copies:
            copy.wait_send()


class ScatterUnits:
    def __init__(self, links, part, got_c, near, got, rows):
        self.links, self.part, self.got_c, self.near, self.got = links, part, got_c, near, got
        self.rows, self.model = rows, part.shape[1]
        self.sends = []

    def send(self, src, dst, mask):
        copy = self.links.send(src, dst, mask)
        self.sends.append(copy)
        return copy

    def block(self, m):
        return self.part.at[pl.ds(m * self.rows, self.rows)]

    def start(self):
        self.from_c = [self.send(self.block(2 * i + 1), self.got_c.at[i], 1) for i in range(4)]

    def add(self, m, slot, lo, n):
        rows = pl.ds(lo, n)
        add_pipe(
            rows_spec(n, self.model),
            n,
            self.block(m).at[rows],
            self.got_c.at[m // 2].at[rows],
            self.near.at[slot].at[rows],
        )

    def across(self):
        tp, rows, half = self.links.tp, self.rows, self.rows // 2
        low, high = pl.ds(0, half), pl.ds(half, half)
        near, got = self.near, self.got
        for copy in self.from_c:
            copy.wait_recv()
        self.add(6, 2, 0, half)
        self.top = self.send(near.at[2].at[low], got.at[2].at[low], tp)
        self.add(6, 2, half, half)
        self.bottom = self.send(near.at[2].at[high], got.at[2].at[high], 2)
        self.add(4, 0, 0, half)
        self.x_low = self.send(near.at[0].at[low], got.at[0].at[low], tp)
        self.add(2, 1, half, half)
        self.y_high = self.send(near.at[1].at[high], got.at[1].at[high], 2)

    def finish(self):
        tp, half = self.links.tp, self.rows // 2
        low, high = pl.ds(0, half), pl.ds(half, half)
        near, got = self.near, self.got

        def add3(m, slot, rows):
            def body(a_ref, b_ref, c_ref, o_ref):
                o_ref[...] = (
                    a_ref[...].astype(F32) + b_ref[...].astype(F32) + c_ref[...].astype(F32)
                ).astype(BF16)

            spec = rows_spec(half, self.model)
            pipe(
                body,
                (1,),
                [spec] * 3,
                [spec],
                self.block(m).at[rows],
                self.got_c.at[m // 2].at[rows],
                got.at[2].at[rows],
                near.at[slot].at[rows],
            )

        self.top.wait_recv()
        add3(2, 1, low)
        self.y_low = self.send(near.at[1].at[low], got.at[1].at[low], 2)
        self.bottom.wait_recv()
        add3(4, 0, high)
        self.x_high = self.send(near.at[0].at[high], got.at[0].at[high], tp)

    def arrive(self):
        for copy in (self.x_low, self.x_high, self.y_low, self.y_high):
            copy.wait_recv()
        return [self.block(0), self.got_c.at[0], self.got.at[0], self.got.at[1]]

    def sent(self):
        for copy in self.sends:
            copy.wait_send()


def sum_refs(refs):
    value = refs[0][...].astype(F32)
    for ref in refs[1:]:
        value = value + ref[...].astype(F32)
    return value


class GatherTree:
    def __init__(self, links, full, rows):
        self.links, self.full, self.rows = links, full, rows

    def block(self, mask):
        rows = self.rows
        return self.full.at[
            pl.ds(pl.multiple_of(flip(self.links.ti, mask) * rows, rows), rows)
        ]

    def start(self):
        self.y = self.links.send(self.block(0), self.block(0), 2)
        self.c = self.links.send(self.block(0), self.block(0), 1)

    def across(self):
        self.y.wait_recv()
        self.yc = self.links.send(self.block(2), self.block(2), 1)

    def arrive(self):
        self.c.wait_recv()
        self.yc.wait_recv()

    def sent(self):
        for copy in (self.y, self.c, self.yc):
            copy.wait_send()


def greet_all(links, outer):
    step = 2 * links.tp
    links.greet([1, 2, links.tp] + [k * step for k in range(1, outer)])


def forward_kernel(
    outer,
    tp,
    wa,
    wg,
    wu,
    wd,
    gn,
    x,
    xh,
    cot,
    cosine,
    sine,
    bias,
    wa_all,
    gate_w,
    up_w,
    down_w,
    gain_rows,
    h1,
    qkv,
    probs,
    att,
    x1,
    h2,
    cot_all,
    gate,
    upper,
    hid,
    grad_down,
    gn_all,
    part,
    got_c,
    got_y,
    far,
    send_sems,
    recv_sems,
):
    links = Links(tp, send_sems, recv_sems)
    shard, attn_width = wa.shape
    units = gate_w.shape[1]
    rows, model = xh.shape
    tree_len = rows * tp
    q_width = att.shape[1]
    qkv_width = qkv.shape[1]
    kv_width = (qkv_width - q_width) // 2
    head = HEAD_SIZE
    xi = links.di % 2
    greet_all(links, outer)

    def shard_block(full, k):
        return full.at[pl.ds(pl.multiple_of((2 * k + xi) * shard, shard), shard)]

    mine = pl.ds(pl.multiple_of(xi * units, units), units)
    peers = pl.ds(pl.multiple_of((1 - xi) * units, units), units)
    place = pl.ds(pl.multiple_of(xi * shard, shard), shard)

    def send_pair(w, full):
        return links.send(w.at[:, peers], full.at[place], tp)

    def mlp_spread(full):
        return Spread(
            links,
            outer,
            full.at[pl.ds(0, 2 * shard)],
            lambda k: full.at[pl.ds(k * 2 * shard, 2 * shard)],
        )

    gains = Spread(links, outer, gn, lambda k: shard_block(gn_all, k))
    attn = Spread(links, outer, wa, lambda k: shard_block(wa_all, k))
    gains.start()
    across_gn = [links.send(gn, shard_block(gn_all, 0), tp)]
    attn.start()
    across = [links.send(wa, shard_block(wa_all, 0), tp)]
    pair = [send_pair(wg, gate_w)]
    keep(gn, shard_block(gn_all, 0))
    keep(wg.at[:, mine], gate_w.at[place])

    gains.forward()
    for k in range(1, outer):
        gains.arrive(k)
        across_gn.append(links.send(shard_block(gn_all, k), shard_block(gn_all, k), tp))
    keep(wa, shard_block(wa_all, 0))
    for copy in across_gn:
        copy.wait_recv()

    def gain_rows_of(g_ref, o_ref):
        lane = lax.broadcasted_iota(jnp.int32, (8, 128), 1)
        row = lax.broadcasted_iota(jnp.int32, (8, 128), 0)
        pick = jnp.where((row < 2) & (lane == row * 64), 1.0, 0.0).astype(BF16)
        o_ref[...] = dot_nt(pick, g_ref[...])

    pipe(gain_rows_of, (1,), [whole_spec(model, 128)], [whole_spec(8, model)], gn_all, gain_rows)
    spec = rows_spec(rows // 2, model)
    gain_spec = whole_spec(8, model)

    def scale_tokens(x_ref, g_ref, o_ref):
        o_ref[...] = (x_ref[...] * g_ref[0:1]).astype(BF16)

    tree = GatherTree(links, h1, rows)
    pipe(scale_tokens, (2,), [spec, gain_spec], [spec], xh, gain_rows, tree.block(0))
    tree.start()
    keep(wu.at[:, mine], up_w.at[place])
    keep(wd.at[:, mine], down_w.at[place])
    keep(cot, cot_all.at[pl.ds(0, rows)])

    spreads = [mlp_spread(full) for full in (gate_w, up_w, down_w)]
    attn.forward()
    across.append(links.send(shard_block(wa_all, 2), shard_block(wa_all, 2), tp))
    pair[0].wait_recv()
    spreads[0].start()
    tree.across()
    for k in range(1, outer):
        if k != 2:
            attn.arrive(k)
            across.append(links.send(shard_block(wa_all, k), shard_block(wa_all, k), tp))
        if k == 1:
            pair.append(send_pair(wu, up_w))
    pair.append(send_pair(wd, down_w))
    tree.arrive()
    pair[1].wait_recv()
    spreads[1].start()
    for copy in across:
        copy.wait_recv()

    def project(x_ref, w_ref, cos_ref, sin_ref, out_ref):
        raw = dot_nn(x_ref[...], w_ref[...])
        for slot in range((q_width + kv_width) // head):
            cols = slice(slot * head, (slot + 1) * head)
            out_ref[:, cols] = rotate(raw[:, cols], cos_ref[...], sin_ref[...], 1.0).astype(BF16)
        out_ref[:, q_width + kv_width :] = raw[:, q_width + kv_width :].astype(BF16)

    pipe(
        project,
        (tp,),
        [
            rows_spec(rows, model),
            whole_spec(model, qkv_width),
            rows_spec(rows, head // 2),
            rows_spec(rows, head // 2),
        ],
        [rows_spec(rows, qkv_width)],
        h1,
        wa_all.at[:, pl.ds(0, qkv_width)],
        cosine,
        sine,
        qkv,
    )
    spreads[0].forward()
    pair[2].wait_recv()
    spreads[2].start()

    group = q_width // kv_width

    def attend(q_ref, k_ref, v_ref, b_ref, p_ref, o_ref):
        scores = dot_nt(q_ref[...], k_ref[...]) * (head**-0.5) + b_ref[...].astype(F32)
        weights = jnp.exp(scores - jnp.max(scores, axis=-1, keepdims=True))
        weights = (weights / jnp.sum(weights, axis=-1, keepdims=True)).astype(BF16)
        p_ref[0] = weights
        o_ref[...] = dot_nn(weights, v_ref[...]).astype(BF16)

    k_at, v_at = q_width // head, (q_width + kv_width) // head
    pipe(
        attend,
        (tp, q_width // head),
        [
            pl.BlockSpec((rows, head), lambda i, h: (i, h)),
            pl.BlockSpec((tree_len, head), lambda i, h: (0, k_at + h // group)),
            pl.BlockSpec((tree_len, head), lambda i, h: (0, v_at + h // group)),
            pl.BlockSpec((rows, tree_len), lambda i, h: (i, 0)),
        ],
        [
            pl.BlockSpec((1, rows, tree_len), lambda i, h: (h, i, 0)),
            pl.BlockSpec((rows, head), lambda i, h: (i, h)),
        ],
        qkv,
        qkv,
        qkv,
        bias,
        probs,
        att,
    )
    pipe(
        nt_body,
        (tp,),
        [rows_spec(rows, q_width), whole_spec(model, q_width)],
        [rows_spec(rows, model)],
        att,
        wa_all.at[:, pl.ds(qkv_width, q_width)],
        part,
    )
    mixed = ScatterTensor(links, part, got_c, got_y, far, rows)
    mixed.start()
    mixed.across()
    parts = mixed.arrive()

    def residual(x_ref, a_ref, b_ref, c_ref, g_ref, x1_ref, h_ref):
        total = x_ref[...] + sum_refs((a_ref, b_ref, c_ref))
        x1_ref[...] = total
        h_ref[...] = (normalize(total)[0] * g_ref[1:2]).astype(BF16)

    pipe(
        residual,
        (2,),
        [spec] * 4 + [gain_spec],
        [spec] * 2,
        x,
        *parts,
        gain_rows,
        x1,
        h2.at[pl.ds(0, rows)],
    )
    stages = gather_units(links, h2, rows)
    next(stages)
    later = gather_units(links, cot_all, rows)
    next(later)
    next(stages)
    spreads[1].forward()
    next(stages)
    next(later)
    next(stages)

    for spread in spreads[:2]:
        for k in range(1, outer):
            spread.arrive(k)

    def expand(x_ref, g_ref, u_ref, go_ref, uo_ref, h_ref):
        g = dot_nn(x_ref[...], g_ref[...])
        u = dot_nn(x_ref[...], u_ref[...])
        go_ref[...] = g.astype(BF16)
        uo_ref[...] = u.astype(BF16)
        h_ref[...] = (g * jax.nn.sigmoid(g) * u).astype(BF16)

    pipe(
        expand,
        (2 * tp,),
        [rows_spec(rows, model), whole_spec(model, units), whole_spec(model, units)],
        [rows_spec(rows, units)] * 3,
        h2,
        gate_w,
        up_w,
        gate,
        upper,
        hid,
    )
    run(later)
    spreads[2].forward()
    weight_grad(cot_all, hid, grad_down, 4)
    for k in range(1, outer):
        spreads[2].arrive(k)
    for spread in [gains, attn] + spreads:
        spread.sent()
    for copy in across_gn + across + pair:
        copy.wait_send()
    tree.sent()
    mixed.sent()


def backward_kernel(
    outer,
    tp,
    wa_all,
    gate_w,
    up_w,
    down_w,
    gain_rows,
    h1,
    qkv,
    probs,
    att,
    x1,
    h2,
    cot_all,
    gate,
    upper,
    hid,
    grad_down,
    x,
    cosine,
    sine,
    out,
    grad_tok,
    down_mine,
    down_theirs,
    gate_mine,
    gate_theirs,
    up_mine,
    up_theirs,
    out_total,
    qkv_total,
    dgate,
    dupper,
    e_part,
    y_part,
    e_got_c,
    y_got_c,
    e_near,
    y_near,
    e_got,
    y_got,
    dx1,
    dx1_low,
    dout,
    dscores,
    dqkv,
    f_part,
    f_got_c,
    f_got_y,
    f_far,
    grad_gate,
    grad_up,
    grad_out,
    grad_qkv,
    out_pair,
    qkv_pair,
    out_sum,
    qkv_sum,
    down_held,
    gate_held,
    up_held,
    out_held,
    qkv_held,
    down_staged,
    gate_staged,
    up_staged,
    out_staged,
    qkv_staged,
    down_give,
    gate_give,
    up_give,
    send_sems,
    recv_sems,
):
    links = Links(tp, send_sems, recv_sems)
    rows, model = x.shape
    tree_len = rows * tp
    units = gate_w.shape[1]
    q_width = att.shape[1]
    qkv_width = qkv.shape[1]
    kv_width = (qkv_width - q_width) // 2
    head = HEAD_SIZE
    group = q_width // kv_width
    shard = model // (2 * outer)
    xi = links.di % 2
    half = pl.multiple_of(xi * shard, shard)
    other = pl.multiple_of((1 - xi) * shard, shard)
    spec = rows_spec(rows // 2, model)
    gain_spec = whole_spec(8, model)
    greet_all(links, outer)

    def mlp_reduce(grad, held, staged):
        return ReduceZ(
            links, outer, lambda k: grad.at[pl.ds(k * 2 * shard, 2 * shard)], held, staged
        )

    def trade(reduce, mine, give, theirs):
        reduce.arrive()
        reduce.total(other, shard, give)
        copy = links.send(give, theirs, tp)
        reduce.total(half, shard, mine)
        return copy

    red_down = mlp_reduce(grad_down, down_held, down_staged)
    red_gate = mlp_reduce(grad_gate, gate_held, gate_staged)
    red_up = mlp_reduce(grad_up, up_held, up_staged)
    red_down.start_all()

    def contract(c_ref, w_ref, g_ref, u_ref, dg_ref, du_ref):
        dhid = dot_nn(c_ref[...], w_ref[...])
        g = g_ref[...].astype(F32)
        sigma = jax.nn.sigmoid(g)
        dg_ref[...] = (dhid * u_ref[...].astype(F32) * sigma * (1.0 + g * (1.0 - sigma))).astype(
            BF16
        )
        du_ref[...] = (dhid * g * sigma).astype(BF16)

    unit_spec = rows_spec(rows, units)
    pipe(
        contract,
        (2 * tp,),
        [rows_spec(rows, model), whole_spec(model, units), unit_spec, unit_spec],
        [unit_spec] * 2,
        cot_all,
        down_w,
        gate,
        upper,
        dgate,
        dupper,
    )

    def every_other(first, block_rows, width):
        return pl.BlockSpec((block_rows, width), lambda i: (2 * i + first, 0))

    def back(dg_ref, du_ref, g_ref, u_ref, o_ref):
        o_ref[...] = (dot_nt(dg_ref[...], g_ref[...]) + dot_nt(du_ref[...], u_ref[...])).astype(
            BF16
        )

    def back_blocks(first):
        pipe(
            back,
            (tp,),
            [every_other(first, rows, units)] * 2 + [whole_spec(model, units)] * 2,
            [every_other(first, rows, model)],
            dgate,
            dupper,
            gate_w,
            up_w,
            e_part,
        )

    def down_blocks(first):
        pipe(
            nt_body,
            (tp,),
            [every_other(first, rows, units), whole_spec(model, units)],
            [every_other(first, rows, model)],
            hid,
            down_w,
            y_part,
        )

    e_sum = ScatterUnits(links, e_part, e_got_c, e_near, e_got, rows)
    y_sum = ScatterUnits(links, y_part, y_got_c, y_near, y_got, rows)
    back_blocks(1)
    e_sum.start()
    red_down.pump()
    back_blocks(0)
    e_sum.across()
    weight_grad(h2, dgate, grad_gate, 4)
    red_gate.start_all()
    e_sum.finish()
    weight_grad(h2, dupper, grad_up, 4)
    red_up.start_all()
    down_blocks(1)
    y_sum.start()
    down_blocks(0)
    trades = [trade(red_down, down_mine, down_give, down_theirs)]

    tree = GatherTree(links, dx1_low, rows)

    def through_norm(c_ref, x_ref, g_ref, *refs):
        value = c_ref[...].astype(F32) + norm_back(sum_refs(refs[:-2]), g_ref[1:2], x_ref[...])
        refs[-2][...] = value
        refs[-1][...] = value.astype(BF16)

    parts = e_sum.arrive()
    pipe(
        through_norm,
        (2,),
        [spec, spec, gain_spec] + [spec] * len(parts),
        [spec] * 2,
        cot_all.at[pl.ds(0, rows)],
        x1,
        gain_rows,
        *parts,
        dx1,
        tree.block(0),
    )
    tree.start()
    y_sum.across()
    red_gate.pump()
    tree.across()
    tree.arrive()

    pipe(
        nn_body,
        (tp,),
        [rows_spec(rows, model), whole_spec(model, q_width)],
        [rows_spec(rows, q_width)],
        dx1_low,
        wa_all.at[:, pl.ds(qkv_width, q_width)],
        dout,
    )

    def pair_block(full, k, at):
        return full.at[pl.ds(pl.multiple_of(k * 2 * shard + at, shard), shard)]

    def pair_send(grad, held, k):
        return links.send(pair_block(grad, k, other), held.at[k], tp)

    red_out = ReduceZ(links, outer, lambda k: out_sum.at[k], out_held, out_staged)
    red_qkv = ReduceZ(links, outer, lambda k: qkv_sum.at[k], qkv_held, qkv_staged)
    weight_grad(dx1_low, att, grad_out, 4)
    order = list(range(outer - 1, -1, -1))
    out_across = {k: pair_send(grad_out, out_pair, k) for k in order}
    y_sum.finish()

    def score_grads(do_ref, k_ref, v_ref, p_ref, cos_ref, sin_ref, ds_ref, dq_ref):
        p = p_ref[0].astype(F32)
        dp = dot_nt(do_ref[...], v_ref[...])
        inner = jnp.sum(p * dp, axis=-1, keepdims=True)
        ds = (p * (dp - inner) * (head**-0.5)).astype(BF16)
        ds_ref[0] = ds
        dq_ref[...] = rotate(dot_nn(ds, k_ref[...]), cos_ref[...], sin_ref[...], -1.0).astype(BF16)

    k_at, v_at = q_width // head, (q_width + kv_width) // head
    pipe(
        score_grads,
        (tp, q_width // head),
        [
            pl.BlockSpec((rows, head), lambda i, h: (i, h)),
            pl.BlockSpec((tree_len, head), lambda i, h: (0, k_at + h // group)),
            pl.BlockSpec((tree_len, head), lambda i, h: (0, v_at + h // group)),
            pl.BlockSpec((1, rows, tree_len), lambda i, h: (h, i, 0)),
            pl.BlockSpec((rows, head // 2), lambda i, h: (i, 0)),
            pl.BlockSpec((rows, head // 2), lambda i, h: (i, 0)),
        ],
        [
            pl.BlockSpec((1, rows, tree_len), lambda i, h: (h, i, 0)),
            pl.BlockSpec((rows, head), lambda i, h: (i, h)),
        ],
        dout,
        qkv,
        qkv,
        probs,
        cosine,
        sine,
        dscores,
        dqkv,
    )

    def key_grads(ds_ref, p_ref, q_ref, do_ref, cos_ref, sin_ref, dkv_ref):
        dk = jnp.zeros((rows, head), F32)
        dv = jnp.zeros((rows, head), F32)
        for h in range(group):
            cols = slice(h * head, (h + 1) * head)
            dk = dk + dot_tn(ds_ref[h], q_ref[:, cols])
            dv = dv + dot_tn(p_ref[h], do_ref[:, cols])
        dkv_ref[:, :head] = rotate(dk, cos_ref[...], sin_ref[...], -1.0).astype(BF16)
        dkv_ref[:, head:] = dv.astype(BF16)

    by_key = pl.BlockSpec((group, tree_len, rows), lambda i: (0, 0, i))
    pipe(
        key_grads,
        (tp,),
        [by_key, by_key]
        + [whole_spec(tree_len, q_width)] * 2
        + [rows_spec(rows, head // 2)] * 2,
        [rows_spec(rows, 2 * kv_width)],
        dscores,
        probs,
        qkv.at[:, pl.ds(0, q_width)],
        dout,
        cosine,
        sine,
        dqkv.at[:, pl.ds(q_width, 2 * kv_width)],
    )

    def pair_add(grad, held, total, k):
        add_pipe(
            rows_spec(min(shard, 128), grad.shape[1]),
            shard,
            pair_block(grad, k, half),
            held.at[k],
            total.at[k],
        )

    qkv_across = {}
    for k in order:
        weight_grad(h1, dqkv, grad_qkv, outer, k, 1)
        qkv_across[k] = pair_send(grad_qkv, qkv_pair, k)
    pipe(
        nt_body,
        (tp,),
        [rows_spec(rows, qkv_width), whole_spec(model, qkv_width)],
        [rows_spec(rows, model)],
        dqkv,
        wa_all.at[:, pl.ds(0, qkv_width)],
        f_part,
    )
    f_sum = ScatterTensor(links, f_part, f_got_c, f_got_y, f_far, rows)
    f_sum.start()
    f_sum.across()
    red_up.pump()
    for k in order:
        out_across[k].wait_recv()
        pair_add(grad_out, out_pair, out_sum, k)
        if k:
            red_out.start(k)
    trades.append(trade(red_gate, gate_mine, gate_give, gate_theirs))

    def finish_output(x_ref, *refs):
        refs[-1][...] = (x_ref[...] + sum_refs(refs[:-1])).astype(BF16)

    parts = y_sum.arrive()
    pipe(finish_output, (2,), [spec] * (1 + len(parts)), [spec], x1, *parts, out)

    for k in order:
        qkv_across[k].wait_recv()
        pair_add(grad_qkv, qkv_pair, qkv_sum, k)
        if k:
            red_qkv.start(k)

    def finish_tokens(d_ref, x_ref, g_ref, *refs):
        refs[-1][...] = (
            d_ref[...] + norm_back(sum_refs(refs[:-1]), g_ref[0:1], x_ref[...])
        ).astype(BF16)

    parts = f_sum.arrive()
    pipe(
        finish_tokens,
        (2,),
        [spec, spec, gain_spec] + [spec] * len(parts),
        [spec],
        dx1,
        x,
        gain_rows,
        *parts,
        grad_tok,
    )
    trades.append(trade(red_up, up_mine, up_give, up_theirs))
    red_out.pump()
    red_qkv.pump()
    red_out.arrive()
    red_out.total(0, shard, out_total)
    red_qkv.arrive()
    red_qkv.total(0, shard, qkv_total)
    for copy in trades:
        copy.wait()
    for copy in list(out_across.values()) + list(qkv_across.values()):
        copy.wait_send()
    for item in (red_down, red_gate, red_up, red_out, red_qkv, e_sum, y_sum, f_sum, tree):
        item.sent()


def call(kernel, name, collective, count, shapes, operands):
    anywhere = pl.BlockSpec(memory_space=pl.ANY)
    return pl.pallas_call(
        kernel,
        out_shape=[jax.ShapeDtypeStruct(shape, dtype) for shape, dtype in shapes],
        in_specs=[anywhere] * len(operands),
        out_specs=[anywhere] * len(shapes),
        scratch_shapes=[
            pltpu.SemaphoreType.DMA((count,)),
            pltpu.SemaphoreType.DMA((count,)),
        ],
        compiler_params=pltpu.CompilerParams(
            collective_id=collective, has_side_effects=True, vmem_limit_bytes=VMEM_LIMIT
        ),
        name=name,
    )(*operands)


def make_body(dp, tp):
    outer = dp // 2
    assert tp == 4 and dp == 2 * outer and outer >= 4 and outer & (outer - 1) == 0

    def swap(value, mask):
        return lax.ppermute(value, ("dp", "tensor"), [(i, i ^ mask) for i in range(dp * tp)])

    def relative(value, zi):
        width = value.shape[-1] // outer
        step = 1
        while step < outer:
            blocks = [value[..., i * width : (i + 1) * width] for i in range(outer)]
            swapped = jnp.concatenate([blocks[i ^ step] for i in range(outer)], -1)
            value = jnp.where((zi // step) % 2 == 1, swapped, value)
            step *= 2
        return value

    def body(
        tokens,
        parents,
        attn_gain,
        w_query,
        key_matrix,
        value_matrix,
        w_out,
        mlp_gain,
        w_gate,
        w_up,
        w_down,
        cotangent,
    ):
        di = lax.axis_index("dp")
        zi = di // 2
        upper_x = di % 2 == 1
        rows, model = tokens.shape
        tree_len = rows * tp
        q_width = w_query.shape[1]
        kv_width = key_matrix.shape[1]
        qkv_width = q_width + 2 * kv_width
        heads = q_width // HEAD_SIZE
        assert kv_width == HEAD_SIZE
        shard = w_query.shape[0]
        units = w_gate.shape[1] // 2

        wa = jnp.concatenate([w_query, key_matrix, value_matrix, w_out.T], 1)
        gn = jnp.concatenate(
            [
                jnp.broadcast_to(attn_gain[:, None], (shard, 64)),
                jnp.broadcast_to(mlp_gain[:, None], (shard, 64)),
            ],
            1,
        )
        allowed_mask, place = tree_tables(parents[0], tree_len, BLK)
        cosine, sine = rope_tables(place, HEAD_SIZE)
        bias = jnp.where(allowed_mask, 0.0, NEG).astype(BF16)
        x = relative(tokens, zi).astype(F32)
        xh = normalize(x)[0]
        cot = relative(cotangent, zi)
        (
            wa_all,
            gate_w,
            up_w,
            down_w,
            gain_rows,
            h1,
            qkv,
            probs,
            att,
            x1,
            h2,
            cot_all,
            gate,
            upper,
            hid,
            grad_down,
        ) = call(
            functools.partial(forward_kernel, outer, tp),
            "layer_forward",
            0,
            50 + 7 * outer,
            [
                ((model, qkv_width + q_width), BF16),
                ((model, units), BF16),
                ((model, units), BF16),
                ((model, units), BF16),
                ((8, model), F32),
                ((tree_len, model), BF16),
                ((tree_len, qkv_width), BF16),
                ((heads, tree_len, tree_len), BF16),
                ((tree_len, q_width), BF16),
                ((rows, model), F32),
                ((2 * tree_len, model), BF16),
                ((2 * tree_len, model), BF16),
                ((2 * tree_len, units), BF16),
                ((2 * tree_len, units), BF16),
                ((2 * tree_len, units), BF16),
                ((model, units), BF16),
                ((model, 128), BF16),
                ((tree_len, model), BF16),
                ((2, rows, model), BF16),
                ((rows, model), BF16),
                ((rows, model), BF16),
            ],
            (wa, w_gate, w_up, w_down.T, gn, x, xh, cot, cosine, sine, bias),
        )[:16]

        mlp_held = [((outer, 2 * shard, units), BF16)]
        (
            out,
            grad_tok,
            down_mine,
            down_theirs,
            gate_mine,
            gate_theirs,
            up_mine,
            up_theirs,
            out_total,
            qkv_total,
        ) = call(
            functools.partial(backward_kernel, outer, tp),
            "layer_backward",
            1,
            60 + 10 * outer,
            [((rows, model), BF16)] * 2
            + [((shard, units), F32), ((shard, units), BF16)] * 3
            + [((shard, q_width), F32), ((shard, qkv_width), F32)]
            + [((2 * tree_len, units), BF16)] * 2
            + [((2 * tree_len, model), BF16)] * 2
            + [((4, rows, model), BF16)] * 2
            + [((3, rows, model), BF16)] * 4
            + [((rows, model), F32), ((tree_len, model), BF16)]
            + [((tree_len, q_width), BF16), ((heads, tree_len, tree_len), BF16)]
            + [((tree_len, qkv_width), BF16), ((tree_len, model), BF16)]
            + [((2, rows, model), BF16)]
            + [((rows, model), BF16)] * 2
            + [((model, units), BF16)] * 2
            + [((model, q_width), BF16), ((model, qkv_width), BF16)]
            + [((outer, shard, q_width), BF16), ((outer, shard, qkv_width), BF16)] * 2
            + mlp_held * 3
            + [((outer, shard, q_width), BF16), ((outer, shard, qkv_width), BF16)]
            + [((2 * shard, units), BF16)] * 3
            + [((shard, q_width), BF16), ((shard, qkv_width), BF16)]
            + [((shard, units), BF16)] * 3,
            (
                wa_all,
                gate_w,
                up_w,
                down_w,
                gain_rows,
                h1,
                qkv,
                probs,
                att,
                x1,
                h2,
                cot_all,
                gate,
                upper,
                hid,
                grad_down,
                x,
                cosine,
                sine,
            ),
        )[:10]

        def order_x(mine, theirs):
            theirs = theirs.astype(F32)
            low = jnp.where(upper_x, theirs, mine)
            high = jnp.where(upper_x, mine, theirs)
            return jnp.concatenate([low, high], 1)

        grad_gate = order_x(gate_mine, gate_theirs)
        grad_up = order_x(up_mine, up_theirs)
        grad_query = qkv_total[:, :q_width]
        grad_key = qkv_total[:, q_width : q_width + kv_width]
        grad_value = qkv_total[:, q_width + kv_width :]

        gain_sums = jnp.stack(
            [
                jnp.sum(w_query.astype(F32) * grad_query, 1)
                + jnp.sum(key_matrix.astype(F32) * grad_key, 1)
                + jnp.sum(value_matrix.astype(F32) * grad_value, 1),
                jnp.sum(w_gate.astype(F32) * grad_gate, 1)
                + jnp.sum(w_up.astype(F32) * grad_up, 1),
            ]
        )
        gain_sums = gain_sums + swap(gain_sums, 1)
        gain_sums = gain_sums + swap(gain_sums, 2)
        return (
            relative(out, zi),
            relative(grad_tok, zi),
            gain_sums[0] / attn_gain.astype(F32),
            grad_query,
            grad_key,
            grad_value,
            out_total.T,
            gain_sums[1] / mlp_gain.astype(F32),
            grad_gate,
            grad_up,
            order_x(down_mine, down_theirs).T,
        )

    return body


def solution(mesh):
    in_specs = (
        P(("dp", "tensor"), None),
        P("dp", None),
        P("dp"),
        P("dp", "tensor"),
        P("dp", "tensor"),
        P("dp", "tensor"),
        P("tensor", "dp"),
        P("dp"),
        P("dp", "tensor"),
        P("dp", "tensor"),
        P("tensor", "dp"),
        P(("dp", "tensor"), None),
    )
    out_specs = (
        P(("dp", "tensor"), None),
        P(("dp", "tensor"), None),
        P("dp"),
        P("dp", "tensor"),
        P("dp", "tensor"),
        P("dp", "tensor"),
        P("tensor", "dp"),
        P("dp"),
        P("dp", "tensor"),
        P("dp", "tensor"),
        P("tensor", "dp"),
    )
    body = make_body(mesh.shape["dp"], mesh.shape["tensor"])
    return jax.shard_map(body, mesh=mesh, in_specs=in_specs, out_specs=out_specs, check_vma=False)
```

```python
import functools

import jax
import jax.numpy as jnp
from jax import lax
from jax.experimental import pallas as pl
from jax.experimental.pallas import tpu as pltpu
from jax.sharding import PartitionSpec as P

HEAD_SIZE = 256
BLK = 128


EPS = 1e-06
THETA = 1000042.0
NEG = -1e30
HIGH = lax.Precision.HIGHEST
F32 = jnp.float32
BF16 = jnp.bfloat16
MESH = pl.DeviceIdType.MESH
VMEM_LIMIT = 60 * 2**20


def tree_tables(parent_row, tree_len, block_len):
    blocks = parent_row.shape[0]
    nodes = jnp.arange(blocks, dtype=jnp.int32)
    hops = (parent_row[:, None] == nodes[None, :]).astype(F32)
    reach = jnp.eye(blocks, dtype=F32)
    walk = reach
    for hop_count in range(blocks):
        walk = jnp.dot(walk, hops, precision=HIGH)
        reach = jnp.maximum(reach, walk)
    depth = jnp.sum(reach, axis=1) - 1.0
    rows = jnp.arange(tree_len, dtype=jnp.int32)
    member = (rows[:, None] // block_len == nodes[None, :]).astype(F32)
    visible = jnp.dot(jnp.dot(member, reach, precision=HIGH), member.T, precision=HIGH) > 0.5
    allowed_mask = visible & (rows[None, :] <= rows[:, None])
    place = jnp.dot(member, depth, precision=HIGH) * block_len + (rows % block_len).astype(F32)
    return (allowed_mask, place)


def rope_tables(place, head_dim):
    half = head_dim // 2
    freq = THETA ** (-2.0 * jnp.arange(half, dtype=F32) / head_dim)
    angle = place[:, None] * freq[None, :]
    return (jnp.cos(angle), jnp.sin(angle))


def rotate(values, cosine, sine, sign):
    half = values.shape[-1] // 2
    first, second = values[..., :half], values[..., half:]
    return jnp.concatenate(
        [first * cosine - sign * second * sine, second * cosine + sign * first * sine], -1
    )


def normalize(values):
    inverse = lax.rsqrt(jnp.mean(values * values, axis=-1, keepdims=True) + EPS)
    return (values * inverse, inverse)


def norm_back(grad_normed, gain, values):
    scaled, inverse = normalize(values)
    grad_scaled = grad_normed * gain
    inner = jnp.mean(grad_scaled * scaled, axis=-1, keepdims=True)
    return inverse * (grad_scaled - scaled * inner)


def dot_nn(left, right):
    return jnp.dot(left, right, preferred_element_type=F32)


def dot_nt(left, right):
    return lax.dot_general(left, right, (((1,), (1,)), ((), ())), preferred_element_type=F32)


def dot_tn(left, right):
    return lax.dot_general(left, right, (((0,), (0,)), ((), ())), preferred_element_type=F32)


def flip(index, mask):
    out = index
    bit = 1
    while bit <= mask:
        if mask & bit:
            out = out + bit * (1 - 2 * (index // bit % 2))
        bit *= 2
    return out


class Links:
    def __init__(self, tp, send_sems, recv_sems):
        self.tp = tp
        self.di = lax.axis_index("dp")
        self.ti = lax.axis_index("tensor")
        self.send_sems, self.recv_sems = send_sems, recv_sems
        self.used = 0

    def partner(self, mask):
        return (flip(self.di, mask // self.tp), flip(self.ti, mask % self.tp))

    def greet(self, masks):
        barrier = pltpu.get_barrier_semaphore()
        for mask in masks:
            pl.semaphore_signal(barrier, inc=1, device_id=self.partner(mask), device_id_type=MESH)
        pl.semaphore_wait(barrier, len(masks))

    def remote(self, src, dst, mask):
        index = self.used
        self.used += 1
        return pltpu.make_async_remote_copy(
            src_ref=src,
            dst_ref=dst,
            send_sem=self.send_sems.at[index],
            recv_sem=self.recv_sems.at[index],
            device_id=self.partner(mask),
            device_id_type=MESH,
        )

    def send(self, src, dst, mask):
        copy = self.remote(src, dst, mask)
        copy.start()
        return copy


def line_middle(links):
    zi = links.di // 2
    return (zi == 1) | (zi == 2)


class Spread:
    def __init__(self, links, outer, own, block):
        self.links, self.outer = links, outer
        step = 2 * links.tp
        self.middle = line_middle(links)
        self.copies = {k: links.remote(own, block(k), k * step) for k in range(1, outer)}
        if outer == 4:
            self.onward = links.remote(block(2), block(3), step)

    def start(self):
        if self.outer != 4:
            for copy in self.copies.values():
                copy.start()
            return
        self.copies[2].start()
        self.copies[1].start()

        @pl.when(self.middle)
        def _():
            self.copies[3].start()

    def forward(self):
        self.copies[2].wait_recv()
        if self.outer != 4:
            return

        @pl.when(self.middle)
        def _():
            self.onward.start()

    def arrive(self, k):
        if k == 1 or (self.outer != 4 and k != 2):
            self.copies[k].wait_recv()
        elif k == 3:

            @pl.when(self.middle)
            def _():
                self.copies[3].wait_recv()

            @pl.when(jnp.logical_not(self.middle))
            def _():
                self.onward.wait_recv()

    def sent(self):
        if self.outer != 4:
            for copy in self.copies.values():
                copy.wait_send()
            return
        self.copies[1].wait_send()
        self.copies[2].wait_send()

        @pl.when(self.middle)
        def _():
            self.copies[3].wait_send()
            self.onward.wait_send()


class ReduceZ:
    def __init__(self, links, outer, block, held, staged):
        self.links, self.outer, self.block, self.held, self.staged = (
            links,
            outer,
            block,
            held,
            staged,
        )
        step = 2 * links.tp
        self.middle = line_middle(links)
        self.copies = {k: links.remote(block(k), held.at[k], k * step) for k in range(1, outer)}
        if outer == 4:
            self.inward = links.remote(block(3), held.at[0], step)
            self.summed = links.remote(staged, held.at[2], 2 * step)

    def on_ends(self, *actions):
        @pl.when(jnp.logical_not(self.middle))
        def _():
            for action in actions:
                action()

    def on_middle(self, *actions):
        @pl.when(self.middle)
        def _():
            for action in actions:
                action()

    def start(self, k):
        if self.outer != 4 or k == 1:
            self.copies[k].start()
        elif k == 3:
            self.on_ends(self.inward.start)
            self.on_middle(self.copies[3].start)
        elif k == 2:
            self.on_ends(self.copies[2].start)

    def start_all(self):
        for k in range(self.outer - 1, 0, -1):
            self.start(k)

    def pump(self):
        if self.outer != 4:
            return

        def add():
            rows, width = self.staged.shape
            spec = rows_spec(min(rows, 128), width)
            add_pipe(spec, rows, self.block(2), self.held.at[0], self.staged)

        self.on_middle(self.inward.wait_recv, add, self.summed.start)

    def arrive(self):
        if self.outer != 4:
            for copy in self.copies.values():
                copy.wait_recv()
            return
        self.copies[1].wait_recv()
        self.on_middle(self.copies[2].wait_recv, self.copies[3].wait_recv)
        self.on_ends(self.summed.wait_recv)

    def total(self, lo, rows, out):
        width = self.staged.shape[1]
        spec = rows_spec(min(rows, 128), width)

        def add(*refs):
            value = refs[0][...].astype(F32)
            for ref in refs[1:-1]:
                value = value + ref[...].astype(F32)
            refs[-1][...] = value.astype(refs[-1].dtype)

        def over(kept):
            parts = [self.block(0)] + [self.held.at[k] for k in kept]
            parts = [part.at[pl.ds(lo, rows)] for part in parts]
            grid = (rows // min(rows, 128),)
            pipe(add, grid, [spec] * len(parts), [spec], *parts, out)

        if self.outer != 4:
            over(range(1, self.outer))
            return
        self.on_middle(lambda: over([1, 2, 3]))
        self.on_ends(lambda: over([1, 2]))

    def sent(self):
        if self.outer != 4:
            for copy in self.copies.values():
                copy.wait_send()
            return
        self.copies[1].wait_send()
        self.on_middle(self.copies[3].wait_send, self.summed.wait_send)
        self.on_ends(self.copies[2].wait_send, self.inward.wait_send)


def gather_units(links, full, rows):
    tp = links.tp

    def block(m, lo=0, n=None):
        return full.at[pl.ds(m * rows + lo, rows if n is None else n)]

    half = rows // 2
    sent = []

    def send(m, mask, lo=0, n=None):
        copy = links.send(block(m, lo, n), block(m ^ mask, lo, n), mask)
        sent.append(copy)
        return copy

    x = send(0, tp)
    y = send(0, 2)
    c0 = send(0, 1)
    yield
    y.wait_recv()
    low = send(2, tp, half, half)
    c2 = send(2, 1)
    x.wait_recv()
    high = send(tp, 2, 0, half)
    c4 = send(tp, 1)
    yield
    low.wait_recv()
    high.wait_recv()
    c6 = send(tp + 2, 1)
    yield
    for copy in (c0, c2, c4, c6):
        copy.wait_recv()
    for copy in sent:
        copy.wait_send()
    yield


def run(stages):
    for _ in stages:
        pass


def pipe(body, grid, in_specs, out_specs, *refs):
    pltpu.emit_pipeline(body, grid=grid, in_specs=in_specs, out_specs=out_specs)(*refs)


def rows_spec(rows, width):
    return pl.BlockSpec((rows, width), lambda i: (i, 0))


def whole_spec(rows, width):
    return pl.BlockSpec((rows, width), lambda i: (0, 0))


def once_spec(rows, width):
    return pl.BlockSpec((rows, width), lambda i: (0, 0), pipeline_mode=pl.Buffered(1))


def add_refs(a_ref, b_ref, o_ref):
    o_ref[...] = (a_ref[...].astype(F32) + b_ref[...].astype(F32)).astype(o_ref.dtype)


def add_pipe(spec, rows, a, b, out):
    pipe(add_refs, (rows // spec.block_shape[0],), [spec, spec], [spec], a, b, out)


def copy_body(a_ref, o_ref):
    o_ref[...] = a_ref[...]


def keep(src, dst):
    rows, width = src.shape
    spec = rows_spec(min(rows, 128), width)
    pipe(copy_body, (rows // min(rows, 128),), [spec], [spec], src, dst)


def nt_body(a_ref, b_ref, o_ref):
    o_ref[...] = dot_nt(a_ref[...], b_ref[...]).astype(BF16)


def nn_body(a_ref, b_ref, o_ref):
    o_ref[...] = dot_nn(a_ref[...], b_ref[...]).astype(BF16)


def tn_body(a_ref, b_ref, o_ref):
    o_ref[...] = dot_tn(a_ref[...], b_ref[...]).astype(BF16)


def weight_grad(acts, grads, out, blocks, first=0, count=None):
    tokens, model = acts.shape
    width = grads.shape[1]
    size = model // blocks
    count = blocks if count is None else count
    pipe(
        tn_body,
        (count,),
        [pl.BlockSpec((tokens, size), lambda i: (0, first + i)), once_spec(tokens, width)],
        [pl.BlockSpec((size, width), lambda i: (first + i, 0))],
        acts,
        grads,
        out,
    )


class ScatterTensor:
    def __init__(self, links, part, got_c, got_y, far, rows):
        self.links, self.part, self.got_c, self.got_y, self.far = links, part, got_c, got_y, far
        self.rows = rows
        self.model = part.shape[1]
        self.spec = rows_spec(rows // 2, self.model)

    def block(self, mask):
        rows = self.rows
        return self.part.at[
            pl.ds(pl.multiple_of(flip(self.links.ti, mask) * rows, rows), rows)
        ]

    def start(self):
        self.copies = [
            self.links.send(self.block(3), self.got_c.at[1], 1),
            self.links.send(self.block(1), self.got_c.at[0], 1),
        ]

    def across(self):
        self.copies[0].wait_recv()
        add_pipe(self.spec, self.rows, self.block(2), self.got_c.at[1], self.far)
        self.copies.append(self.links.send(self.far, self.got_y, 2))

    def arrive(self):
        self.copies[1].wait_recv()
        self.copies[2].wait_recv()
        return [self.block(0), self.got_c.at[0], self.got_y]

    def sent(self):
        for copy in self.copies:
            copy.wait_send()


class ScatterUnits:
    def __init__(self, links, part, got_c, near, got, rows):
        self.links, self.part, self.got_c, self.near, self.got = links, part, got_c, near, got
        self.rows, self.model = rows, part.shape[1]
        self.sends = []

    def send(self, src, dst, mask):
        copy = self.links.send(src, dst, mask)
        self.sends.append(copy)
        return copy

    def block(self, m):
        return self.part.at[pl.ds(m * self.rows, self.rows)]

    def start(self):
        self.from_c = [self.send(self.block(2 * i + 1), self.got_c.at[i], 1) for i in range(4)]

    def add(self, m, slot, lo, n):
        rows = pl.ds(lo, n)
        add_pipe(
            rows_spec(n, self.model),
            n,
            self.block(m).at[rows],
            self.got_c.at[m // 2].at[rows],
            self.near.at[slot].at[rows],
        )

    def across(self):
        tp, rows, half = self.links.tp, self.rows, self.rows // 2
        low, high = pl.ds(0, half), pl.ds(half, half)
        near, got = self.near, self.got
        for copy in self.from_c:
            copy.wait_recv()
        self.add(6, 2, 0, half)
        self.top = self.send(near.at[2].at[low], got.at[2].at[low], tp)
        self.add(6, 2, half, half)
        self.bottom = self.send(near.at[2].at[high], got.at[2].at[high], 2)
        self.add(4, 0, 0, half)
        self.x_low = self.send(near.at[0].at[low], got.at[0].at[low], tp)
        self.add(2, 1, half, half)
        self.y_high = self.send(near.at[1].at[high], got.at[1].at[high], 2)

    def finish(self):
        tp, half = self.links.tp, self.rows // 2
        low, high = pl.ds(0, half), pl.ds(half, half)
        near, got = self.near, self.got

        def add3(m, slot, rows):
            def body(a_ref, b_ref, c_ref, o_ref):
                o_ref[...] = (
                    a_ref[...].astype(F32) + b_ref[...].astype(F32) + c_ref[...].astype(F32)
                ).astype(BF16)

            spec = rows_spec(half, self.model)
            pipe(
                body,
                (1,),
                [spec] * 3,
                [spec],
                self.block(m).at[rows],
                self.got_c.at[m // 2].at[rows],
                got.at[2].at[rows],
                near.at[slot].at[rows],
            )

        self.top.wait_recv()
        add3(2, 1, low)
        self.y_low = self.send(near.at[1].at[low], got.at[1].at[low], 2)
        self.bottom.wait_recv()
        add3(4, 0, high)
        self.x_high = self.send(near.at[0].at[high], got.at[0].at[high], tp)

    def arrive(self):
        for copy in (self.x_low, self.x_high, self.y_low, self.y_high):
            copy.wait_recv()
        return [self.block(0), self.got_c.at[0], self.got.at[0], self.got.at[1]]

    def sent(self):
        for copy in self.sends:
            copy.wait_send()


def sum_refs(refs):
    value = refs[0][...].astype(F32)
    for ref in refs[1:]:
        value = value + ref[...].astype(F32)
    return value


class GatherTree:
    def __init__(self, links, full, rows):
        self.links, self.full, self.rows = links, full, rows

    def block(self, mask):
        rows = self.rows
        return self.full.at[
            pl.ds(pl.multiple_of(flip(self.links.ti, mask) * rows, rows), rows)
        ]

    def start(self):
        self.y = self.links.send(self.block(0), self.block(0), 2)
        self.c = self.links.send(self.block(0), self.block(0), 1)

    def across(self):
        self.y.wait_recv()
        self.yc = self.links.send(self.block(2), self.block(2), 1)

    def arrive(self):
        self.c.wait_recv()
        self.yc.wait_recv()

    def sent(self):
        for copy in (self.y, self.c, self.yc):
            copy.wait_send()


def greet_all(links, outer):
    step = 2 * links.tp
    links.greet([1, 2, links.tp] + [k * step for k in range(1, outer)])


def forward_kernel(
    outer,
    tp,
    wq,
    wo,
    wg,
    wu,
    wd,
    gn,
    x,
    xh,
    cot,
    cosine,
    sine,
    bias,
    wq_all,
    wo_all,
    gate_w,
    up_w,
    gain_rows,
    h1,
    qkv,
    probs,
    att,
    x1,
    h2,
    cot_all,
    dgate,
    dupper,
    hid,
    down_w,
    grad_down,
    gate,
    upper,
    gn_all,
    part,
    got_c,
    got_y,
    far,
    dhid,
    send_sems,
    recv_sems,
):
    links = Links(tp, send_sems, recv_sems)
    shard, qkv_width = wq.shape
    units = gate_w.shape[1]
    rows, model = xh.shape
    tree_len = rows * tp
    q_width = att.shape[1]
    kv_width = (qkv_width - q_width) // 2
    head = HEAD_SIZE
    xi = links.di % 2
    greet_all(links, outer)

    def shard_block(full, k):
        return full.at[pl.ds(pl.multiple_of((2 * k + xi) * shard, shard), shard)]

    mine = pl.ds(pl.multiple_of(xi * units, units), units)
    peers = pl.ds(pl.multiple_of((1 - xi) * units, units), units)
    place = pl.ds(pl.multiple_of(xi * shard, shard), shard)

    def send_pair(w, full):
        return links.send(w.at[:, peers], full.at[place], tp)

    def mlp_spread(full):
        return Spread(
            links,
            outer,
            full.at[pl.ds(0, 2 * shard)],
            lambda k: full.at[pl.ds(k * 2 * shard, 2 * shard)],
        )

    gains = Spread(links, outer, gn, lambda k: shard_block(gn_all, k))
    attn = Spread(links, outer, wq, lambda k: shard_block(wq_all, k))
    attn_out = Spread(links, outer, wo, lambda k: shard_block(wo_all, k))
    gains.start()
    across_gn = [links.send(gn, shard_block(gn_all, 0), tp)]
    attn.start()
    across = [links.send(wq, shard_block(wq_all, 0), tp)]
    attn_out.start()
    pair = [send_pair(wg, gate_w)]
    across_out = [links.send(wo, shard_block(wo_all, 0), tp)]

    def cross(full, k, copies):
        copies.append(links.send(shard_block(full, k), shard_block(full, k), tp))

    keep(gn, shard_block(gn_all, 0))
    keep(wg.at[:, mine], gate_w.at[place])

    gains.forward()
    for k in range(1, outer):
        gains.arrive(k)
        across_gn.append(links.send(shard_block(gn_all, k), shard_block(gn_all, k), tp))
    keep(wq, shard_block(wq_all, 0))
    keep(wo, shard_block(wo_all, 0))
    for copy in across_gn:
        copy.wait_recv()

    def gain_rows_of(g_ref, o_ref):
        lane = lax.broadcasted_iota(jnp.int32, (8, 128), 1)
        row = lax.broadcasted_iota(jnp.int32, (8, 128), 0)
        pick = jnp.where((row < 2) & (lane == row * 64), 1.0, 0.0).astype(BF16)
        o_ref[...] = dot_nt(pick, g_ref[...])

    pipe(gain_rows_of, (1,), [whole_spec(model, 128)], [whole_spec(8, model)], gn_all, gain_rows)
    spec = rows_spec(rows // 2, model)
    gain_spec = whole_spec(8, model)

    def scale_tokens(x_ref, g_ref, o_ref):
        o_ref[...] = (x_ref[...] * g_ref[0:1]).astype(BF16)

    tree = GatherTree(links, h1, rows)
    pipe(scale_tokens, (2,), [spec, gain_spec], [spec], xh, gain_rows, tree.block(0))
    tree.start()
    keep(wu.at[:, mine], up_w.at[place])
    keep(wd.at[:, mine], down_w.at[place])
    keep(cot, cot_all.at[pl.ds(0, rows)])

    spreads = [mlp_spread(full) for full in (gate_w, up_w, down_w)]
    attn.forward()
    cross(wq_all, 2, across)
    for k in range(1, outer):
        if k != 2:
            attn.arrive(k)
            cross(wq_all, k, across)
    tree.across()
    attn_out.forward()
    cross(wo_all, 2, across_out)
    pair[0].wait_recv()
    spreads[0].start()
    for k in range(1, outer):
        if k != 2:
            attn_out.arrive(k)
            cross(wo_all, k, across_out)
    pair.append(send_pair(wu, up_w))
    later = gather_units(links, cot_all, rows)
    next(later)
    pair.append(send_pair(wd, down_w))
    tree.arrive()
    for copy in across:
        copy.wait_recv()

    def project(x_ref, w_ref, cos_ref, sin_ref, out_ref):
        raw = dot_nn(x_ref[...], w_ref[...])
        for slot in range((q_width + kv_width) // head):
            cols = slice(slot * head, (slot + 1) * head)
            out_ref[:, cols] = rotate(raw[:, cols], cos_ref[...], sin_ref[...], 1.0).astype(BF16)
        out_ref[:, q_width + kv_width :] = raw[:, q_width + kv_width :].astype(BF16)

    pipe(
        project,
        (tp,),
        [
            rows_spec(rows, model),
            whole_spec(model, qkv_width),
            rows_spec(rows, head // 2),
            rows_spec(rows, head // 2),
        ],
        [rows_spec(rows, qkv_width)],
        h1,
        wq_all,
        cosine,
        sine,
        qkv,
    )

    group = q_width // kv_width

    def attend(q_ref, k_ref, v_ref, b_ref, p_ref, o_ref):
        scores = dot_nt(q_ref[...], k_ref[...]) * (head**-0.5) + b_ref[...].astype(F32)
        weights = jnp.exp(scores - jnp.max(scores, axis=-1, keepdims=True))
        weights = (weights / jnp.sum(weights, axis=-1, keepdims=True)).astype(BF16)
        p_ref[0] = weights
        o_ref[...] = dot_nn(weights, v_ref[...]).astype(BF16)

    k_at, v_at = q_width // head, (q_width + kv_width) // head
    pipe(
        attend,
        (tp, q_width // head),
        [
            pl.BlockSpec((rows, head), lambda i, h: (i, h)),
            pl.BlockSpec((tree_len, head), lambda i, h: (0, k_at + h // group)),
            pl.BlockSpec((tree_len, head), lambda i, h: (0, v_at + h // group)),
            pl.BlockSpec((rows, tree_len), lambda i, h: (i, 0)),
        ],
        [
            pl.BlockSpec((1, rows, tree_len), lambda i, h: (h, i, 0)),
            pl.BlockSpec((rows, head), lambda i, h: (i, h)),
        ],
        qkv,
        qkv,
        qkv,
        bias,
        probs,
        att,
    )
    for copy in across_out:
        copy.wait_recv()
    pipe(
        nt_body,
        (tp,),
        [rows_spec(rows, q_width), whole_spec(model, q_width)],
        [rows_spec(rows, model)],
        att,
        wo_all,
        part,
    )
    mixed = ScatterTensor(links, part, got_c, got_y, far, rows)
    mixed.start()
    spreads[0].forward()
    pair[1].wait_recv()
    spreads[1].start()
    mixed.across()
    next(later)
    parts = mixed.arrive()

    def residual(x_ref, a_ref, b_ref, c_ref, g_ref, x1_ref, h_ref):
        total = x_ref[...] + sum_refs((a_ref, b_ref, c_ref))
        x1_ref[...] = total
        h_ref[...] = (normalize(total)[0] * g_ref[1:2]).astype(BF16)

    pipe(
        residual,
        (2,),
        [spec] * 4 + [gain_spec],
        [spec] * 2,
        x,
        *parts,
        gain_rows,
        x1,
        h2.at[pl.ds(0, rows)],
    )
    stages = gather_units(links, h2, rows)
    next(stages)
    next(later)
    next(stages)
    spreads[1].forward()
    pair[2].wait_recv()
    spreads[2].start()
    next(stages)
    next(stages)
    run(later)

    for spread in spreads[:2]:
        for k in range(1, outer):
            spread.arrive(k)

    def expand(x_ref, g_ref, u_ref, a_ref, b_ref, h_ref):
        @pl.when(pl.program_id(0) == tp)
        def _():
            spreads[2].forward()

        g = dot_nn(x_ref[...], g_ref[...])
        u = dot_nn(x_ref[...], u_ref[...])
        sigma = jax.nn.sigmoid(g)
        swish = g * sigma
        a_ref[...] = (u * sigma * (1.0 + g * (1.0 - sigma))).astype(BF16)
        b_ref[...] = swish.astype(BF16)
        h_ref[...] = (swish * u).astype(BF16)

    pipe(
        expand,
        (2 * tp,),
        [rows_spec(rows, model), whole_spec(model, units), whole_spec(model, units)],
        [rows_spec(rows, units)] * 3,
        h2,
        gate_w,
        up_w,
        gate,
        upper,
        hid,
    )
    weight_grad(cot_all, hid, grad_down, 4)

    known = (outer - 1) * 2 * shard
    unit_spec = rows_spec(rows, units)

    def contract_known(c_ref, d_ref):
        at = pl.ds(pl.multiple_of(pl.program_id(0) * rows, rows), rows)
        dhid[at] = dot_nn(c_ref[...], d_ref[...])

    def contract_last(c_ref, d_ref, a_ref, b_ref, dg_ref, du_ref):
        at = pl.ds(pl.multiple_of(pl.program_id(0) * rows, rows), rows)
        value = dhid[at] + dot_nn(c_ref[...], d_ref[...])
        dg_ref[...] = (value * a_ref[...].astype(F32)).astype(BF16)
        du_ref[...] = (value * b_ref[...].astype(F32)).astype(BF16)

    for k in range(1, outer - 1):
        spreads[2].arrive(k)
    pipe(
        contract_known,
        (2 * tp,),
        [rows_spec(rows, known), once_spec(known, units)],
        [],
        cot_all.at[:, pl.ds(0, known)],
        down_w.at[pl.ds(0, known)],
    )
    spreads[2].arrive(outer - 1)
    pipe(
        contract_last,
        (2 * tp,),
        [rows_spec(rows, model - known), once_spec(model - known, units), unit_spec, unit_spec],
        [unit_spec] * 2,
        cot_all.at[:, pl.ds(known, model - known)],
        down_w.at[pl.ds(known, model - known)],
        gate,
        upper,
        dgate,
        dupper,
    )
    for spread in [gains, attn, attn_out] + spreads:
        spread.sent()
    for copy in across_gn + across + across_out + pair:
        copy.wait_send()
    tree.sent()
    mixed.sent()


def backward_kernel(
    outer,
    tp,
    wq_all,
    wo_all,
    gate_w,
    up_w,
    gain_rows,
    h1,
    qkv,
    probs,
    att,
    x1,
    h2,
    cot,
    dgate,
    dupper,
    hid,
    down_w,
    grad_down,
    x,
    cosine,
    sine,
    out,
    grad_tok,
    down_mine,
    down_theirs,
    gate_mine,
    gate_theirs,
    up_mine,
    up_theirs,
    out_total,
    qkv_total,
    dx1,
    dscores,
    grad_gate,
    grad_up,
    grad_out,
    grad_qkv,
    down_held,
    gate_held,
    up_held,
    out_held,
    qkv_held,
    down_staged,
    gate_staged,
    up_staged,
    out_staged,
    qkv_staged,
    down_give,
    gate_give,
    up_give,
    y_part,
    e_part,
    e_got_c,
    y_got_c,
    e_near,
    y_near,
    e_got,
    y_got,
    dx1_low,
    dout,
    dqkv,
    f_got_c,
    f_got_y,
    f_far,
    out_pair,
    qkv_pair,
    out_sum,
    qkv_sum,
    send_sems,
    recv_sems,
):
    links = Links(tp, send_sems, recv_sems)
    rows, model = x.shape
    tree_len = rows * tp
    units = gate_w.shape[1]
    q_width = att.shape[1]
    qkv_width = qkv.shape[1]
    kv_width = (qkv_width - q_width) // 2
    head = HEAD_SIZE
    group = q_width // kv_width
    shard = model // (2 * outer)
    xi = links.di % 2
    half = pl.multiple_of(xi * shard, shard)
    other = pl.multiple_of((1 - xi) * shard, shard)
    spec = rows_spec(rows // 2, model)
    gain_spec = whole_spec(8, model)
    greet_all(links, outer)

    def mlp_reduce(grad, held, staged):
        return ReduceZ(
            links, outer, lambda k: grad.at[pl.ds(k * 2 * shard, 2 * shard)], held, staged
        )

    def trade(reduce, mine, give, theirs):
        reduce.arrive()
        reduce.total(other, shard, give)
        copy = links.send(give, theirs, tp)
        reduce.total(half, shard, mine)
        return copy

    red_down = mlp_reduce(grad_down, down_held, down_staged)
    red_gate = mlp_reduce(grad_gate, gate_held, gate_staged)
    red_up = mlp_reduce(grad_up, up_held, up_staged)
    red_down.start_all()

    y_sum = ScatterUnits(links, y_part, y_got_c, y_near, y_got, rows)

    def every_other(first, block_rows, width):
        return pl.BlockSpec((block_rows, width), lambda i: (2 * i + first, 0))

    def back(dg_ref, du_ref, g_ref, u_ref, o_ref):
        o_ref[...] = (dot_nt(dg_ref[...], g_ref[...]) + dot_nt(du_ref[...], u_ref[...])).astype(
            BF16
        )

    def back_blocks(first):
        pipe(
            back,
            (tp,),
            [every_other(first, rows, units)] * 2 + [once_spec(model, units)] * 2,
            [every_other(first, rows, model)],
            dgate,
            dupper,
            gate_w,
            up_w,
            e_part,
        )

    e_sum = ScatterUnits(links, e_part, e_got_c, e_near, e_got, rows)
    back_blocks(1)
    e_sum.start()
    red_down.pump()
    back_blocks(0)
    e_sum.across()
    weight_grad(h2, dgate, grad_gate, 4)
    red_gate.start_all()
    e_sum.finish()
    weight_grad(h2, dupper, grad_up, 4)
    red_up.start_all()
    trades = [trade(red_down, down_mine, down_give, down_theirs)]

    tree = GatherTree(links, dx1_low, rows)

    def through_norm(c_ref, x_ref, g_ref, *refs):
        value = c_ref[...].astype(F32) + norm_back(sum_refs(refs[:-2]), g_ref[1:2], x_ref[...])
        refs[-2][...] = value
        refs[-1][...] = value.astype(BF16)

    parts = e_sum.arrive()
    pipe(
        through_norm,
        (2,),
        [spec, spec, gain_spec] + [spec] * len(parts),
        [spec] * 2,
        cot,
        x1,
        gain_rows,
        *parts,
        dx1,
        tree.block(0),
    )
    tree.start()
    red_gate.pump()
    pipe(
        nt_body,
        (2 * tp,),
        [rows_spec(rows, units), once_spec(model, units)],
        [rows_spec(rows, model)],
        hid,
        down_w,
        y_part,
    )
    tree.across()
    y_sum.start()
    tree.arrive()

    pipe(
        nn_body,
        (tp,),
        [rows_spec(rows, model), whole_spec(model, q_width)],
        [rows_spec(rows, q_width)],
        dx1_low,
        wo_all,
        dout,
    )

    def pair_block(full, k, at):
        return full.at[pl.ds(pl.multiple_of(k * 2 * shard + at, shard), shard)]

    def pair_send(grad, held, k):
        return links.send(pair_block(grad, k, other), held.at[k], tp)

    red_out = ReduceZ(links, outer, lambda k: out_sum.at[k], out_held, out_staged)
    red_qkv = ReduceZ(links, outer, lambda k: qkv_sum.at[k], qkv_held, qkv_staged)
    weight_grad(dx1_low, att, grad_out, 4)
    order = list(range(outer - 1, -1, -1))
    out_across = {k: pair_send(grad_out, out_pair, k) for k in order}
    y_sum.across()

    def score_grads(do_ref, k_ref, v_ref, p_ref, cos_ref, sin_ref, ds_ref, dq_ref):
        p = p_ref[0].astype(F32)
        dp = dot_nt(do_ref[...], v_ref[...])
        inner = jnp.sum(p * dp, axis=-1, keepdims=True)
        ds = (p * (dp - inner) * (head**-0.5)).astype(BF16)
        ds_ref[0] = ds
        dq_ref[...] = rotate(dot_nn(ds, k_ref[...]), cos_ref[...], sin_ref[...], -1.0).astype(BF16)

    k_at, v_at = q_width // head, (q_width + kv_width) // head
    pipe(
        score_grads,
        (tp, q_width // head),
        [
            pl.BlockSpec((rows, head), lambda i, h: (i, h)),
            pl.BlockSpec((tree_len, head), lambda i, h: (0, k_at + h // group)),
            pl.BlockSpec((tree_len, head), lambda i, h: (0, v_at + h // group)),
            pl.BlockSpec((1, rows, tree_len), lambda i, h: (h, i, 0)),
            pl.BlockSpec((rows, head // 2), lambda i, h: (i, 0)),
            pl.BlockSpec((rows, head // 2), lambda i, h: (i, 0)),
        ],
        [
            pl.BlockSpec((1, rows, tree_len), lambda i, h: (h, i, 0)),
            pl.BlockSpec((rows, head), lambda i, h: (i, h)),
        ],
        dout,
        qkv,
        qkv,
        probs,
        cosine,
        sine,
        dscores,
        dqkv,
    )

    def key_grads(ds_ref, p_ref, q_ref, do_ref, cos_ref, sin_ref, dkv_ref):
        dk = jnp.zeros((rows, head), F32)
        dv = jnp.zeros((rows, head), F32)
        for h in range(group):
            cols = slice(h * head, (h + 1) * head)
            dk = dk + dot_tn(ds_ref[h], q_ref[:, cols])
            dv = dv + dot_tn(p_ref[h], do_ref[:, cols])
        dkv_ref[:, :head] = rotate(dk, cos_ref[...], sin_ref[...], -1.0).astype(BF16)
        dkv_ref[:, head:] = dv.astype(BF16)

    by_key = pl.BlockSpec((group, tree_len, rows), lambda i: (0, 0, i))
    pipe(
        key_grads,
        (tp,),
        [by_key, by_key]
        + [whole_spec(tree_len, q_width)] * 2
        + [rows_spec(rows, head // 2)] * 2,
        [rows_spec(rows, 2 * kv_width)],
        dscores,
        probs,
        qkv.at[:, pl.ds(0, q_width)],
        dout,
        cosine,
        sine,
        dqkv.at[:, pl.ds(q_width, 2 * kv_width)],
    )

    y_sum.finish()

    def pair_add(grad, held, total, k):
        add_pipe(
            rows_spec(min(shard, 128), grad.shape[1]),
            shard,
            pair_block(grad, k, half),
            held.at[k],
            total.at[k],
        )

    qkv_across = {}
    weight_grad(h1, dqkv, grad_qkv, 4)
    for k in order:
        qkv_across[k] = pair_send(grad_qkv, qkv_pair, k)
    e_sum.sent()
    f_part = e_part.at[pl.ds(0, tree_len)]
    pipe(
        nt_body,
        (tp,),
        [rows_spec(rows, qkv_width), whole_spec(model, qkv_width)],
        [rows_spec(rows, model)],
        dqkv,
        wq_all,
        f_part,
    )
    f_sum = ScatterTensor(links, f_part, f_got_c, f_got_y, f_far, rows)
    f_sum.start()
    f_sum.across()
    red_up.pump()
    for k in order:
        out_across[k].wait_recv()
        pair_add(grad_out, out_pair, out_sum, k)
        if k:
            red_out.start(k)
    trades.append(trade(red_gate, gate_mine, gate_give, gate_theirs))

    def finish_output(x_ref, *refs):
        refs[-1][...] = (x_ref[...] + sum_refs(refs[:-1])).astype(BF16)

    parts = y_sum.arrive()
    pipe(finish_output, (2,), [spec] * (1 + len(parts)), [spec], x1, *parts, out)

    for k in order:
        qkv_across[k].wait_recv()
        pair_add(grad_qkv, qkv_pair, qkv_sum, k)
        if k:
            red_qkv.start(k)

    def finish_tokens(d_ref, x_ref, g_ref, *refs):
        refs[-1][...] = (
            d_ref[...] + norm_back(sum_refs(refs[:-1]), g_ref[0:1], x_ref[...])
        ).astype(BF16)

    parts = f_sum.arrive()
    pipe(
        finish_tokens,
        (2,),
        [spec, spec, gain_spec] + [spec] * len(parts),
        [spec],
        dx1,
        x,
        gain_rows,
        *parts,
        grad_tok,
    )
    trades.append(trade(red_up, up_mine, up_give, up_theirs))
    red_out.pump()
    red_qkv.pump()
    red_out.arrive()
    red_out.total(0, shard, out_total)
    red_qkv.arrive()
    red_qkv.total(0, shard, qkv_total)
    for copy in trades:
        copy.wait()
    for copy in list(out_across.values()) + list(qkv_across.values()):
        copy.wait_send()
    for item in (red_down, red_gate, red_up, red_out, red_qkv, y_sum, f_sum, tree):
        item.sent()


def call(kernel, name, collective, count, shapes, scratch, operands):
    anywhere = pl.BlockSpec(memory_space=pl.ANY)
    return pl.pallas_call(
        kernel,
        out_shape=[jax.ShapeDtypeStruct(shape, dtype) for shape, dtype in shapes],
        in_specs=[anywhere] * len(operands),
        out_specs=[anywhere] * len(shapes),
        scratch_shapes=[pltpu.VMEM(shape, dtype) for shape, dtype in scratch]
        + [
            pltpu.SemaphoreType.DMA((count,)),
            pltpu.SemaphoreType.DMA((count,)),
        ],
        compiler_params=pltpu.CompilerParams(
            collective_id=collective, has_side_effects=True, vmem_limit_bytes=VMEM_LIMIT
        ),
        name=name,
    )(*operands)


def make_body(dp, tp):
    outer = dp // 2
    assert tp == 4 and dp == 2 * outer and outer >= 4 and outer & (outer - 1) == 0

    def swap(value, mask):
        return lax.ppermute(value, ("dp", "tensor"), [(i, i ^ mask) for i in range(dp * tp)])

    def relative(value, zi):
        width = value.shape[-1] // outer
        step = 1
        while step < outer:
            blocks = [value[..., i * width : (i + 1) * width] for i in range(outer)]
            swapped = jnp.concatenate([blocks[i ^ step] for i in range(outer)], -1)
            value = jnp.where((zi // step) % 2 == 1, swapped, value)
            step *= 2
        return value

    def body(
        tokens,
        parents,
        attn_gain,
        w_query,
        key_matrix,
        value_matrix,
        w_out,
        mlp_gain,
        w_gate,
        w_up,
        w_down,
        cotangent,
    ):
        di = lax.axis_index("dp")
        zi = di // 2
        upper_x = di % 2 == 1
        rows, model = tokens.shape
        tree_len = rows * tp
        q_width = w_query.shape[1]
        kv_width = key_matrix.shape[1]
        qkv_width = q_width + 2 * kv_width
        heads = q_width // HEAD_SIZE
        assert kv_width == HEAD_SIZE
        shard = w_query.shape[0]
        units = w_gate.shape[1] // 2

        wq = jnp.concatenate([w_query, key_matrix, value_matrix], 1)
        gn = jnp.concatenate(
            [
                jnp.broadcast_to(attn_gain[:, None], (shard, 64)),
                jnp.broadcast_to(mlp_gain[:, None], (shard, 64)),
            ],
            1,
        )
        allowed_mask, place = tree_tables(parents[0], tree_len, BLK)
        cosine, sine = rope_tables(place, HEAD_SIZE)
        bias = jnp.where(allowed_mask, 0.0, NEG).astype(BF16)
        x = relative(tokens, zi).astype(F32)
        xh = normalize(x)[0]
        cot = relative(cotangent, zi)
        (
            wq_all,
            wo_all,
            gate_w,
            up_w,
            gain_rows,
            h1,
            qkv,
            probs,
            att,
            x1,
            h2,
            cot_all,
            dgate,
            dupper,
            hid,
            down_w,
            grad_down,
        ) = call(
            functools.partial(forward_kernel, outer, tp),
            "layer_forward",
            0,
            60 + 9 * outer,
            [
                ((model, qkv_width), BF16),
                ((model, q_width), BF16),
                ((model, units), BF16),
                ((model, units), BF16),
                ((8, model), F32),
                ((tree_len, model), BF16),
                ((tree_len, qkv_width), BF16),
                ((heads, tree_len, tree_len), BF16),
                ((tree_len, q_width), BF16),
                ((rows, model), F32),
                ((2 * tree_len, model), BF16),
                ((2 * tree_len, model), BF16),
                ((2 * tree_len, units), BF16),
                ((2 * tree_len, units), BF16),
                ((2 * tree_len, units), BF16),
                ((model, units), BF16),
                ((model, units), BF16),
                ((2 * tree_len, units), BF16),
                ((2 * tree_len, units), BF16),
                ((model, 128), BF16),
            ],
            [
                ((tree_len, model), BF16),
                ((2, rows, model), BF16),
                ((rows, model), BF16),
                ((rows, model), BF16),
                ((2 * tree_len, units), F32),
            ],
            (wq, w_out.T, w_gate, w_up, w_down.T, gn, x, xh, cot, cosine, sine, bias),
        )[:17]

        (
            out,
            grad_tok,
            down_mine,
            down_theirs,
            gate_mine,
            gate_theirs,
            up_mine,
            up_theirs,
            out_total,
            qkv_total,
        ) = call(
            functools.partial(backward_kernel, outer, tp),
            "layer_backward",
            1,
            60 + 10 * outer,
            [((rows, model), BF16)] * 2
            + [((shard, units), F32), ((shard, units), BF16)] * 3
            + [((shard, q_width), F32), ((shard, qkv_width), F32)]
            + [((rows, model), F32), ((heads, tree_len, tree_len), BF16)]
            + [((model, units), BF16)] * 2
            + [((model, q_width), BF16), ((model, qkv_width), BF16)]
            + [((outer, 2 * shard, units), BF16)] * 3
            + [((outer, shard, q_width), BF16), ((outer, shard, qkv_width), BF16)]
            + [((2 * shard, units), BF16)] * 3
            + [((shard, q_width), BF16), ((shard, qkv_width), BF16)]
            + [((shard, units), BF16)] * 3
            + [((2 * tree_len, model), BF16)],
            [((2 * tree_len, model), BF16)]
            + [((4, rows, model), BF16)] * 2
            + [((3, rows, model), BF16)] * 4
            + [((tree_len, model), BF16), ((tree_len, q_width), BF16)]
            + [((tree_len, qkv_width), BF16), ((2, rows, model), BF16)]
            + [((rows, model), BF16)] * 2
            + [((outer, shard, q_width), BF16), ((outer, shard, qkv_width), BF16)] * 2,
            (
                wq_all,
                wo_all,
                gate_w,
                up_w,
                gain_rows,
                h1,
                qkv,
                probs,
                att,
                x1,
                h2,
                cot,
                dgate,
                dupper,
                hid,
                down_w,
                grad_down,
                x,
                cosine,
                sine,
            ),
        )[:10]

        def order_x(mine, theirs):
            theirs = theirs.astype(F32)
            low = jnp.where(upper_x, theirs, mine)
            high = jnp.where(upper_x, mine, theirs)
            return jnp.concatenate([low, high], 1)

        grad_gate = order_x(gate_mine, gate_theirs)
        grad_up = order_x(up_mine, up_theirs)
        grad_query = qkv_total[:, :q_width]
        grad_key = qkv_total[:, q_width : q_width + kv_width]
        grad_value = qkv_total[:, q_width + kv_width :]

        gain_sums = jnp.stack(
            [
                jnp.sum(w_query.astype(F32) * grad_query, 1)
                + jnp.sum(key_matrix.astype(F32) * grad_key, 1)
                + jnp.sum(value_matrix.astype(F32) * grad_value, 1),
                jnp.sum(w_gate.astype(F32) * grad_gate, 1)
                + jnp.sum(w_up.astype(F32) * grad_up, 1),
            ]
        )
        gain_sums = gain_sums + swap(gain_sums, 1)
        gain_sums = gain_sums + swap(gain_sums, 2)
        return (
            relative(out, zi),
            relative(grad_tok, zi),
            gain_sums[0] / attn_gain.astype(F32),
            grad_query,
            grad_key,
            grad_value,
            out_total.T,
            gain_sums[1] / mlp_gain.astype(F32),
            grad_gate,
            grad_up,
            order_x(down_mine, down_theirs).T,
        )

    return body


def solution(mesh):
    in_specs = (
        P(("dp", "tensor"), None),
        P("dp", None),
        P("dp"),
        P("dp", "tensor"),
        P("dp", "tensor"),
        P("dp", "tensor"),
        P("tensor", "dp"),
        P("dp"),
        P("dp", "tensor"),
        P("dp", "tensor"),
        P("tensor", "dp"),
        P(("dp", "tensor"), None),
    )
    out_specs = (
        P(("dp", "tensor"), None),
        P(("dp", "tensor"), None),
        P("dp"),
        P("dp", "tensor"),
        P("dp", "tensor"),
        P("dp", "tensor"),
        P("tensor", "dp"),
        P("dp"),
        P("dp", "tensor"),
        P("dp", "tensor"),
        P("tensor", "dp"),
    )
    body = make_body(mesh.shape["dp"], mesh.shape["tensor"])
    return jax.shard_map(body, mesh=mesh, in_specs=in_specs, out_specs=out_specs, check_vma=False)
```

```python
import functools

import jax
import jax.numpy as jnp
from jax import lax
from jax.experimental import pallas as pl
from jax.experimental.pallas import tpu as pltpu
from jax.sharding import PartitionSpec as P

HEAD_SIZE = 256
BLK = 128


EPS = 1e-06
THETA = 1000042.0
NEG = -1e30
HIGH = lax.Precision.HIGHEST
F32 = jnp.float32
BF16 = jnp.bfloat16
MESH = pl.DeviceIdType.MESH
VMEM_LIMIT = 60 * 2**20


def tree_tables(parent_row, tree_len, block_len):
    blocks = parent_row.shape[0]
    nodes = jnp.arange(blocks, dtype=jnp.int32)
    walks = jnp.eye(blocks, dtype=F32) + (parent_row[:, None] == nodes[None, :]).astype(F32)
    hops = 1
    while hops < blocks - 1:
        walks = jnp.dot(walks, walks, precision=HIGH)
        hops *= 2
    reach = (walks > 0.5).astype(F32)
    depth = jnp.sum(reach, axis=1) - 1.0
    row_reach = jnp.repeat(jnp.pad(reach, ((0, 0), (0, 128 - blocks))), block_len, axis=0)
    place = depth[:, None] * block_len + jnp.arange(block_len, dtype=F32)[None, :]
    return (row_reach.astype(BF16), place.reshape(tree_len))


def rope_tables(place, head_dim):
    half = head_dim // 2
    freq = THETA ** (-2.0 * jnp.arange(half, dtype=F32) / head_dim)
    angle = place[:, None] * freq[None, :]
    return (jnp.cos(angle), jnp.sin(angle))


def rotate(values, cosine, sine, sign):
    half = values.shape[-1] // 2
    first, second = values[..., :half], values[..., half:]
    return jnp.concatenate(
        [first * cosine - sign * second * sine, second * cosine + sign * first * sine], -1
    )


def normalize(values):
    inverse = lax.rsqrt(jnp.mean(values * values, axis=-1, keepdims=True) + EPS)
    return (values * inverse, inverse)


def norm_back(grad_normed, gain, values):
    scaled, inverse = normalize(values)
    grad_scaled = grad_normed * gain
    inner = jnp.mean(grad_scaled * scaled, axis=-1, keepdims=True)
    return inverse * (grad_scaled - scaled * inner)


def dot_nn(left, right):
    return jnp.dot(left, right, preferred_element_type=F32)


def dot_nt(left, right):
    return lax.dot_general(left, right, (((1,), (1,)), ((), ())), preferred_element_type=F32)


def dot_tn(left, right):
    return lax.dot_general(left, right, (((0,), (0,)), ((), ())), preferred_element_type=F32)


def flip(index, mask):
    out = index
    bit = 1
    while bit <= mask:
        if mask & bit:
            out = out + bit * (1 - 2 * (index // bit % 2))
        bit *= 2
    return out


class Links:
    def __init__(self, tp, send_sems, recv_sems):
        self.tp = tp
        self.di = lax.axis_index("dp")
        self.ti = lax.axis_index("tensor")
        self.send_sems, self.recv_sems = send_sems, recv_sems
        self.used = 0

    def partner(self, mask):
        return (flip(self.di, mask // self.tp), flip(self.ti, mask % self.tp))

    def greet(self, masks):
        barrier = pltpu.get_barrier_semaphore()
        for mask in masks:
            pl.semaphore_signal(barrier, inc=1, device_id=self.partner(mask), device_id_type=MESH)
        pl.semaphore_wait(barrier, len(masks))

    def remote(self, src, dst, mask):
        index = self.used
        self.used += 1
        return pltpu.make_async_remote_copy(
            src_ref=src,
            dst_ref=dst,
            send_sem=self.send_sems.at[index],
            recv_sem=self.recv_sems.at[index],
            device_id=self.partner(mask),
            device_id_type=MESH,
        )

    def send(self, src, dst, mask):
        copy = self.remote(src, dst, mask)
        copy.start()
        return copy


def line_middle(links):
    zi = links.di // 2
    return (zi == 1) | (zi == 2)


class Spread:
    def __init__(self, links, outer, own, block):
        self.links, self.outer = links, outer
        step = 2 * links.tp
        self.middle = line_middle(links)
        self.copies = {k: links.remote(own, block(k), k * step) for k in range(1, outer)}
        if outer == 4:
            self.onward = links.remote(block(2), block(3), step)

    def start(self, near=True):
        if self.outer != 4:
            for copy in self.copies.values():
                copy.start()
            return
        self.copies[2].start()
        if near:
            self.copies[1].start()
        else:

            @pl.when(jnp.logical_not(self.middle))
            def _():
                self.copies[1].start()

        @pl.when(self.middle)
        def _():
            self.copies[3].start()

    def start_near(self):
        if self.outer == 4:

            @pl.when(self.middle)
            def _():
                self.copies[1].start()

    def forward(self):
        self.copies[2].wait_recv()
        if self.outer != 4:
            return

        @pl.when(self.middle)
        def _():
            self.onward.start()

    def arrive(self, k):
        if k == 1 or (self.outer != 4 and k != 2):
            self.copies[k].wait_recv()
        elif k == 3:

            @pl.when(self.middle)
            def _():
                self.copies[3].wait_recv()

            @pl.when(jnp.logical_not(self.middle))
            def _():
                self.onward.wait_recv()

    def sent(self):
        if self.outer != 4:
            for copy in self.copies.values():
                copy.wait_send()
            return
        self.copies[1].wait_send()
        self.copies[2].wait_send()

        @pl.when(self.middle)
        def _():
            self.copies[3].wait_send()
            self.onward.wait_send()


class ReduceZ:
    def __init__(self, links, outer, block, held, staged):
        self.links, self.outer, self.block, self.held, self.staged = (
            links,
            outer,
            block,
            held,
            staged,
        )
        step = 2 * links.tp
        self.middle = line_middle(links)
        self.copies = {k: links.remote(block(k), held.at[k], k * step) for k in range(1, outer)}
        if outer == 4:
            self.inward = links.remote(block(3), held.at[0], step)
            self.summed = links.remote(staged, held.at[2], 2 * step)

    def on_ends(self, *actions):
        @pl.when(jnp.logical_not(self.middle))
        def _():
            for action in actions:
                action()

    def on_middle(self, *actions):
        @pl.when(self.middle)
        def _():
            for action in actions:
                action()

    def start(self, k):
        if self.outer != 4 or k == 1:
            self.copies[k].start()
        elif k == 3:
            self.on_ends(self.inward.start)
            self.on_middle(self.copies[3].start)
        elif k == 2:
            self.on_ends(self.copies[2].start)

    def start_all(self):
        for k in range(self.outer - 1, 0, -1):
            self.start(k)

    def pump(self):
        if self.outer != 4:
            return

        def add():
            rows, width = self.staged.shape
            spec = rows_spec(min(rows, 128), width)
            add_pipe(spec, rows, self.block(2), self.held.at[0], self.staged)

        self.on_middle(self.inward.wait_recv, add, self.summed.start)

    def arrive(self):
        if self.outer != 4:
            for copy in self.copies.values():
                copy.wait_recv()
            return
        self.copies[1].wait_recv()
        self.on_middle(self.copies[2].wait_recv, self.copies[3].wait_recv)
        self.on_ends(self.summed.wait_recv)

    def total(self, lo, rows, out):
        width = self.staged.shape[1]
        spec = rows_spec(min(rows, 128), width)

        def add(*refs):
            value = refs[0][...].astype(F32)
            for ref in refs[1:-1]:
                value = value + ref[...].astype(F32)
            refs[-1][...] = value.astype(refs[-1].dtype)

        def over(kept):
            parts = [self.block(0)] + [self.held.at[k] for k in kept]
            parts = [part.at[pl.ds(lo, rows)] for part in parts]
            grid = (rows // min(rows, 128),)
            pipe(add, grid, [spec] * len(parts), [spec], *parts, out)

        if self.outer != 4:
            over(range(1, self.outer))
            return
        self.on_middle(lambda: over([1, 2, 3]))
        self.on_ends(lambda: over([1, 2]))

    def sent(self):
        if self.outer != 4:
            for copy in self.copies.values():
                copy.wait_send()
            return
        self.copies[1].wait_send()
        self.on_middle(self.copies[3].wait_send, self.summed.wait_send)
        self.on_ends(self.copies[2].wait_send, self.inward.wait_send)


def gather_units(links, full, rows):
    tp = links.tp

    def block(m, lo=0, n=None):
        return full.at[pl.ds(m * rows + lo, rows if n is None else n)]

    half = rows // 2
    sent = []

    def send(m, mask, lo=0, n=None):
        copy = links.send(block(m, lo, n), block(m ^ mask, lo, n), mask)
        sent.append(copy)
        return copy

    x = send(0, tp)
    y = send(0, 2)
    c0 = send(0, 1)
    yield
    y.wait_recv()
    low = send(2, tp, half, half)
    c2 = send(2, 1)
    x.wait_recv()
    high = send(tp, 2, 0, half)
    c4 = send(tp, 1)
    yield
    low.wait_recv()
    high.wait_recv()
    c6 = send(tp + 2, 1)
    yield
    for copy in (c0, c2, c4, c6):
        copy.wait_recv()
    for copy in sent:
        copy.wait_send()
    yield


def run(stages):
    for _ in stages:
        pass


def pipe(body, grid, in_specs, out_specs, *refs):
    pltpu.emit_pipeline(body, grid=grid, in_specs=in_specs, out_specs=out_specs)(*refs)


def rows_spec(rows, width):
    return pl.BlockSpec((rows, width), lambda i: (i, 0))


def whole_spec(rows, width):
    return pl.BlockSpec((rows, width), lambda i: (0, 0))


def once_spec(rows, width):
    return pl.BlockSpec((rows, width), lambda i: (0, 0), pipeline_mode=pl.Buffered(1))


def add_refs(a_ref, b_ref, o_ref):
    o_ref[...] = (a_ref[...].astype(F32) + b_ref[...].astype(F32)).astype(o_ref.dtype)


def add_pipe(spec, rows, a, b, out):
    pipe(add_refs, (rows // spec.block_shape[0],), [spec, spec], [spec], a, b, out)


def copy_body(a_ref, o_ref):
    o_ref[...] = a_ref[...]


def keep(src, dst):
    rows, width = src.shape
    spec = rows_spec(min(rows, 128), width)
    pipe(copy_body, (rows // min(rows, 128),), [spec], [spec], src, dst)


def nt_body(a_ref, b_ref, o_ref):
    o_ref[...] = dot_nt(a_ref[...], b_ref[...]).astype(BF16)


def nn_body(a_ref, b_ref, o_ref):
    o_ref[...] = dot_nn(a_ref[...], b_ref[...]).astype(BF16)


def tn_body(a_ref, b_ref, o_ref):
    o_ref[...] = dot_tn(a_ref[...], b_ref[...]).astype(BF16)


def weight_grad(acts, grads, out, blocks, first=0, count=None):
    tokens, model = acts.shape
    width = grads.shape[1]
    size = model // blocks
    count = blocks if count is None else count
    pipe(
        tn_body,
        (count,),
        [pl.BlockSpec((tokens, size), lambda i: (0, first + i)), once_spec(tokens, width)],
        [pl.BlockSpec((size, width), lambda i: (first + i, 0))],
        acts,
        grads,
        out,
    )


class ScatterTensor:
    def __init__(self, links, part, got_c, got_y, far, rows):
        self.links, self.part, self.got_c, self.got_y, self.far = links, part, got_c, got_y, far
        self.rows = rows
        self.model = part.shape[1]
        self.spec = rows_spec(rows // 2, self.model)

    def block(self, mask):
        rows = self.rows
        return self.part.at[
            pl.ds(pl.multiple_of(flip(self.links.ti, mask) * rows, rows), rows)
        ]

    def start(self):
        self.copies = [
            self.links.send(self.block(3), self.got_c.at[1], 1),
            self.links.send(self.block(1), self.got_c.at[0], 1),
        ]

    def across(self):
        self.copies[0].wait_recv()
        add_pipe(self.spec, self.rows, self.block(2), self.got_c.at[1], self.far)
        self.copies.append(self.links.send(self.far, self.got_y, 2))

    def arrive(self):
        self.copies[1].wait_recv()
        self.copies[2].wait_recv()
        return [self.block(0), self.got_c.at[0], self.got_y]

    def sent(self):
        for copy in self.copies:
            copy.wait_send()


class ScatterUnits:
    def __init__(self, links, part, got_c, near, got, rows):
        self.links, self.part, self.got_c, self.near, self.got = links, part, got_c, near, got
        self.rows, self.model = rows, part.shape[1]
        self.sends = []

    def send(self, src, dst, mask):
        copy = self.links.send(src, dst, mask)
        self.sends.append(copy)
        return copy

    def block(self, m):
        return self.part.at[pl.ds(m * self.rows, self.rows)]

    def start(self):
        self.from_c = [self.send(self.block(2 * i + 1), self.got_c.at[i], 1) for i in range(4)]

    def add(self, m, slot, lo, n):
        rows = pl.ds(lo, n)
        add_pipe(
            rows_spec(n, self.model),
            n,
            self.block(m).at[rows],
            self.got_c.at[m // 2].at[rows],
            self.near.at[slot].at[rows],
        )

    def across(self):
        tp, rows, half = self.links.tp, self.rows, self.rows // 2
        low, high = pl.ds(0, half), pl.ds(half, half)
        near, got = self.near, self.got
        for copy in self.from_c:
            copy.wait_recv()
        self.add(6, 2, 0, half)
        self.top = self.send(near.at[2].at[low], got.at[2].at[low], tp)
        self.add(6, 2, half, half)
        self.bottom = self.send(near.at[2].at[high], got.at[2].at[high], 2)
        self.add(4, 0, 0, half)
        self.x_low = self.send(near.at[0].at[low], got.at[0].at[low], tp)
        self.add(2, 1, half, half)
        self.y_high = self.send(near.at[1].at[high], got.at[1].at[high], 2)

    def finish(self):
        tp, half = self.links.tp, self.rows // 2
        low, high = pl.ds(0, half), pl.ds(half, half)
        near, got = self.near, self.got

        def add3(m, slot, rows):
            def body(a_ref, b_ref, c_ref, o_ref):
                o_ref[...] = (
                    a_ref[...].astype(F32) + b_ref[...].astype(F32) + c_ref[...].astype(F32)
                ).astype(BF16)

            spec = rows_spec(half, self.model)
            pipe(
                body,
                (1,),
                [spec] * 3,
                [spec],
                self.block(m).at[rows],
                self.got_c.at[m // 2].at[rows],
                got.at[2].at[rows],
                near.at[slot].at[rows],
            )

        self.top.wait_recv()
        add3(2, 1, low)
        self.y_low = self.send(near.at[1].at[low], got.at[1].at[low], 2)
        self.bottom.wait_recv()
        add3(4, 0, high)
        self.x_high = self.send(near.at[0].at[high], got.at[0].at[high], tp)

    def arrive(self):
        for copy in (self.x_low, self.x_high, self.y_low, self.y_high):
            copy.wait_recv()
        return [self.block(0), self.got_c.at[0], self.got.at[0], self.got.at[1]]

    def sent(self):
        for copy in self.sends:
            copy.wait_send()


def sum_refs(refs):
    value = refs[0][...].astype(F32)
    for ref in refs[1:]:
        value = value + ref[...].astype(F32)
    return value


class GatherTree:
    def __init__(self, links, full, rows):
        self.links, self.full, self.rows = links, full, rows

    def block(self, mask):
        rows = self.rows
        return self.full.at[
            pl.ds(pl.multiple_of(flip(self.links.ti, mask) * rows, rows), rows)
        ]

    def start(self):
        self.y = self.links.send(self.block(0), self.block(0), 2)
        self.c = self.links.send(self.block(0), self.block(0), 1)

    def across(self):
        self.y.wait_recv()
        self.yc = self.links.send(self.block(2), self.block(2), 1)

    def arrive(self):
        self.c.wait_recv()
        self.yc.wait_recv()

    def sent(self):
        for copy in (self.y, self.c, self.yc):
            copy.wait_send()


def greet_all(links, outer):
    step = 2 * links.tp
    links.greet([1, 2, links.tp] + [k * step for k in range(1, outer)])


def forward_kernel(
    outer,
    tp,
    wq,
    wo,
    wg,
    wu,
    wd,
    gn,
    x,
    xh,
    cot,
    cosine,
    sine,
    row_reach,
    wq_all,
    wo_all,
    gate_w,
    up_w,
    gain_rows,
    h1,
    qkv,
    probs,
    att,
    x1,
    h2,
    cot_all,
    dgate,
    dupper,
    hid,
    down_w,
    grad_down,
    gn_all,
    part,
    got_c,
    got_y,
    far,
    dhid,
    gate,
    upper,
    send_sems,
    recv_sems,
):
    links = Links(tp, send_sems, recv_sems)
    shard, qkv_width = wq.shape
    units = gate_w.shape[1]
    rows, model = xh.shape
    tree_len = rows * tp
    q_width = att.shape[1]
    kv_width = (qkv_width - q_width) // 2
    head = HEAD_SIZE
    xi = links.di % 2
    greet_all(links, outer)

    def shard_block(full, k):
        return full.at[pl.ds(pl.multiple_of((2 * k + xi) * shard, shard), shard)]

    mine = pl.ds(pl.multiple_of(xi * units, units), units)
    peers = pl.ds(pl.multiple_of((1 - xi) * units, units), units)
    place = pl.ds(pl.multiple_of(xi * shard, shard), shard)

    def send_pair(w, full):
        return links.send(w.at[:, peers], full.at[place], tp)

    def mlp_spread(full):
        return Spread(
            links,
            outer,
            full.at[pl.ds(0, 2 * shard)],
            lambda k: full.at[pl.ds(k * 2 * shard, 2 * shard)],
        )

    gains = Spread(links, outer, gn, lambda k: shard_block(gn_all, k))
    attn = Spread(links, outer, wq, lambda k: shard_block(wq_all, k))
    attn_out = Spread(links, outer, wo, lambda k: shard_block(wo_all, k))
    gains.start()
    across_gn = [links.send(gn, shard_block(gn_all, 0), tp)]
    attn.start()
    across = [links.send(wq, shard_block(wq_all, 0), tp)]
    attn_out.start()
    pair = [send_pair(wg, gate_w)]
    across_out = [links.send(wo, shard_block(wo_all, 0), tp)]

    def cross(full, k, copies):
        copies.append(links.send(shard_block(full, k), shard_block(full, k), tp))

    keep(gn, shard_block(gn_all, 0))
    keep(wg.at[:, mine], gate_w.at[place])

    gains.forward()
    for k in range(1, outer):
        gains.arrive(k)
        across_gn.append(links.send(shard_block(gn_all, k), shard_block(gn_all, k), tp))
    keep(wq, shard_block(wq_all, 0))
    keep(wo, shard_block(wo_all, 0))
    for copy in across_gn:
        copy.wait_recv()

    def gain_rows_of(g_ref, o_ref):
        lane = lax.broadcasted_iota(jnp.int32, (8, 128), 1)
        row = lax.broadcasted_iota(jnp.int32, (8, 128), 0)
        pick = jnp.where((row < 2) & (lane == row * 64), 1.0, 0.0).astype(BF16)
        o_ref[...] = dot_nt(pick, g_ref[...])

    pipe(gain_rows_of, (1,), [whole_spec(model, 128)], [whole_spec(8, model)], gn_all, gain_rows)
    spec = rows_spec(rows // 2, model)
    gain_spec = whole_spec(8, model)

    def scale_tokens(x_ref, g_ref, o_ref):
        o_ref[...] = (x_ref[...] * g_ref[0:1]).astype(BF16)

    tree = GatherTree(links, h1, rows)
    pipe(scale_tokens, (2,), [spec, gain_spec], [spec], xh, gain_rows, tree.block(0))
    tree.start()
    keep(wu.at[:, mine], up_w.at[place])
    keep(wd.at[:, mine], down_w.at[place])
    keep(cot, cot_all.at[pl.ds(0, rows)])

    spreads = [mlp_spread(full) for full in (gate_w, up_w, down_w)]
    attn.forward()
    cross(wq_all, 2, across)
    for k in range(1, outer):
        if k != 2:
            attn.arrive(k)
            cross(wq_all, k, across)
    tree.across()
    attn_out.forward()
    cross(wo_all, 2, across_out)
    pair[0].wait_recv()
    spreads[0].start()
    for k in range(1, outer):
        if k != 2:
            attn_out.arrive(k)
            cross(wo_all, k, across_out)
    pair.append(send_pair(wu, up_w))
    later = gather_units(links, cot_all, rows)
    next(later)
    pair.append(send_pair(wd, down_w))
    tree.arrive()
    for copy in across:
        copy.wait_recv()

    def project(x_ref, w_ref, cos_ref, sin_ref, out_ref):
        raw = dot_nn(x_ref[...], w_ref[...])
        for slot in range((q_width + kv_width) // head):
            cols = slice(slot * head, (slot + 1) * head)
            out_ref[:, cols] = rotate(raw[:, cols], cos_ref[...], sin_ref[...], 1.0).astype(BF16)
        out_ref[:, q_width + kv_width :] = raw[:, q_width + kv_width :].astype(BF16)

    pipe(
        project,
        (tp,),
        [
            rows_spec(rows, model),
            whole_spec(model, qkv_width),
            rows_spec(rows, head // 2),
            rows_spec(rows, head // 2),
        ],
        [rows_spec(rows, qkv_width)],
        h1,
        wq_all,
        cosine,
        sine,
        qkv,
    )
    pair[1].wait_recv()
    spreads[1].start(near=False)

    group = q_width // kv_width

    def attend(q_ref, k_ref, v_ref, r_ref, p_ref, o_ref):
        segment = lax.broadcasted_iota(jnp.int32, (128, tree_len), 0)
        key_row = lax.broadcasted_iota(jnp.int32, (128, tree_len), 1)
        member = jnp.where(key_row // BLK == segment, 1.0, 0.0).astype(BF16)
        seen = dot_nn(r_ref[...], member)
        query = lax.broadcasted_iota(jnp.int32, (rows, tree_len), 0) + pl.program_id(0) * rows
        key = lax.broadcasted_iota(jnp.int32, (rows, tree_len), 1)
        scores = dot_nt(q_ref[...], k_ref[...]) * (head**-0.5)
        scores = jnp.where((seen > 0.5) & (key <= query), scores, NEG)
        weights = jnp.exp(scores - jnp.max(scores, axis=-1, keepdims=True))
        weights = (weights / jnp.sum(weights, axis=-1, keepdims=True)).astype(BF16)
        p_ref[0] = weights
        o_ref[...] = dot_nn(weights, v_ref[...]).astype(BF16)

    k_at, v_at = q_width // head, (q_width + kv_width) // head
    pipe(
        attend,
        (tp, q_width // head),
        [
            pl.BlockSpec((rows, head), lambda i, h: (i, h)),
            pl.BlockSpec((tree_len, head), lambda i, h: (0, k_at + h // group)),
            pl.BlockSpec((tree_len, head), lambda i, h: (0, v_at + h // group)),
            pl.BlockSpec((rows, 128), lambda i, h: (i, 0)),
        ],
        [
            pl.BlockSpec((1, rows, tree_len), lambda i, h: (h, i, 0)),
            pl.BlockSpec((rows, head), lambda i, h: (i, h)),
        ],
        qkv,
        qkv,
        qkv,
        row_reach,
        probs,
        att,
    )
    for copy in across_out:
        copy.wait_recv()
    pipe(
        nt_body,
        (tp,),
        [rows_spec(rows, q_width), whole_spec(model, q_width)],
        [rows_spec(rows, model)],
        att,
        wo_all,
        part,
    )
    mixed = ScatterTensor(links, part, got_c, got_y, far, rows)
    mixed.start()
    spreads[0].forward()
    spreads[1].start_near()
    mixed.across()
    next(later)
    pair[2].wait_recv()
    spreads[2].start(near=False)
    parts = mixed.arrive()

    def residual(x_ref, a_ref, b_ref, c_ref, g_ref, x1_ref, h_ref):
        total = x_ref[...] + sum_refs((a_ref, b_ref, c_ref))
        x1_ref[...] = total
        h_ref[...] = (normalize(total)[0] * g_ref[1:2]).astype(BF16)

    pipe(
        residual,
        (2,),
        [spec] * 4 + [gain_spec],
        [spec] * 2,
        x,
        *parts,
        gain_rows,
        x1,
        h2.at[pl.ds(0, rows)],
    )
    stages = gather_units(links, h2, rows)
    next(stages)
    next(later)
    next(stages)
    spreads[1].forward()
    spreads[2].start_near()
    next(stages)
    next(stages)
    run(later)

    for spread in spreads[:2]:
        for k in range(1, outer):
            spread.arrive(k)

    def expand(x_ref, g_ref, u_ref, a_ref, b_ref, h_ref):
        @pl.when(pl.program_id(0) == tp)
        def _():
            spreads[2].forward()

        g = dot_nn(x_ref[...], g_ref[...])
        u = dot_nn(x_ref[...], u_ref[...])
        sigma = jax.nn.sigmoid(g)
        swish = g * sigma
        a_ref[...] = (u * sigma * (1.0 + g * (1.0 - sigma))).astype(BF16)
        b_ref[...] = swish.astype(BF16)
        h_ref[...] = (swish * u).astype(BF16)

    pipe(
        expand,
        (2 * tp,),
        [rows_spec(rows, model), once_spec(model, units), once_spec(model, units)],
        [rows_spec(rows, units)] * 3,
        h2,
        gate_w,
        up_w,
        gate,
        upper,
        hid,
    )
    weight_grad(cot_all, hid, grad_down, 4)

    known = (outer - 1) * 2 * shard
    unit_spec = rows_spec(rows, units)

    def contract_known(c_ref, d_ref):
        at = pl.ds(pl.multiple_of(pl.program_id(0) * rows, rows), rows)
        dhid[at] = dot_nn(c_ref[...], d_ref[...])

    def contract_last(c_ref, d_ref, a_ref, b_ref, dg_ref, du_ref):
        at = pl.ds(pl.multiple_of(pl.program_id(0) * rows, rows), rows)
        value = dhid[at] + dot_nn(c_ref[...], d_ref[...])
        dg_ref[...] = (value * a_ref[...].astype(F32)).astype(BF16)
        du_ref[...] = (value * b_ref[...].astype(F32)).astype(BF16)

    for k in range(1, outer - 1):
        spreads[2].arrive(k)
    pipe(
        contract_known,
        (2 * tp,),
        [rows_spec(rows, known), once_spec(known, units)],
        [],
        cot_all.at[:, pl.ds(0, known)],
        down_w.at[pl.ds(0, known)],
    )
    spreads[2].arrive(outer - 1)
    pipe(
        contract_last,
        (2 * tp,),
        [rows_spec(rows, model - known), once_spec(model - known, units), unit_spec, unit_spec],
        [unit_spec] * 2,
        cot_all.at[:, pl.ds(known, model - known)],
        down_w.at[pl.ds(known, model - known)],
        gate,
        upper,
        dgate,
        dupper,
    )
    for spread in [gains, attn, attn_out] + spreads:
        spread.sent()
    for copy in across_gn + across + across_out + pair:
        copy.wait_send()
    tree.sent()
    mixed.sent()


def backward_kernel(
    outer,
    tp,
    wq_all,
    wo_all,
    gate_w,
    up_w,
    gain_rows,
    h1,
    qkv,
    probs,
    att,
    x1,
    h2,
    cot,
    dgate,
    dupper,
    hid,
    down_w,
    grad_down,
    x,
    cosine,
    sine,
    out,
    grad_tok,
    down_mine,
    down_theirs,
    gate_mine,
    gate_theirs,
    up_mine,
    up_theirs,
    out_total,
    qkv_total,
    dx1,
    dscores,
    grad_gate,
    grad_up,
    grad_out,
    grad_qkv,
    down_held,
    gate_held,
    up_held,
    out_held,
    qkv_held,
    down_staged,
    gate_staged,
    up_staged,
    out_staged,
    qkv_staged,
    down_give,
    gate_give,
    up_give,
    y_part,
    e_part,
    e_got_c,
    y_got_c,
    e_near,
    y_near,
    e_got,
    y_got,
    dx1_low,
    dout,
    dqkv,
    f_got_c,
    f_got_y,
    f_far,
    out_pair,
    qkv_pair,
    out_sum,
    qkv_sum,
    send_sems,
    recv_sems,
):
    links = Links(tp, send_sems, recv_sems)
    rows, model = x.shape
    tree_len = rows * tp
    units = gate_w.shape[1]
    q_width = att.shape[1]
    qkv_width = qkv.shape[1]
    kv_width = (qkv_width - q_width) // 2
    head = HEAD_SIZE
    group = q_width // kv_width
    shard = model // (2 * outer)
    xi = links.di % 2
    half = pl.multiple_of(xi * shard, shard)
    other = pl.multiple_of((1 - xi) * shard, shard)
    spec = rows_spec(rows // 2, model)
    gain_spec = whole_spec(8, model)
    greet_all(links, outer)

    def mlp_reduce(grad, held, staged):
        return ReduceZ(
            links, outer, lambda k: grad.at[pl.ds(k * 2 * shard, 2 * shard)], held, staged
        )

    def trade(reduce, mine, give, theirs):
        reduce.arrive()
        reduce.total(other, shard, give)
        copy = links.send(give, theirs, tp)
        reduce.total(half, shard, mine)
        return copy

    red_down = mlp_reduce(grad_down, down_held, down_staged)
    red_gate = mlp_reduce(grad_gate, gate_held, gate_staged)
    red_up = mlp_reduce(grad_up, up_held, up_staged)
    red_down.start_all()

    y_sum = ScatterUnits(links, y_part, y_got_c, y_near, y_got, rows)

    def every_other(first, block_rows, width):
        return pl.BlockSpec((block_rows, width), lambda i: (2 * i + first, 0))

    def back(dg_ref, du_ref, g_ref, u_ref, o_ref):
        o_ref[...] = (dot_nt(dg_ref[...], g_ref[...]) + dot_nt(du_ref[...], u_ref[...])).astype(
            BF16
        )

    def back_blocks(first):
        pipe(
            back,
            (tp,),
            [every_other(first, rows, units)] * 2 + [once_spec(model, units)] * 2,
            [every_other(first, rows, model)],
            dgate,
            dupper,
            gate_w,
            up_w,
            e_part,
        )

    e_sum = ScatterUnits(links, e_part, e_got_c, e_near, e_got, rows)
    back_blocks(1)
    e_sum.start()
    red_down.pump()
    back_blocks(0)
    e_sum.across()
    weight_grad(h2, dgate, grad_gate, 4)
    red_gate.start_all()
    e_sum.finish()
    weight_grad(h2, dupper, grad_up, 4)
    red_up.start_all()
    trades = [trade(red_down, down_mine, down_give, down_theirs)]

    tree = GatherTree(links, dx1_low, rows)

    def through_norm(c_ref, x_ref, g_ref, *refs):
        value = c_ref[...].astype(F32) + norm_back(sum_refs(refs[:-2]), g_ref[1:2], x_ref[...])
        refs[-2][...] = value
        refs[-1][...] = value.astype(BF16)

    parts = e_sum.arrive()
    pipe(
        through_norm,
        (2,),
        [spec, spec, gain_spec] + [spec] * len(parts),
        [spec] * 2,
        cot,
        x1,
        gain_rows,
        *parts,
        dx1,
        tree.block(0),
    )
    tree.start()
    red_gate.pump()
    pipe(
        nt_body,
        (2 * tp,),
        [rows_spec(rows, units), once_spec(model, units)],
        [rows_spec(rows, model)],
        hid,
        down_w,
        y_part,
    )
    tree.across()
    y_sum.start()
    tree.arrive()

    pipe(
        nn_body,
        (tp,),
        [rows_spec(rows, model), whole_spec(model, q_width)],
        [rows_spec(rows, q_width)],
        dx1_low,
        wo_all,
        dout,
    )

    def pair_block(full, k, at):
        return full.at[pl.ds(pl.multiple_of(k * 2 * shard + at, shard), shard)]

    def pair_send(grad, held, k):
        return links.send(pair_block(grad, k, other), held.at[k], tp)

    red_out = ReduceZ(links, outer, lambda k: out_sum.at[k], out_held, out_staged)
    red_qkv = ReduceZ(links, outer, lambda k: qkv_sum.at[k], qkv_held, qkv_staged)
    weight_grad(dx1_low, att, grad_out, 4)
    order = list(range(outer - 1, -1, -1))
    out_across = {k: pair_send(grad_out, out_pair, k) for k in order}
    y_sum.across()

    def score_grads(do_ref, k_ref, v_ref, p_ref, cos_ref, sin_ref, ds_ref, dq_ref):
        p = p_ref[0].astype(F32)
        dp = dot_nt(do_ref[...], v_ref[...])
        inner = jnp.sum(p * dp, axis=-1, keepdims=True)
        ds = (p * (dp - inner) * (head**-0.5)).astype(BF16)
        ds_ref[0] = ds
        dq_ref[...] = rotate(dot_nn(ds, k_ref[...]), cos_ref[...], sin_ref[...], -1.0).astype(BF16)

    k_at, v_at = q_width // head, (q_width + kv_width) // head
    pipe(
        score_grads,
        (tp, q_width // head),
        [
            pl.BlockSpec((rows, head), lambda i, h: (i, h)),
            pl.BlockSpec((tree_len, head), lambda i, h: (0, k_at + h // group)),
            pl.BlockSpec((tree_len, head), lambda i, h: (0, v_at + h // group)),
            pl.BlockSpec((1, rows, tree_len), lambda i, h: (h, i, 0)),
            pl.BlockSpec((rows, head // 2), lambda i, h: (i, 0)),
            pl.BlockSpec((rows, head // 2), lambda i, h: (i, 0)),
        ],
        [
            pl.BlockSpec((1, rows, tree_len), lambda i, h: (h, i, 0)),
            pl.BlockSpec((rows, head), lambda i, h: (i, h)),
        ],
        dout,
        qkv,
        qkv,
        probs,
        cosine,
        sine,
        dscores,
        dqkv,
    )

    def key_grads(ds_ref, p_ref, q_ref, do_ref, cos_ref, sin_ref, dkv_ref):
        dk = jnp.zeros((rows, head), F32)
        dv = jnp.zeros((rows, head), F32)
        for h in range(group):
            cols = slice(h * head, (h + 1) * head)
            dk = dk + dot_tn(ds_ref[h], q_ref[:, cols])
            dv = dv + dot_tn(p_ref[h], do_ref[:, cols])
        dkv_ref[:, :head] = rotate(dk, cos_ref[...], sin_ref[...], -1.0).astype(BF16)
        dkv_ref[:, head:] = dv.astype(BF16)

    by_key = pl.BlockSpec((group, tree_len, rows), lambda i: (0, 0, i))
    pipe(
        key_grads,
        (tp,),
        [by_key, by_key]
        + [whole_spec(tree_len, q_width)] * 2
        + [rows_spec(rows, head // 2)] * 2,
        [rows_spec(rows, 2 * kv_width)],
        dscores,
        probs,
        qkv.at[:, pl.ds(0, q_width)],
        dout,
        cosine,
        sine,
        dqkv.at[:, pl.ds(q_width, 2 * kv_width)],
    )

    y_sum.finish()

    def pair_add(grad, held, total, k):
        add_pipe(
            rows_spec(min(shard, 128), grad.shape[1]),
            shard,
            pair_block(grad, k, half),
            held.at[k],
            total.at[k],
        )

    qkv_across = {}
    weight_grad(h1, dqkv, grad_qkv, 4)
    for k in order:
        qkv_across[k] = pair_send(grad_qkv, qkv_pair, k)
    e_sum.sent()
    f_part = e_part.at[pl.ds(0, tree_len)]
    pipe(
        nt_body,
        (tp,),
        [rows_spec(rows, qkv_width), whole_spec(model, qkv_width)],
        [rows_spec(rows, model)],
        dqkv,
        wq_all,
        f_part,
    )
    f_sum = ScatterTensor(links, f_part, f_got_c, f_got_y, f_far, rows)
    f_sum.start()
    f_sum.across()
    red_up.pump()
    for k in order:
        out_across[k].wait_recv()
        pair_add(grad_out, out_pair, out_sum, k)
        if k:
            red_out.start(k)
    trades.append(trade(red_gate, gate_mine, gate_give, gate_theirs))

    def finish_output(x_ref, *refs):
        refs[-1][...] = (x_ref[...] + sum_refs(refs[:-1])).astype(BF16)

    parts = y_sum.arrive()
    pipe(finish_output, (2,), [spec] * (1 + len(parts)), [spec], x1, *parts, out)

    for k in order:
        qkv_across[k].wait_recv()
        pair_add(grad_qkv, qkv_pair, qkv_sum, k)
        if k:
            red_qkv.start(k)

    def finish_tokens(d_ref, x_ref, g_ref, *refs):
        refs[-1][...] = (
            d_ref[...] + norm_back(sum_refs(refs[:-1]), g_ref[0:1], x_ref[...])
        ).astype(BF16)

    parts = f_sum.arrive()
    pipe(
        finish_tokens,
        (2,),
        [spec, spec, gain_spec] + [spec] * len(parts),
        [spec],
        dx1,
        x,
        gain_rows,
        *parts,
        grad_tok,
    )
    trades.append(trade(red_up, up_mine, up_give, up_theirs))
    red_out.pump()
    red_qkv.pump()
    red_out.arrive()
    red_out.total(0, shard, out_total)
    red_qkv.arrive()
    red_qkv.total(0, shard, qkv_total)
    for copy in trades:
        copy.wait()
    for copy in list(out_across.values()) + list(qkv_across.values()):
        copy.wait_send()
    for item in (red_down, red_gate, red_up, red_out, red_qkv, y_sum, f_sum, tree):
        item.sent()


def call(kernel, name, collective, count, shapes, scratch, operands):
    anywhere = pl.BlockSpec(memory_space=pl.ANY)
    return pl.pallas_call(
        kernel,
        out_shape=[jax.ShapeDtypeStruct(shape, dtype) for shape, dtype in shapes],
        in_specs=[anywhere] * len(operands),
        out_specs=[anywhere] * len(shapes),
        scratch_shapes=[pltpu.VMEM(shape, dtype) for shape, dtype in scratch]
        + [
            pltpu.SemaphoreType.DMA((count,)),
            pltpu.SemaphoreType.DMA((count,)),
        ],
        compiler_params=pltpu.CompilerParams(
            collective_id=collective, has_side_effects=True, vmem_limit_bytes=VMEM_LIMIT
        ),
        name=name,
    )(*operands)


def make_body(dp, tp):
    outer = dp // 2
    assert tp == 4 and dp == 2 * outer and outer >= 4 and outer & (outer - 1) == 0

    def swap(value, mask):
        return lax.ppermute(value, ("dp", "tensor"), [(i, i ^ mask) for i in range(dp * tp)])

    def relative(value, zi):
        width = value.shape[-1] // outer
        step = 1
        while step < outer:
            blocks = [value[..., i * width : (i + 1) * width] for i in range(outer)]
            swapped = jnp.concatenate([blocks[i ^ step] for i in range(outer)], -1)
            value = jnp.where((zi // step) % 2 == 1, swapped, value)
            step *= 2
        return value

    def body(
        tokens,
        parents,
        attn_gain,
        w_query,
        key_matrix,
        value_matrix,
        w_out,
        mlp_gain,
        w_gate,
        w_up,
        w_down,
        cotangent,
    ):
        di = lax.axis_index("dp")
        zi = di // 2
        upper_x = di % 2 == 1
        rows, model = tokens.shape
        tree_len = rows * tp
        q_width = w_query.shape[1]
        kv_width = key_matrix.shape[1]
        qkv_width = q_width + 2 * kv_width
        heads = q_width // HEAD_SIZE
        assert kv_width == HEAD_SIZE
        shard = w_query.shape[0]
        units = w_gate.shape[1] // 2

        wq = jnp.concatenate([w_query, key_matrix, value_matrix], 1)
        gn = jnp.concatenate(
            [
                jnp.broadcast_to(attn_gain[:, None], (shard, 64)),
                jnp.broadcast_to(mlp_gain[:, None], (shard, 64)),
            ],
            1,
        )
        row_reach, place = tree_tables(parents[0], tree_len, BLK)
        cosine, sine = rope_tables(place, HEAD_SIZE)
        x = relative(tokens, zi).astype(F32)
        xh = normalize(x)[0]
        cot = relative(cotangent, zi)
        (
            wq_all,
            wo_all,
            gate_w,
            up_w,
            gain_rows,
            h1,
            qkv,
            probs,
            att,
            x1,
            h2,
            cot_all,
            dgate,
            dupper,
            hid,
            down_w,
            grad_down,
        ) = call(
            functools.partial(forward_kernel, outer, tp),
            "layer_forward",
            0,
            60 + 9 * outer,
            [
                ((model, qkv_width), BF16),
                ((model, q_width), BF16),
                ((model, units), BF16),
                ((model, units), BF16),
                ((8, model), F32),
                ((tree_len, model), BF16),
                ((tree_len, qkv_width), BF16),
                ((heads, tree_len, tree_len), BF16),
                ((tree_len, q_width), BF16),
                ((rows, model), F32),
                ((2 * tree_len, model), BF16),
                ((2 * tree_len, model), BF16),
                ((2 * tree_len, units), BF16),
                ((2 * tree_len, units), BF16),
                ((2 * tree_len, units), BF16),
                ((model, units), BF16),
                ((model, units), BF16),
                ((model, 128), BF16),
            ],
            [
                ((tree_len, model), BF16),
                ((2, rows, model), BF16),
                ((rows, model), BF16),
                ((rows, model), BF16),
                ((2 * tree_len, units), F32),
                ((2 * tree_len, units), BF16),
                ((2 * tree_len, units), BF16),
            ],
            (wq, w_out.T, w_gate, w_up, w_down.T, gn, x, xh, cot, cosine, sine, row_reach),
        )[:17]

        (
            out,
            grad_tok,
            down_mine,
            down_theirs,
            gate_mine,
            gate_theirs,
            up_mine,
            up_theirs,
            out_total,
            qkv_total,
        ) = call(
            functools.partial(backward_kernel, outer, tp),
            "layer_backward",
            1,
            60 + 10 * outer,
            [((rows, model), BF16)] * 2
            + [((shard, units), F32), ((shard, units), BF16)] * 3
            + [((shard, q_width), F32), ((shard, qkv_width), F32)]
            + [((rows, model), F32), ((heads, tree_len, tree_len), BF16)]
            + [((model, units), BF16)] * 2
            + [((model, q_width), BF16), ((model, qkv_width), BF16)]
            + [((outer, 2 * shard, units), BF16)] * 3
            + [((outer, shard, q_width), BF16), ((outer, shard, qkv_width), BF16)]
            + [((2 * shard, units), BF16)] * 3
            + [((shard, q_width), BF16), ((shard, qkv_width), BF16)]
            + [((shard, units), BF16)] * 3
            + [((2 * tree_len, model), BF16)],
            [((2 * tree_len, model), BF16)]
            + [((4, rows, model), BF16)] * 2
            + [((3, rows, model), BF16)] * 4
            + [((tree_len, model), BF16), ((tree_len, q_width), BF16)]
            + [((tree_len, qkv_width), BF16), ((2, rows, model), BF16)]
            + [((rows, model), BF16)] * 2
            + [((outer, shard, q_width), BF16), ((outer, shard, qkv_width), BF16)] * 2,
            (
                wq_all,
                wo_all,
                gate_w,
                up_w,
                gain_rows,
                h1,
                qkv,
                probs,
                att,
                x1,
                h2,
                cot,
                dgate,
                dupper,
                hid,
                down_w,
                grad_down,
                x,
                cosine,
                sine,
            ),
        )[:10]

        def order_x(mine, theirs):
            theirs = theirs.astype(F32)
            low = jnp.where(upper_x, theirs, mine)
            high = jnp.where(upper_x, mine, theirs)
            return jnp.concatenate([low, high], 1)

        grad_gate = order_x(gate_mine, gate_theirs)
        grad_up = order_x(up_mine, up_theirs)
        grad_query = qkv_total[:, :q_width]
        grad_key = qkv_total[:, q_width : q_width + kv_width]
        grad_value = qkv_total[:, q_width + kv_width :]

        gain_sums = jnp.stack(
            [
                jnp.sum(w_query.astype(F32) * grad_query, 1)
                + jnp.sum(key_matrix.astype(F32) * grad_key, 1)
                + jnp.sum(value_matrix.astype(F32) * grad_value, 1),
                jnp.sum(w_gate.astype(F32) * grad_gate, 1)
                + jnp.sum(w_up.astype(F32) * grad_up, 1),
            ]
        )
        gain_sums = gain_sums + swap(gain_sums, 1)
        gain_sums = gain_sums + swap(gain_sums, 2)
        return (
            relative(out, zi),
            relative(grad_tok, zi),
            gain_sums[0] / attn_gain.astype(F32),
            grad_query,
            grad_key,
            grad_value,
            out_total.T,
            gain_sums[1] / mlp_gain.astype(F32),
            grad_gate,
            grad_up,
            order_x(down_mine, down_theirs).T,
        )

    return body


def solution(mesh):
    in_specs = (
        P(("dp", "tensor"), None),
        P("dp", None),
        P("dp"),
        P("dp", "tensor"),
        P("dp", "tensor"),
        P("dp", "tensor"),
        P("tensor", "dp"),
        P("dp"),
        P("dp", "tensor"),
        P("dp", "tensor"),
        P("tensor", "dp"),
        P(("dp", "tensor"), None),
    )
    out_specs = (
        P(("dp", "tensor"), None),
        P(("dp", "tensor"), None),
        P("dp"),
        P("dp", "tensor"),
        P("dp", "tensor"),
        P("dp", "tensor"),
        P("tensor", "dp"),
        P("dp"),
        P("dp", "tensor"),
        P("dp", "tensor"),
        P("tensor", "dp"),
    )
    body = make_body(mesh.shape["dp"], mesh.shape["tensor"])
    return jax.shard_map(body, mesh=mesh, in_specs=in_specs, out_specs=out_specs, check_vma=False)
```

```python
import functools

import jax
import jax.numpy as jnp
from jax import lax
from jax.experimental import pallas as pl
from jax.experimental.pallas import tpu as pltpu
from jax.sharding import PartitionSpec as P

HEAD_SIZE = 256
BLK = 128


EPS = 1e-06
THETA = 1000042.0
NEG = -1e30
HIGH = lax.Precision.HIGHEST
F32 = jnp.float32
BF16 = jnp.bfloat16
MESH = pl.DeviceIdType.MESH
VMEM_LIMIT = 60 * 2**20


def tree_tables(parent_row, tree_len, block_len):
    blocks = parent_row.shape[0]
    nodes = jnp.arange(blocks, dtype=jnp.int32)
    walks = jnp.eye(blocks, dtype=F32) + (parent_row[:, None] == nodes[None, :]).astype(F32)
    hops = 1
    while hops < blocks - 1:
        walks = jnp.dot(walks, walks, precision=HIGH)
        hops *= 2
    reach = (walks > 0.5).astype(F32)
    depth = jnp.sum(reach, axis=1) - 1.0
    row_reach = jnp.repeat(jnp.pad(reach, ((0, 0), (0, 128 - blocks))), block_len, axis=0)
    place = depth[:, None] * block_len + jnp.arange(block_len, dtype=F32)[None, :]
    return (row_reach.astype(BF16), place.reshape(tree_len))


def rope_tables(place, head_dim):
    half = head_dim // 2
    freq = THETA ** (-2.0 * jnp.arange(half, dtype=F32) / head_dim)
    angle = place[:, None] * freq[None, :]
    return (jnp.cos(angle), jnp.sin(angle))


def rotate(values, cosine, sine, sign):
    half = values.shape[-1] // 2
    first, second = values[..., :half], values[..., half:]
    return jnp.concatenate(
        [first * cosine - sign * second * sine, second * cosine + sign * first * sine], -1
    )


def normalize(values):
    inverse = lax.rsqrt(jnp.mean(values * values, axis=-1, keepdims=True) + EPS)
    return (values * inverse, inverse)


def norm_back(grad_normed, gain, values):
    scaled, inverse = normalize(values)
    grad_scaled = grad_normed * gain
    inner = jnp.mean(grad_scaled * scaled, axis=-1, keepdims=True)
    return inverse * (grad_scaled - scaled * inner)


def dot_nn(left, right):
    return jnp.dot(left, right, preferred_element_type=F32)


def dot_nt(left, right):
    return lax.dot_general(left, right, (((1,), (1,)), ((), ())), preferred_element_type=F32)


def dot_tn(left, right):
    return lax.dot_general(left, right, (((0,), (0,)), ((), ())), preferred_element_type=F32)


def flip(index, mask):
    out = index
    bit = 1
    while bit <= mask:
        if mask & bit:
            out = out + bit * (1 - 2 * (index // bit % 2))
        bit *= 2
    return out


class Links:
    def __init__(self, tp, send_sems, recv_sems):
        self.tp = tp
        self.di = lax.axis_index("dp")
        self.ti = lax.axis_index("tensor")
        self.send_sems, self.recv_sems = send_sems, recv_sems
        self.used = 0

    def partner(self, mask):
        return (flip(self.di, mask // self.tp), flip(self.ti, mask % self.tp))

    def greet(self, masks):
        barrier = pltpu.get_barrier_semaphore()
        for mask in masks:
            pl.semaphore_signal(barrier, inc=1, device_id=self.partner(mask), device_id_type=MESH)
        pl.semaphore_wait(barrier, len(masks))

    def remote(self, src, dst, mask):
        index = self.used
        self.used += 1
        return pltpu.make_async_remote_copy(
            src_ref=src,
            dst_ref=dst,
            send_sem=self.send_sems.at[index],
            recv_sem=self.recv_sems.at[index],
            device_id=self.partner(mask),
            device_id_type=MESH,
        )

    def send(self, src, dst, mask):
        copy = self.remote(src, dst, mask)
        copy.start()
        return copy


def line_middle(links):
    zi = links.di // 2
    return (zi == 1) | (zi == 2)


class Spread:
    def __init__(self, links, outer, own, block):
        self.links, self.outer = links, outer
        step = 2 * links.tp
        self.middle = line_middle(links)
        self.copies = {k: links.remote(own, block(k), k * step) for k in range(1, outer)}
        if outer == 4:
            self.onward = links.remote(block(2), block(3), step)

    def start(self):
        if self.outer != 4:
            for copy in self.copies.values():
                copy.start()
            return
        self.copies[2].start()
        self.copies[1].start()

        @pl.when(self.middle)
        def _():
            self.copies[3].start()

    def forward(self):
        self.copies[2].wait_recv()
        if self.outer != 4:
            return

        @pl.when(self.middle)
        def _():
            self.onward.start()

    def arrive(self, k):
        if k == 1 or (self.outer != 4 and k != 2):
            self.copies[k].wait_recv()
        elif k == 3:

            @pl.when(self.middle)
            def _():
                self.copies[3].wait_recv()

            @pl.when(jnp.logical_not(self.middle))
            def _():
                self.onward.wait_recv()

    def sent(self):
        if self.outer != 4:
            for copy in self.copies.values():
                copy.wait_send()
            return
        self.copies[1].wait_send()
        self.copies[2].wait_send()

        @pl.when(self.middle)
        def _():
            self.copies[3].wait_send()
            self.onward.wait_send()


class ReduceZ:
    def __init__(self, links, outer, block, held, staged):
        self.links, self.outer, self.block, self.held, self.staged = (
            links,
            outer,
            block,
            held,
            staged,
        )
        step = 2 * links.tp
        self.middle = line_middle(links)
        self.copies = {k: links.remote(block(k), held.at[k], k * step) for k in range(1, outer)}
        if outer == 4:
            self.inward = links.remote(block(3), held.at[0], step)
            self.summed = links.remote(staged, held.at[2], 2 * step)

    def on_ends(self, *actions):
        @pl.when(jnp.logical_not(self.middle))
        def _():
            for action in actions:
                action()

    def on_middle(self, *actions):
        @pl.when(self.middle)
        def _():
            for action in actions:
                action()

    def start(self, k):
        if self.outer != 4 or k == 1:
            self.copies[k].start()
        elif k == 3:
            self.on_ends(self.inward.start)
            self.on_middle(self.copies[3].start)
        elif k == 2:
            self.on_ends(self.copies[2].start)

    def start_all(self):
        for k in range(self.outer - 1, 0, -1):
            self.start(k)

    def pump(self):
        if self.outer != 4:
            return

        def add():
            rows, width = self.staged.shape
            spec = rows_spec(min(rows, 128), width)
            add_pipe(spec, rows, self.block(2), self.held.at[0], self.staged)

        self.on_middle(self.inward.wait_recv, add, self.summed.start)

    def arrive(self):
        if self.outer != 4:
            for copy in self.copies.values():
                copy.wait_recv()
            return
        self.copies[1].wait_recv()
        self.on_middle(self.copies[2].wait_recv, self.copies[3].wait_recv)
        self.on_ends(self.summed.wait_recv)

    def total(self, lo, rows, out):
        width = self.staged.shape[1]
        spec = rows_spec(min(rows, 128), width)

        def add(*refs):
            value = refs[0][...].astype(F32)
            for ref in refs[1:-1]:
                value = value + ref[...].astype(F32)
            refs[-1][...] = value.astype(refs[-1].dtype)

        def over(kept):
            parts = [self.block(0)] + [self.held.at[k] for k in kept]
            parts = [part.at[pl.ds(lo, rows)] for part in parts]
            grid = (rows // min(rows, 128),)
            pipe(add, grid, [spec] * len(parts), [spec], *parts, out)

        if self.outer != 4:
            over(range(1, self.outer))
            return
        self.on_middle(lambda: over([1, 2, 3]))
        self.on_ends(lambda: over([1, 2]))

    def sent(self):
        if self.outer != 4:
            for copy in self.copies.values():
                copy.wait_send()
            return
        self.copies[1].wait_send()
        self.on_middle(self.copies[3].wait_send, self.summed.wait_send)
        self.on_ends(self.copies[2].wait_send, self.inward.wait_send)


def gather_units(links, full, rows):
    tp = links.tp

    def block(m, lo=0, n=None):
        return full.at[pl.ds(m * rows + lo, rows if n is None else n)]

    half = rows // 2
    sent = []

    def send(m, mask, lo=0, n=None):
        copy = links.send(block(m, lo, n), block(m ^ mask, lo, n), mask)
        sent.append(copy)
        return copy

    x = send(0, tp)
    y = send(0, 2)
    c0 = send(0, 1)
    yield
    y.wait_recv()
    low = send(2, tp, half, half)
    c2 = send(2, 1)
    x.wait_recv()
    high = send(tp, 2, 0, half)
    c4 = send(tp, 1)
    yield
    low.wait_recv()
    high.wait_recv()
    c6 = send(tp + 2, 1)
    yield
    for copy in (c0, c2, c4, c6):
        copy.wait_recv()
    for copy in sent:
        copy.wait_send()
    yield


def run(stages):
    for _ in stages:
        pass


def pipe(body, grid, in_specs, out_specs, *refs):
    pltpu.emit_pipeline(body, grid=grid, in_specs=in_specs, out_specs=out_specs)(*refs)


def rows_spec(rows, width):
    return pl.BlockSpec((rows, width), lambda i: (i, 0))


def whole_spec(rows, width):
    return pl.BlockSpec((rows, width), lambda i: (0, 0))


def once_spec(rows, width):
    return pl.BlockSpec((rows, width), lambda i: (0, 0), pipeline_mode=pl.Buffered(1))


def add_refs(a_ref, b_ref, o_ref):
    o_ref[...] = (a_ref[...].astype(F32) + b_ref[...].astype(F32)).astype(o_ref.dtype)


def add_pipe(spec, rows, a, b, out):
    pipe(add_refs, (rows // spec.block_shape[0],), [spec, spec], [spec], a, b, out)


def copy_body(a_ref, o_ref):
    o_ref[...] = a_ref[...]


def keep(src, dst):
    rows, width = src.shape
    spec = rows_spec(min(rows, 128), width)
    pipe(copy_body, (rows // min(rows, 128),), [spec], [spec], src, dst)


def nt_body(a_ref, b_ref, o_ref):
    o_ref[...] = dot_nt(a_ref[...], b_ref[...]).astype(BF16)


def nn_body(a_ref, b_ref, o_ref):
    o_ref[...] = dot_nn(a_ref[...], b_ref[...]).astype(BF16)


def tn_body(a_ref, b_ref, o_ref):
    o_ref[...] = dot_tn(a_ref[...], b_ref[...]).astype(BF16)


def weight_grad(acts, grads, out, blocks, first=0, count=None):
    tokens, model = acts.shape
    width = grads.shape[1]
    size = model // blocks
    count = blocks if count is None else count
    pipe(
        tn_body,
        (count,),
        [pl.BlockSpec((tokens, size), lambda i: (0, first + i)), once_spec(tokens, width)],
        [pl.BlockSpec((size, width), lambda i: (first + i, 0))],
        acts,
        grads,
        out,
    )


class ScatterTensor:
    def __init__(self, links, part, got_c, got_y, far, rows):
        self.links, self.part, self.got_c, self.got_y, self.far = links, part, got_c, got_y, far
        self.rows = rows
        self.model = part.shape[1]
        self.spec = rows_spec(rows // 2, self.model)

    def block(self, mask):
        rows = self.rows
        return self.part.at[
            pl.ds(pl.multiple_of(flip(self.links.ti, mask) * rows, rows), rows)
        ]

    def start(self):
        self.copies = [
            self.links.send(self.block(3), self.got_c.at[1], 1),
            self.links.send(self.block(1), self.got_c.at[0], 1),
        ]

    def across(self):
        self.copies[0].wait_recv()
        add_pipe(self.spec, self.rows, self.block(2), self.got_c.at[1], self.far)
        self.copies.append(self.links.send(self.far, self.got_y, 2))

    def arrive(self):
        self.copies[1].wait_recv()
        self.copies[2].wait_recv()
        return [self.block(0), self.got_c.at[0], self.got_y]

    def sent(self):
        for copy in self.copies:
            copy.wait_send()


class ScatterUnits:
    def __init__(self, links, part, got_c, near, got, rows):
        self.links, self.part, self.got_c, self.near, self.got = links, part, got_c, near, got
        self.rows, self.model = rows, part.shape[1]
        self.sends = []

    def send(self, src, dst, mask):
        copy = self.links.send(src, dst, mask)
        self.sends.append(copy)
        return copy

    def block(self, m):
        return self.part.at[pl.ds(m * self.rows, self.rows)]

    def start(self):
        self.from_c = [self.send(self.block(2 * i + 1), self.got_c.at[i], 1) for i in range(4)]

    def add(self, m, slot, lo, n):
        rows = pl.ds(lo, n)
        add_pipe(
            rows_spec(n, self.model),
            n,
            self.block(m).at[rows],
            self.got_c.at[m // 2].at[rows],
            self.near.at[slot].at[rows],
        )

    def across(self):
        tp, rows, half = self.links.tp, self.rows, self.rows // 2
        low, high = pl.ds(0, half), pl.ds(half, half)
        near, got = self.near, self.got
        for copy in self.from_c:
            copy.wait_recv()
        self.add(6, 2, 0, half)
        self.top = self.send(near.at[2].at[low], got.at[2].at[low], tp)
        self.add(6, 2, half, half)
        self.bottom = self.send(near.at[2].at[high], got.at[2].at[high], 2)
        self.add(4, 0, 0, half)
        self.x_low = self.send(near.at[0].at[low], got.at[0].at[low], tp)
        self.add(2, 1, half, half)
        self.y_high = self.send(near.at[1].at[high], got.at[1].at[high], 2)

    def finish(self):
        tp, half = self.links.tp, self.rows // 2
        low, high = pl.ds(0, half), pl.ds(half, half)
        near, got = self.near, self.got

        def add3(m, slot, rows):
            def body(a_ref, b_ref, c_ref, o_ref):
                o_ref[...] = (
                    a_ref[...].astype(F32) + b_ref[...].astype(F32) + c_ref[...].astype(F32)
                ).astype(BF16)

            spec = rows_spec(half, self.model)
            pipe(
                body,
                (1,),
                [spec] * 3,
                [spec],
                self.block(m).at[rows],
                self.got_c.at[m // 2].at[rows],
                got.at[2].at[rows],
                near.at[slot].at[rows],
            )

        self.top.wait_recv()
        add3(2, 1, low)
        self.y_low = self.send(near.at[1].at[low], got.at[1].at[low], 2)
        self.bottom.wait_recv()
        add3(4, 0, high)
        self.x_high = self.send(near.at[0].at[high], got.at[0].at[high], tp)

    def arrive(self):
        for copy in (self.x_low, self.x_high, self.y_low, self.y_high):
            copy.wait_recv()
        return [self.block(0), self.got_c.at[0], self.got.at[0], self.got.at[1]]

    def sent(self):
        for copy in self.sends:
            copy.wait_send()


def sum_refs(refs):
    value = refs[0][...].astype(F32)
    for ref in refs[1:]:
        value = value + ref[...].astype(F32)
    return value


class GatherTree:
    def __init__(self, links, full, rows):
        self.links, self.full, self.rows = links, full, rows

    def block(self, mask):
        rows = self.rows
        return self.full.at[
            pl.ds(pl.multiple_of(flip(self.links.ti, mask) * rows, rows), rows)
        ]

    def start(self):
        self.y = self.links.send(self.block(0), self.block(0), 2)
        self.c = self.links.send(self.block(0), self.block(0), 1)

    def across(self):
        self.y.wait_recv()
        self.yc = self.links.send(self.block(2), self.block(2), 1)

    def arrive(self):
        self.c.wait_recv()
        self.yc.wait_recv()

    def sent(self):
        for copy in (self.y, self.c, self.yc):
            copy.wait_send()


def greet_all(links, outer):
    step = 2 * links.tp
    links.greet([1, 2, links.tp] + [k * step for k in range(1, outer)])


def forward_kernel(
    outer,
    tp,
    wq,
    wo,
    wg,
    wu,
    wd,
    gn,
    x,
    xh,
    cot,
    cosine,
    sine,
    row_reach,
    wq_all,
    wo_all,
    gate_w,
    up_w,
    gain_rows,
    h1,
    qkv,
    probs,
    att,
    x1,
    h2,
    cot_all,
    dgate,
    dupper,
    hid,
    down_w,
    grad_down,
    gn_all,
    part,
    got_c,
    got_y,
    far,
    dhid,
    gate,
    upper,
    send_sems,
    recv_sems,
):
    links = Links(tp, send_sems, recv_sems)
    shard, qkv_width = wq.shape
    units = gate_w.shape[1]
    rows, model = xh.shape
    tree_len = rows * tp
    q_width = att.shape[1]
    kv_width = (qkv_width - q_width) // 2
    head = HEAD_SIZE
    xi = links.di % 2
    greet_all(links, outer)

    def shard_block(full, k):
        return full.at[pl.ds(pl.multiple_of((2 * k + xi) * shard, shard), shard)]

    mine = pl.ds(pl.multiple_of(xi * units, units), units)
    peers = pl.ds(pl.multiple_of((1 - xi) * units, units), units)
    place = pl.ds(pl.multiple_of(xi * shard, shard), shard)

    def send_pair(w, full):
        return links.send(w.at[:, peers], full.at[place], tp)

    def mlp_spread(full):
        return Spread(
            links,
            outer,
            full.at[pl.ds(0, 2 * shard)],
            lambda k: full.at[pl.ds(k * 2 * shard, 2 * shard)],
        )

    gains = Spread(links, outer, gn, lambda k: shard_block(gn_all, k))
    attn = Spread(links, outer, wq, lambda k: shard_block(wq_all, k))
    attn_out = Spread(links, outer, wo, lambda k: shard_block(wo_all, k))
    gains.start()
    across_gn = [links.send(gn, shard_block(gn_all, 0), tp)]
    attn.start()
    across = [links.send(wq, shard_block(wq_all, 0), tp)]
    attn_out.start()
    pair = [send_pair(wg, gate_w)]
    across_out = [links.send(wo, shard_block(wo_all, 0), tp)]

    def cross(full, k, copies):
        copies.append(links.send(shard_block(full, k), shard_block(full, k), tp))

    keep(gn, shard_block(gn_all, 0))
    keep(wg.at[:, mine], gate_w.at[place])

    gains.forward()
    for k in range(1, outer):
        gains.arrive(k)
        across_gn.append(links.send(shard_block(gn_all, k), shard_block(gn_all, k), tp))
    keep(wq, shard_block(wq_all, 0))
    keep(wo, shard_block(wo_all, 0))
    for copy in across_gn:
        copy.wait_recv()

    def gain_rows_of(g_ref, o_ref):
        lane = lax.broadcasted_iota(jnp.int32, (8, 128), 1)
        row = lax.broadcasted_iota(jnp.int32, (8, 128), 0)
        pick = jnp.where((row < 2) & (lane == row * 64), 1.0, 0.0).astype(BF16)
        o_ref[...] = dot_nt(pick, g_ref[...])

    pipe(gain_rows_of, (1,), [whole_spec(model, 128)], [whole_spec(8, model)], gn_all, gain_rows)
    spec = rows_spec(rows // 2, model)
    gain_spec = whole_spec(8, model)

    def scale_tokens(x_ref, g_ref, o_ref):
        o_ref[...] = (x_ref[...] * g_ref[0:1]).astype(BF16)

    tree = GatherTree(links, h1, rows)
    pipe(scale_tokens, (2,), [spec, gain_spec], [spec], xh, gain_rows, tree.block(0))
    tree.start()
    keep(wu.at[:, mine], up_w.at[place])
    keep(wd.at[:, mine], down_w.at[place])
    keep(cot, cot_all.at[pl.ds(0, rows)])

    spreads = [mlp_spread(full) for full in (gate_w, up_w, down_w)]
    attn.forward()
    cross(wq_all, 2, across)
    for k in range(1, outer):
        if k != 2:
            attn.arrive(k)
            cross(wq_all, k, across)
    tree.across()
    attn_out.forward()
    cross(wo_all, 2, across_out)
    pair[0].wait_recv()
    spreads[0].start()
    for k in range(1, outer):
        if k != 2:
            attn_out.arrive(k)
            cross(wo_all, k, across_out)
    pair.append(send_pair(wu, up_w))
    later = gather_units(links, cot_all, rows)
    next(later)
    pair.append(send_pair(wd, down_w))
    tree.arrive()
    for copy in across:
        copy.wait_recv()

    def project(x_ref, w_ref, cos_ref, sin_ref, out_ref):
        raw = dot_nn(x_ref[...], w_ref[...])
        for slot in range((q_width + kv_width) // head):
            cols = slice(slot * head, (slot + 1) * head)
            out_ref[:, cols] = rotate(raw[:, cols], cos_ref[...], sin_ref[...], 1.0).astype(BF16)
        out_ref[:, q_width + kv_width :] = raw[:, q_width + kv_width :].astype(BF16)

    pipe(
        project,
        (tp,),
        [
            rows_spec(rows, model),
            whole_spec(model, qkv_width),
            rows_spec(rows, head // 2),
            rows_spec(rows, head // 2),
        ],
        [rows_spec(rows, qkv_width)],
        h1,
        wq_all,
        cosine,
        sine,
        qkv,
    )

    group = q_width // kv_width

    def attend(q_ref, k_ref, v_ref, r_ref, p_ref, o_ref):
        segment = lax.broadcasted_iota(jnp.int32, (128, tree_len), 0)
        key_row = lax.broadcasted_iota(jnp.int32, (128, tree_len), 1)
        member = jnp.where(key_row // BLK == segment, 1.0, 0.0).astype(BF16)
        seen = dot_nn(r_ref[...], member)
        query = lax.broadcasted_iota(jnp.int32, (rows, tree_len), 0) + pl.program_id(0) * rows
        key = lax.broadcasted_iota(jnp.int32, (rows, tree_len), 1)
        scores = dot_nt(q_ref[...], k_ref[...]) * (head**-0.5)
        scores = jnp.where((seen > 0.5) & (key <= query), scores, NEG)
        weights = jnp.exp(scores - jnp.max(scores, axis=-1, keepdims=True))
        weights = (weights / jnp.sum(weights, axis=-1, keepdims=True)).astype(BF16)
        p_ref[0] = weights
        o_ref[...] = dot_nn(weights, v_ref[...]).astype(BF16)

    k_at, v_at = q_width // head, (q_width + kv_width) // head
    pipe(
        attend,
        (tp, q_width // head),
        [
            pl.BlockSpec((rows, head), lambda i, h: (i, h)),
            pl.BlockSpec((tree_len, head), lambda i, h: (0, k_at + h // group)),
            pl.BlockSpec((tree_len, head), lambda i, h: (0, v_at + h // group)),
            pl.BlockSpec((rows, 128), lambda i, h: (i, 0)),
        ],
        [
            pl.BlockSpec((1, rows, tree_len), lambda i, h: (h, i, 0)),
            pl.BlockSpec((rows, head), lambda i, h: (i, h)),
        ],
        qkv,
        qkv,
        qkv,
        row_reach,
        probs,
        att,
    )
    for copy in across_out:
        copy.wait_recv()
    pipe(
        nt_body,
        (tp,),
        [rows_spec(rows, q_width), whole_spec(model, q_width)],
        [rows_spec(rows, model)],
        att,
        wo_all,
        part,
    )
    mixed = ScatterTensor(links, part, got_c, got_y, far, rows)
    mixed.start()
    spreads[0].forward()
    pair[1].wait_recv()
    spreads[1].start()
    mixed.across()
    next(later)
    parts = mixed.arrive()

    def residual(x_ref, a_ref, b_ref, c_ref, g_ref, x1_ref, h_ref):
        total = x_ref[...] + sum_refs((a_ref, b_ref, c_ref))
        x1_ref[...] = total
        h_ref[...] = (normalize(total)[0] * g_ref[1:2]).astype(BF16)

    pipe(
        residual,
        (2,),
        [spec] * 4 + [gain_spec],
        [spec] * 2,
        x,
        *parts,
        gain_rows,
        x1,
        h2.at[pl.ds(0, rows)],
    )
    stages = gather_units(links, h2, rows)
    next(stages)
    next(later)
    next(stages)
    spreads[1].forward()
    pair[2].wait_recv()
    spreads[2].start()
    next(stages)
    next(stages)
    run(later)

    for spread in spreads[:2]:
        for k in range(1, outer):
            spread.arrive(k)

    def expand(x_ref, g_ref, u_ref, a_ref, b_ref, h_ref):
        @pl.when(pl.program_id(0) == tp)
        def _():
            spreads[2].forward()

        g = dot_nn(x_ref[...], g_ref[...])
        u = dot_nn(x_ref[...], u_ref[...])
        sigma = jax.nn.sigmoid(g)
        swish = g * sigma
        a_ref[...] = (u * sigma * (1.0 + g * (1.0 - sigma))).astype(BF16)
        b_ref[...] = swish.astype(BF16)
        h_ref[...] = (swish * u).astype(BF16)

    pipe(
        expand,
        (2 * tp,),
        [rows_spec(rows, model), once_spec(model, units), once_spec(model, units)],
        [rows_spec(rows, units)] * 3,
        h2,
        gate_w,
        up_w,
        gate,
        upper,
        hid,
    )
    weight_grad(cot_all, hid, grad_down, 4)

    known = (outer - 1) * 2 * shard
    unit_spec = rows_spec(rows, units)

    def contract_known(c_ref, d_ref):
        at = pl.ds(pl.multiple_of(pl.program_id(0) * rows, rows), rows)
        dhid[at] = dot_nn(c_ref[...], d_ref[...])

    def contract_last(c_ref, d_ref, a_ref, b_ref, dg_ref, du_ref):
        at = pl.ds(pl.multiple_of(pl.program_id(0) * rows, rows), rows)
        value = dhid[at] + dot_nn(c_ref[...], d_ref[...])
        dg_ref[...] = (value * a_ref[...].astype(F32)).astype(BF16)
        du_ref[...] = (value * b_ref[...].astype(F32)).astype(BF16)

    for k in range(1, outer - 1):
        spreads[2].arrive(k)
    pipe(
        contract_known,
        (2 * tp,),
        [rows_spec(rows, known), once_spec(known, units)],
        [],
        cot_all.at[:, pl.ds(0, known)],
        down_w.at[pl.ds(0, known)],
    )
    spreads[2].arrive(outer - 1)
    pipe(
        contract_last,
        (2 * tp,),
        [rows_spec(rows, model - known), once_spec(model - known, units), unit_spec, unit_spec],
        [unit_spec] * 2,
        cot_all.at[:, pl.ds(known, model - known)],
        down_w.at[pl.ds(known, model - known)],
        gate,
        upper,
        dgate,
        dupper,
    )
    for spread in [gains, attn, attn_out] + spreads:
        spread.sent()
    for copy in across_gn + across + across_out + pair:
        copy.wait_send()
    tree.sent()
    mixed.sent()


def backward_kernel(
    outer,
    tp,
    wq_all,
    wo_all,
    gate_w,
    up_w,
    gain_rows,
    h1,
    qkv,
    probs,
    att,
    x1,
    h2,
    cot,
    dgate,
    dupper,
    hid,
    down_w,
    grad_down,
    x,
    cosine,
    sine,
    out,
    grad_tok,
    down_mine,
    down_theirs,
    gate_mine,
    gate_theirs,
    up_mine,
    up_theirs,
    out_total,
    qkv_total,
    dx1,
    dscores,
    grad_gate,
    grad_up,
    grad_out,
    grad_qkv,
    down_held,
    gate_held,
    up_held,
    out_held,
    qkv_held,
    down_staged,
    gate_staged,
    up_staged,
    out_staged,
    qkv_staged,
    down_give,
    gate_give,
    up_give,
    y_part,
    e_part,
    e_got_c,
    y_got_c,
    e_near,
    y_near,
    e_got,
    y_got,
    dx1_low,
    dout,
    dqkv,
    f_got_c,
    f_got_y,
    f_far,
    out_pair,
    qkv_pair,
    out_sum,
    qkv_sum,
    send_sems,
    recv_sems,
):
    links = Links(tp, send_sems, recv_sems)
    rows, model = x.shape
    tree_len = rows * tp
    units = gate_w.shape[1]
    q_width = att.shape[1]
    qkv_width = qkv.shape[1]
    kv_width = (qkv_width - q_width) // 2
    head = HEAD_SIZE
    group = q_width // kv_width
    shard = model // (2 * outer)
    xi = links.di % 2
    half = pl.multiple_of(xi * shard, shard)
    other = pl.multiple_of((1 - xi) * shard, shard)
    spec = rows_spec(rows // 2, model)
    gain_spec = whole_spec(8, model)
    greet_all(links, outer)

    def mlp_reduce(grad, held, staged):
        return ReduceZ(
            links, outer, lambda k: grad.at[pl.ds(k * 2 * shard, 2 * shard)], held, staged
        )

    def trade(reduce, mine, give, theirs):
        reduce.arrive()
        reduce.total(other, shard, give)
        copy = links.send(give, theirs, tp)
        reduce.total(half, shard, mine)
        return copy

    red_down = mlp_reduce(grad_down, down_held, down_staged)
    red_gate = mlp_reduce(grad_gate, gate_held, gate_staged)
    red_up = mlp_reduce(grad_up, up_held, up_staged)
    red_down.start_all()

    y_sum = ScatterUnits(links, y_part, y_got_c, y_near, y_got, rows)

    def every_other(first, block_rows, width):
        return pl.BlockSpec((block_rows, width), lambda i: (2 * i + first, 0))

    def back(dg_ref, du_ref, g_ref, u_ref, o_ref):
        o_ref[...] = (dot_nt(dg_ref[...], g_ref[...]) + dot_nt(du_ref[...], u_ref[...])).astype(
            BF16
        )

    def back_blocks(first):
        pipe(
            back,
            (tp,),
            [every_other(first, rows, units)] * 2 + [once_spec(model, units)] * 2,
            [every_other(first, rows, model)],
            dgate,
            dupper,
            gate_w,
            up_w,
            e_part,
        )

    e_sum = ScatterUnits(links, e_part, e_got_c, e_near, e_got, rows)
    back_blocks(1)
    e_sum.start()
    red_down.pump()
    back_blocks(0)
    e_sum.across()
    weight_grad(h2, dgate, grad_gate, 4)
    red_gate.start_all()
    e_sum.finish()
    weight_grad(h2, dupper, grad_up, 4)
    red_up.start_all()
    trades = [trade(red_down, down_mine, down_give, down_theirs)]

    tree = GatherTree(links, dx1_low, rows)

    def through_norm(c_ref, x_ref, g_ref, *refs):
        value = c_ref[...].astype(F32) + norm_back(sum_refs(refs[:-2]), g_ref[1:2], x_ref[...])
        refs[-2][...] = value
        refs[-1][...] = value.astype(BF16)

    parts = e_sum.arrive()
    pipe(
        through_norm,
        (2,),
        [spec, spec, gain_spec] + [spec] * len(parts),
        [spec] * 2,
        cot,
        x1,
        gain_rows,
        *parts,
        dx1,
        tree.block(0),
    )
    tree.start()
    red_gate.pump()
    pipe(
        nt_body,
        (2 * tp,),
        [rows_spec(rows, units), once_spec(model, units)],
        [rows_spec(rows, model)],
        hid,
        down_w,
        y_part,
    )
    tree.across()
    y_sum.start()
    tree.arrive()

    pipe(
        nn_body,
        (tp,),
        [rows_spec(rows, model), whole_spec(model, q_width)],
        [rows_spec(rows, q_width)],
        dx1_low,
        wo_all,
        dout,
    )

    def pair_block(full, k, at):
        return full.at[pl.ds(pl.multiple_of(k * 2 * shard + at, shard), shard)]

    def pair_send(grad, held, k):
        return links.send(pair_block(grad, k, other), held.at[k], tp)

    red_out = ReduceZ(links, outer, lambda k: out_sum.at[k], out_held, out_staged)
    red_qkv = ReduceZ(links, outer, lambda k: qkv_sum.at[k], qkv_held, qkv_staged)
    weight_grad(dx1_low, att, grad_out, 4)
    order = list(range(outer - 1, -1, -1))
    out_across = {k: pair_send(grad_out, out_pair, k) for k in order}
    y_sum.across()

    def score_grads(do_ref, k_ref, v_ref, p_ref, cos_ref, sin_ref, ds_ref, dq_ref):
        p = p_ref[0].astype(F32)
        dp = dot_nt(do_ref[...], v_ref[...])
        inner = jnp.sum(p * dp, axis=-1, keepdims=True)
        ds = (p * (dp - inner) * (head**-0.5)).astype(BF16)
        ds_ref[0] = ds
        dq_ref[...] = rotate(dot_nn(ds, k_ref[...]), cos_ref[...], sin_ref[...], -1.0).astype(BF16)

    k_at, v_at = q_width // head, (q_width + kv_width) // head
    pipe(
        score_grads,
        (tp, q_width // head),
        [
            pl.BlockSpec((rows, head), lambda i, h: (i, h)),
            pl.BlockSpec((tree_len, head), lambda i, h: (0, k_at + h // group)),
            pl.BlockSpec((tree_len, head), lambda i, h: (0, v_at + h // group)),
            pl.BlockSpec((1, rows, tree_len), lambda i, h: (h, i, 0)),
            pl.BlockSpec((rows, head // 2), lambda i, h: (i, 0)),
            pl.BlockSpec((rows, head // 2), lambda i, h: (i, 0)),
        ],
        [
            pl.BlockSpec((1, rows, tree_len), lambda i, h: (h, i, 0)),
            pl.BlockSpec((rows, head), lambda i, h: (i, h)),
        ],
        dout,
        qkv,
        qkv,
        probs,
        cosine,
        sine,
        dscores,
        dqkv,
    )

    def key_grads(ds_ref, p_ref, q_ref, do_ref, cos_ref, sin_ref, dkv_ref):
        dk = jnp.zeros((rows, head), F32)
        dv = jnp.zeros((rows, head), F32)
        for h in range(group):
            cols = slice(h * head, (h + 1) * head)
            dk = dk + dot_tn(ds_ref[h], q_ref[:, cols])
            dv = dv + dot_tn(p_ref[h], do_ref[:, cols])
        dkv_ref[:, :head] = rotate(dk, cos_ref[...], sin_ref[...], -1.0).astype(BF16)
        dkv_ref[:, head:] = dv.astype(BF16)

    by_key = pl.BlockSpec((group, tree_len, rows), lambda i: (0, 0, i))
    pipe(
        key_grads,
        (tp,),
        [by_key, by_key]
        + [whole_spec(tree_len, q_width)] * 2
        + [rows_spec(rows, head // 2)] * 2,
        [rows_spec(rows, 2 * kv_width)],
        dscores,
        probs,
        qkv.at[:, pl.ds(0, q_width)],
        dout,
        cosine,
        sine,
        dqkv.at[:, pl.ds(q_width, 2 * kv_width)],
    )

    y_sum.finish()

    def pair_add(grad, held, total, k):
        add_pipe(
            rows_spec(min(shard, 128), grad.shape[1]),
            shard,
            pair_block(grad, k, half),
            held.at[k],
            total.at[k],
        )

    qkv_across = {}
    weight_grad(h1, dqkv, grad_qkv, 4)
    for k in order:
        qkv_across[k] = pair_send(grad_qkv, qkv_pair, k)
    e_sum.sent()
    f_part = e_part.at[pl.ds(0, tree_len)]
    pipe(
        nt_body,
        (tp,),
        [rows_spec(rows, qkv_width), whole_spec(model, qkv_width)],
        [rows_spec(rows, model)],
        dqkv,
        wq_all,
        f_part,
    )
    f_sum = ScatterTensor(links, f_part, f_got_c, f_got_y, f_far, rows)
    f_sum.start()
    f_sum.across()
    red_up.pump()
    for k in order:
        out_across[k].wait_recv()
        pair_add(grad_out, out_pair, out_sum, k)
        if k:
            red_out.start(k)
    trades.append(trade(red_gate, gate_mine, gate_give, gate_theirs))

    def finish_output(x_ref, *refs):
        refs[-1][...] = (x_ref[...] + sum_refs(refs[:-1])).astype(BF16)

    parts = y_sum.arrive()
    pipe(finish_output, (2,), [spec] * (1 + len(parts)), [spec], x1, *parts, out)

    for k in order:
        qkv_across[k].wait_recv()
        pair_add(grad_qkv, qkv_pair, qkv_sum, k)
        if k:
            red_qkv.start(k)

    def finish_tokens(d_ref, x_ref, g_ref, *refs):
        refs[-1][...] = (
            d_ref[...] + norm_back(sum_refs(refs[:-1]), g_ref[0:1], x_ref[...])
        ).astype(BF16)

    parts = f_sum.arrive()
    pipe(
        finish_tokens,
        (2,),
        [spec, spec, gain_spec] + [spec] * len(parts),
        [spec],
        dx1,
        x,
        gain_rows,
        *parts,
        grad_tok,
    )
    trades.append(trade(red_up, up_mine, up_give, up_theirs))
    red_out.pump()
    red_qkv.pump()
    red_out.arrive()
    red_out.total(0, shard, out_total)
    red_qkv.arrive()
    red_qkv.total(0, shard, qkv_total)
    for copy in trades:
        copy.wait()
    for copy in list(out_across.values()) + list(qkv_across.values()):
        copy.wait_send()
    for item in (red_down, red_gate, red_up, red_out, red_qkv, y_sum, f_sum, tree):
        item.sent()


def call(kernel, name, collective, count, shapes, scratch, operands):
    anywhere = pl.BlockSpec(memory_space=pl.ANY)
    return pl.pallas_call(
        kernel,
        out_shape=[jax.ShapeDtypeStruct(shape, dtype) for shape, dtype in shapes],
        in_specs=[anywhere] * len(operands),
        out_specs=[anywhere] * len(shapes),
        scratch_shapes=[pltpu.VMEM(shape, dtype) for shape, dtype in scratch]
        + [
            pltpu.SemaphoreType.DMA((count,)),
            pltpu.SemaphoreType.DMA((count,)),
        ],
        compiler_params=pltpu.CompilerParams(
            collective_id=collective, has_side_effects=True, vmem_limit_bytes=VMEM_LIMIT
        ),
        name=name,
    )(*operands)


def make_body(dp, tp):
    outer = dp // 2
    assert tp == 4 and dp == 2 * outer and outer >= 4 and outer & (outer - 1) == 0

    def swap(value, mask):
        return lax.ppermute(value, ("dp", "tensor"), [(i, i ^ mask) for i in range(dp * tp)])

    def relative(value, zi):
        width = value.shape[-1] // outer
        step = 1
        while step < outer:
            blocks = [value[..., i * width : (i + 1) * width] for i in range(outer)]
            swapped = jnp.concatenate([blocks[i ^ step] for i in range(outer)], -1)
            value = jnp.where((zi // step) % 2 == 1, swapped, value)
            step *= 2
        return value

    def body(
        tokens,
        parents,
        attn_gain,
        w_query,
        key_matrix,
        value_matrix,
        w_out,
        mlp_gain,
        w_gate,
        w_up,
        w_down,
        cotangent,
    ):
        di = lax.axis_index("dp")
        zi = di // 2
        upper_x = di % 2 == 1
        rows, model = tokens.shape
        tree_len = rows * tp
        q_width = w_query.shape[1]
        kv_width = key_matrix.shape[1]
        qkv_width = q_width + 2 * kv_width
        heads = q_width // HEAD_SIZE
        assert kv_width == HEAD_SIZE
        shard = w_query.shape[0]
        units = w_gate.shape[1] // 2

        wq = jnp.concatenate([w_query, key_matrix, value_matrix], 1)
        gn = jnp.concatenate(
            [
                jnp.broadcast_to(attn_gain[:, None], (shard, 64)),
                jnp.broadcast_to(mlp_gain[:, None], (shard, 64)),
            ],
            1,
        )
        row_reach, place = tree_tables(parents[0], tree_len, BLK)
        cosine, sine = rope_tables(place, HEAD_SIZE)
        x = relative(tokens, zi).astype(F32)
        xh = normalize(x)[0]
        cot = relative(cotangent, zi)
        (
            wq_all,
            wo_all,
            gate_w,
            up_w,
            gain_rows,
            h1,
            qkv,
            probs,
            att,
            x1,
            h2,
            cot_all,
            dgate,
            dupper,
            hid,
            down_w,
            grad_down,
        ) = call(
            functools.partial(forward_kernel, outer, tp),
            "layer_forward",
            0,
            60 + 9 * outer,
            [
                ((model, qkv_width), BF16),
                ((model, q_width), BF16),
                ((model, units), BF16),
                ((model, units), BF16),
                ((8, model), F32),
                ((tree_len, model), BF16),
                ((tree_len, qkv_width), BF16),
                ((heads, tree_len, tree_len), BF16),
                ((tree_len, q_width), BF16),
                ((rows, model), F32),
                ((2 * tree_len, model), BF16),
                ((2 * tree_len, model), BF16),
                ((2 * tree_len, units), BF16),
                ((2 * tree_len, units), BF16),
                ((2 * tree_len, units), BF16),
                ((model, units), BF16),
                ((model, units), BF16),
                ((model, 128), BF16),
            ],
            [
                ((tree_len, model), BF16),
                ((2, rows, model), BF16),
                ((rows, model), BF16),
                ((rows, model), BF16),
                ((2 * tree_len, units), F32),
                ((2 * tree_len, units), BF16),
                ((2 * tree_len, units), BF16),
            ],
            (wq, w_out.T, w_gate, w_up, w_down.T, gn, x, xh, cot, cosine, sine, row_reach),
        )[:17]

        (
            out,
            grad_tok,
            down_mine,
            down_theirs,
            gate_mine,
            gate_theirs,
            up_mine,
            up_theirs,
            out_total,
            qkv_total,
        ) = call(
            functools.partial(backward_kernel, outer, tp),
            "layer_backward",
            1,
            60 + 10 * outer,
            [((rows, model), BF16)] * 2
            + [((shard, units), F32), ((shard, units), BF16)] * 3
            + [((shard, q_width), F32), ((shard, qkv_width), F32)]
            + [((rows, model), F32), ((heads, tree_len, tree_len), BF16)]
            + [((model, units), BF16)] * 2
            + [((model, q_width), BF16), ((model, qkv_width), BF16)]
            + [((outer, 2 * shard, units), BF16)] * 3
            + [((outer, shard, q_width), BF16), ((outer, shard, qkv_width), BF16)]
            + [((2 * shard, units), BF16)] * 3
            + [((shard, q_width), BF16), ((shard, qkv_width), BF16)]
            + [((shard, units), BF16)] * 3
            + [((2 * tree_len, model), BF16)],
            [((2 * tree_len, model), BF16)]
            + [((4, rows, model), BF16)] * 2
            + [((3, rows, model), BF16)] * 4
            + [((tree_len, model), BF16), ((tree_len, q_width), BF16)]
            + [((tree_len, qkv_width), BF16), ((2, rows, model), BF16)]
            + [((rows, model), BF16)] * 2
            + [((outer, shard, q_width), BF16), ((outer, shard, qkv_width), BF16)] * 2,
            (
                wq_all,
                wo_all,
                gate_w,
                up_w,
                gain_rows,
                h1,
                qkv,
                probs,
                att,
                x1,
                h2,
                cot,
                dgate,
                dupper,
                hid,
                down_w,
                grad_down,
                x,
                cosine,
                sine,
            ),
        )[:10]

        def order_x(mine, theirs):
            theirs = theirs.astype(F32)
            low = jnp.where(upper_x, theirs, mine)
            high = jnp.where(upper_x, mine, theirs)
            return jnp.concatenate([low, high], 1)

        grad_gate = order_x(gate_mine, gate_theirs)
        grad_up = order_x(up_mine, up_theirs)
        grad_query = qkv_total[:, :q_width]
        grad_key = qkv_total[:, q_width : q_width + kv_width]
        grad_value = qkv_total[:, q_width + kv_width :]

        gain_sums = jnp.stack(
            [
                jnp.sum(w_query.astype(F32) * grad_query, 1)
                + jnp.sum(key_matrix.astype(F32) * grad_key, 1)
                + jnp.sum(value_matrix.astype(F32) * grad_value, 1),
                jnp.sum(w_gate.astype(F32) * grad_gate, 1)
                + jnp.sum(w_up.astype(F32) * grad_up, 1),
            ]
        )
        others = [swap(gain_sums, mask) for mask in (1, 2, 3)]
        gain_sums = (gain_sums + others[0]) + (others[1] + others[2])
        return (
            relative(out, zi),
            relative(grad_tok, zi),
            gain_sums[0] / attn_gain.astype(F32),
            grad_query,
            grad_key,
            grad_value,
            out_total.T,
            gain_sums[1] / mlp_gain.astype(F32),
            grad_gate,
            grad_up,
            order_x(down_mine, down_theirs).T,
        )

    return body


def solution(mesh):
    in_specs = (
        P(("dp", "tensor"), None),
        P("dp", None),
        P("dp"),
        P("dp", "tensor"),
        P("dp", "tensor"),
        P("dp", "tensor"),
        P("tensor", "dp"),
        P("dp"),
        P("dp", "tensor"),
        P("dp", "tensor"),
        P("tensor", "dp"),
        P(("dp", "tensor"), None),
    )
    out_specs = (
        P(("dp", "tensor"), None),
        P(("dp", "tensor"), None),
        P("dp"),
        P("dp", "tensor"),
        P("dp", "tensor"),
        P("dp", "tensor"),
        P("tensor", "dp"),
        P("dp"),
        P("dp", "tensor"),
        P("dp", "tensor"),
        P("tensor", "dp"),
    )
    body = make_body(mesh.shape["dp"], mesh.shape["tensor"])
    return jax.shard_map(body, mesh=mesh, in_specs=in_specs, out_specs=out_specs, check_vma=False)
```
